32 devices in a mesh: outer: 8 (over z, core), inner: 4 (over y, x).
Axes of the slice: x: 2, y: 2, z: 4, core: 2. Of those that a mesh axis runs over, the one named last changes fastest.
Arguments:
- right_side: float32 [128, 128, 512], P('outer', 'inner'), may hold values from -6 to 6
- coefficient: float32 [128, 128, 512], P('outer', 'inner'), may hold values from 0.1 to 10
Outputs:
- fine_field: float32 [128, 128, 512], P('outer', 'inner')
- middle_field: float32 [64, 64, 256], P('outer', 'inner')
- coarse_field: float32 [32, 32, 128], P('outer', 'inner')
- coarse_residual: float32 [32, 32, 128], P('outer', 'inner')
The draws below stay inside these ranges and needn't reach their ends.
All inputs are finite; a program needn't handle non-finite values.
Results may differ from the reference program's by a relative error of at most 0.0003.
Values sent between devices are 32-bit elements; how exact they have to be, the bound alone decides.
No kernel may reach another device: no remote copies, remote signals or barrier semaphores. Data moves between devices by JAX's collectives and lax.ppermute only.
A program may use at most 192 MiB of HBM per device.

```python
import math
import jax
import jax.numpy as jnp
from jax import lax

NY = 512
NU = 2
LEVELS = 3
NX = 128
NZ = 128


def level_of(key, extent, shards, low, high):
    factor_of = 1.0
    for axis_at, shards_of in shards:
        heights = jax.random.uniform(jax.random.fold_in(jax.random.fold_in(key, 6), axis_at), (shards_of,), jnp.float32, low / len(shards), high / len(shards))
        factor_of = factor_of * jnp.repeat(jnp.exp(heights), extent[axis_at] // shards_of).reshape((-1,) + (1,) * (len(extent) - 1 - axis_at))
    return factor_of


def scatter_about(rng, shape, spread, limit, cuts=(), kind=jnp.bfloat16):
    array = spread * jax.random.normal(rng, shape, jnp.float32)
    if cuts:
        array = array * level_of(rng, shape, cuts, -0.22, 0.18)
    return jnp.clip(array, -limit, limit).astype(kind)


def setup_inputs(seed: int = 0) -> dict:
    splits = jax.random.split(jax.random.key(seed), 3)
    right_side = scatter_about(splits[0], (NX, NZ, NY), 1.0, 6.0, ((0, 8), (1, 4)), jnp.float32)
    coefficient = jnp.clip(jnp.exp(math.log(10.0) - 4.6051702 * jax.random.uniform(splits[1], (NX, NZ, NY), jnp.float32) ** level_of(splits[1], (NX, NZ, NY), ((0, 8), (1, 4)), -0.2, 0.2)), 0.1, 10.0)
    return {"right_side": right_side, "coefficient": coefficient}


NEIGHBOUR_CUTS = (
    (slice(0, -2), slice(1, -1), slice(1, -1)),
    (slice(2, None), slice(1, -1), slice(1, -1)),
    (slice(1, -1), slice(0, -2), slice(1, -1)),
    (slice(1, -1), slice(2, None), slice(1, -1)),
    (slice(1, -1), slice(1, -1), slice(0, -2)),
    (slice(1, -1), slice(1, -1), slice(2, None)),
)
CENTRE_CUT = (slice(1, -1), slice(1, -1), slice(1, -1))


def pad_last(values):
    return jnp.pad(values, ((0, 0), (0, 0), (1, 1)))


def pad_grid(values):
    return jnp.pad(values, ((1, 1), (1, 1), (0, 0)))


def pad_along(values, dimension):
    widths = [(0, 0), (0, 0), (0, 0)]
    widths[dimension] = (1, 1)
    return jnp.pad(values, widths)


def diagonal_of(padded_coefficient):
    wider = pad_last(padded_coefficient)
    centre = wider[CENTRE_CUT]
    total = wider[NEIGHBOUR_CUTS[0]]
    for neighbour_cut in NEIGHBOUR_CUTS[1:]:
        total = total + wider[neighbour_cut]
    return 3.0 * centre + 0.5 * total


def neighbour_term(padded_coefficient, padded_solution):
    wide_k = pad_last(padded_coefficient)
    wide_u = pad_last(padded_solution)
    centre = wide_k[CENTRE_CUT]
    value_total = wide_u[NEIGHBOUR_CUTS[0]]
    weighted_total = wide_k[NEIGHBOUR_CUTS[0]] * wide_u[NEIGHBOUR_CUTS[0]]
    for neighbour_cut in NEIGHBOUR_CUTS[1:]:
        value_total = value_total + wide_u[neighbour_cut]
        weighted_total = weighted_total + wide_k[neighbour_cut] * wide_u[neighbour_cut]
    return 0.5 * (centre * value_total + weighted_total)


def parity_mask(grid_shape):
    total = (lax.broadcasted_iota(jnp.int32, grid_shape, 0)
             + lax.broadcasted_iota(jnp.int32, grid_shape, 1)
             + lax.broadcasted_iota(jnp.int32, grid_shape, 2))
    return total % 2 == 0


def restrict_padded(padded, dimension):
    moved = jnp.moveaxis(padded, dimension, 0)
    half_count = (moved.shape[0] - 2) // 2
    middle = moved[1:-1].reshape((half_count, 2) + moved.shape[1:])
    earlier = moved[0:-2:2]
    later = moved[3::2]
    coarse = (3.0 * (middle[:, 0] + middle[:, 1]) + (earlier + later)) * 0.125
    return jnp.moveaxis(coarse, 0, dimension)


def block_mean(values):
    grid_shape = values.shape
    blocks = values.reshape((grid_shape[0] // 2, 2, grid_shape[1] // 2, 2, grid_shape[2] // 2, 2))
    return jnp.sum(blocks, axis=(1, 3, 5)) * 0.125


def smooth_level(source, conductivity):
    padded_k = pad_grid(conductivity)
    diagonal = diagonal_of(padded_k)
    red_cells = parity_mask(source.shape)
    black_cells = jnp.logical_not(red_cells)
    solution = jnp.zeros_like(source)
    for sweep_index in range(NU):
        for colour in (red_cells, black_cells):
            term = neighbour_term(padded_k, pad_grid(solution))
            solution = jnp.where(colour, (source + term) / diagonal, solution)
    term = neighbour_term(padded_k, pad_grid(solution))
    residual = source - (diagonal * solution - term)
    return solution, residual


def reference(right_side, coefficient):
    source = right_side
    conductivity = coefficient
    fields = []
    residual = source
    for level_index in range(LEVELS):
        solution, residual = smooth_level(source, conductivity)
        fields.append(solution)
        if level_index + 1 < LEVELS:
            coarse = restrict_padded(pad_along(residual, 0), 0)
            coarse = restrict_padded(pad_along(coarse, 1), 1)
            coarse = restrict_padded(pad_along(coarse, 2), 2)
            source = 4.0 * coarse
            conductivity = block_mean(conductivity)
    return fields[0], fields[1], fields[2], residual
```

```python
import jax
import jax.numpy as jnp
from jax import lax
from jax.experimental import pallas as pl
from jax.experimental.pallas import tpu as pltpu
from jax.sharding import PartitionSpec as P

F32 = jnp.float32
HP = 3
HIGHEST = lax.Precision.HIGHEST


def tiled(tile, rows, lanes):
    wide = jnp.concatenate([tile] * (lanes // 128), axis=1)
    return jnp.concatenate([wide] * (rows // 8), axis=0)


def even_mask(rows, lanes):
    row = lax.broadcasted_iota(jnp.int32, (8, 128), 0)
    lane = lax.broadcasted_iota(jnp.int32, (8, 128), 1)
    return tiled((row + lane) & 1, rows, lanes) == 0


def pick(mask, a, b):
    return jnp.where(mask, a, b)


def row_index(lanes):
    return lax.broadcasted_iota(jnp.int32, (8, lanes), 0)


def lane_edge(value, at_start):
    lanes = value.shape[1]
    lane = lax.broadcasted_iota(jnp.int32, (value.shape[0], 128), 1)
    if at_start:
        edge = pick(lane == 0, 0.0, value[:, :128])
        return edge if lanes == 128 else jnp.concatenate([edge, value[:, 128:]], axis=1)
    edge = pick(lane == 127, 0.0, value[:, lanes - 128 :])
    return edge if lanes == 128 else jnp.concatenate([value[:, : lanes - 128], edge], axis=1)


def neighbours(ref, colour, p, pairs, even):
    other = 1 - colour
    x = ref[other, p]
    below = ref[other, jnp.maximum(p - 1, 0)]
    above = ref[other, jnp.minimum(p + 1, pairs - 1)]
    far = pick(even, below, above) if colour == 0 else pick(even, above, below)
    rows, lanes = x.shape
    return (
        x,
        far,
        pltpu.roll(x, 1, 0),
        pltpu.roll(x, rows - 1, 0),
        pltpu.roll(x, 1, 1),
        pltpu.roll(x, lanes - 1, 1),
    )


def span(own, layers):
    extra = (layers + 1) // 2
    return HP - extra, HP + own + extra


def relax_level(K, S, U, W, D, R, own, depth, residual_layers):
    _, pairs, rows, lanes = K.shape
    even = even_mask(rows, lanes)

    def setup(colour, layers):
        first, last = span(own, layers)

        def step(p, carry):
            near = list(neighbours(K, colour, p, pairs, even))
            near[4] = lane_edge(near[4], True)
            near[5] = lane_edge(near[5], False)
            centre = K[colour, p]
            total = near[0]
            for value in near[1:]:
                total = total + value
            diag = 3.0 * centre + 0.5 * total
            inverse = pick(centre > 0.0, 1.0 / diag, 0.0)
            half = 0.5 * inverse
            for i, value in enumerate(near):
                weight = (centre + value) * half
                if i == 4:
                    weight = lane_edge(weight, True)
                if i == 5:
                    weight = lane_edge(weight, False)
                W[colour * 6 + i, p] = weight
            D[colour, p] = diag
            start = S[colour, p] * inverse
            S[colour, p] = start
            if colour == 0:
                U[0, p] = start
            return carry

        lax.fori_loop(first, last, step, 0)
        zero = jnp.zeros((rows, lanes), F32)
        for p in list(range(first)) + list(range(last, pairs)):
            U[colour, p] = zero

    def relaxed(colour, p):
        near = neighbours(U, colour, p, pairs, even)
        total = S[colour, p]
        for i, value in enumerate(near):
            total = total + W[colour * 6 + i, p] * value
        return total

    def half_sweep(colour, layers):
        first, last = span(own, layers)

        def step(p, carry):
            U[colour, p] = relaxed(colour, p)
            return carry

        lax.fori_loop(first, last, step, 0)

    setup(0, depth)
    setup(1, depth - 1)
    half_sweep(1, depth - 1)
    half_sweep(0, depth - 2)
    half_sweep(1, depth - 3)
    first, last = span(own, residual_layers)

    def left(p, carry):
        for colour in (0, 1):
            rest = D[colour, p] * (relaxed(colour, p) - U[colour, p])
            R[colour, p - first + R_PAD[residual_layers]] = rest[8 : rows - 8]
        return carry

    lax.fori_loop(first, last, left, 0)


R_PAD = {0: 2, 1: 0}


def store_field(U, out, own, even):
    rows = U.shape[2]
    for p in range(own):
        red = U[0, HP + p, 8 : rows - 8]
        black = U[1, HP + p, 8 : rows - 8]
        out[2 * p] = pick(even, red, black)
        out[2 * p + 1] = pick(even, black, red)


def restrict_planes(R, at, even):
    red, black = R[0, at], R[1, at]
    odd_below = pick(even, R[1, at - 1], R[0, at - 1])
    even_above = pick(even, R[0, at + 1], R[1, at + 1])
    return (3.0 * (red + black) + (odd_below + even_above)) * 0.125


def row_restriction(rows):
    half = rows // 2
    j = lax.broadcasted_iota(jnp.int32, (half + 8, rows), 0)
    m = lax.broadcasted_iota(jnp.int32, (half + 8, rows), 1)
    inner = (m == 2 * j) | (m == 2 * j + 1)
    outer = (m == 2 * j - 1) | (m == 2 * j + 2)
    main = pick(inner, 0.375, pick(outer, 0.125, 0.0))
    ends = pick(((j == half) & (m == 0)) | ((j == half + 1) & (m == rows - 1)), 0.125, 0.0)
    return pick(j < half, main, ends).astype(F32)


def row_sum(rows):
    j = 2 * lax.broadcasted_iota(jnp.int32, (rows // 2, rows), 0)
    m = lax.broadcasted_iota(jnp.int32, (rows // 2, rows), 1)
    return pick((m == j) | (m == j + 1), 1.0, 0.0).astype(F32)


def product(a, b):
    return jnp.dot(a, b, precision=HIGHEST, preferred_element_type=F32)


def lane_restriction(lanes):
    m = lax.broadcasted_iota(jnp.int32, (lanes, lanes // 2), 0)
    i = 2 * lax.broadcasted_iota(jnp.int32, (lanes, lanes // 2), 1)
    inner = (m == i) | (m == i + 1)
    outer = (m == i - 1) | (m == i + 2)
    return pick(inner, 1.5, pick(outer, 0.5, 0.0)).astype(F32)


def lane_mean(lanes):
    m = lax.broadcasted_iota(jnp.int32, (lanes, lanes // 2), 0)
    i = 2 * lax.broadcasted_iota(jnp.int32, (lanes, lanes // 2), 1)
    return pick((m == i) | (m == i + 1), 0.125, 0.0).astype(F32)


def coarsen(K, R, Z, Zk, even_own, own, s_pairs, r_pad, k_pairs):
    rows, lanes = R.shape[2:]
    half = rows // 2
    block = half + 8
    for q, pair in enumerate(s_pairs):
        Z[block * q : block * (q + 1)] = product(
            row_restriction(rows), restrict_planes(R, pair + r_pad, even_own))
    for q, pair in enumerate(k_pairs):
        total = K[0, HP + pair, 8 : 8 + rows] + K[1, HP + pair, 8 : 8 + rows]
        Zk[half * q : half * (q + 1)] = product(row_sum(rows), total)
    source = product(Z[...], lane_restriction(lanes))
    mean = product(Zk[...], lane_mean(lanes))
    return source, mean, half, len(s_pairs)


def row_messages(source, mean, half, count, s_at, k_at, planes, to_low, to_high):
    lanes = source.shape[1]
    block = half + 8
    for q in range(planes):
        low, high = [], []
        if q - s_at in range(count):
            at = block * (q - s_at)
            low += [source[at + half : at + half + 1], source[at : at + 4]]
            high += [source[at + half + 1 : at + half + 2], source[at + half - 4 : at + half]]
            pad = [jnp.zeros((3, lanes), F32)]
        else:
            pad = [jnp.zeros((8, lanes), F32)]
        low, high = low + pad, high + pad
        if q - k_at in range(mean.shape[0] // half):
            at = half * (q - k_at)
            low += [mean[at : at + 5]]
            high += [mean[at + half - 5 : at + half]]
            pad = [jnp.zeros((3, lanes), F32)]
        else:
            pad = [jnp.zeros((8, lanes), F32)]
        to_low[q] = jnp.concatenate(low + pad, axis=0)
        to_high[q] = jnp.concatenate(high + pad, axis=0)


def pack_rows_kernel(s_low, s_high, k_low, k_high, to_low, to_high):
    lanes = s_low.shape[2]
    even = even_mask(8, lanes)

    def step(p, carry):
        def pair(ref):
            a, b = ref[2 * p], ref[2 * p + 1]
            return pick(even, a, b), pick(even, b, a)

        sr, sb = pair(s_low)
        kr, kb = pair(k_low)
        to_low[0, p] = jnp.concatenate([kr[0:4], sr[0:4]], axis=0)
        to_low[1, p] = jnp.concatenate([kb[0:5], sb[0:3]], axis=0)
        sr, sb = pair(s_high)
        kr, kb = pair(k_high)
        to_high[0, p] = jnp.concatenate([kr[4:8], sr[4:8]], axis=0)
        to_high[1, p] = jnp.concatenate([kb[3:8], sb[5:8]], axis=0)
        return carry

    lax.fori_loop(0, s_low.shape[0] // 2, step, 0)


def pack_planes_kernel(s, k, from_low, from_high, to_down, to_up):
    planes, rows, lanes = s.shape
    even = even_mask(8, lanes)

    def edges(p, of_k):
        lr, lb = from_low[0, p], from_low[1, p]
        hr, hb = from_high[0, p], from_high[1, p]
        if of_k:
            red = jnp.concatenate([lr[0:4], hr[0:4]], axis=0)
            black = jnp.concatenate([lb[1:5], hb[0:4]], axis=0)
        else:
            red = jnp.concatenate([lr[4:8], hr[4:8]], axis=0)
            black = jnp.concatenate([lb[4:8], hb[5:8], hb[7:8]], axis=0)
        return pick(even, red, black), pick(even, black, red)

    def put(out, at, ref, plane, of_k):
        out[at, 0:rows] = ref[plane]
        out[at, rows : rows + 8] = edges(plane // 2, of_k)[plane % 2]

    for j in range(4):
        put(to_down, j, s, j, False)
        put(to_up, j, s, planes - 4 + j, False)
    for j in range(5):
        put(to_down, 4 + j, k, j, True)
        put(to_up, 4 + j, k, planes - 5 + j, True)


def fine_kernel(s, k, from_low, from_high, from_down, from_up,
                field, source_out, mean_out, to_low, to_high,
                K, S, U, W, D, R, Z, Zk):
    planes, rows, lanes = s.shape
    own = planes // 2
    wide = rows + 16
    even = even_mask(8, lanes)
    even_own = even_mask(rows, lanes)
    row = row_index(lanes)
    zero8 = jnp.zeros((8, lanes), F32)
    zero = jnp.zeros((wide, lanes), F32)

    def fill(p, carry):
        at = HP + p
        lr, lb = from_low[0, p], from_low[1, p]
        hr, hb = from_high[0, p], from_high[1, p]
        K[0, at, 0:8] = pick(row >= 4, pltpu.roll(lr, 4, 0), 0.0)
        K[1, at, 0:8] = pick(row >= 3, pltpu.roll(lb, 3, 0), 0.0)
        S[0, at, 0:8] = pick(row >= 4, lr, 0.0)
        S[1, at, 0:8] = pick(row >= 5, lb, 0.0)
        K[0, at, 8 + rows : wide] = pick(row < 4, hr, 0.0)
        K[1, at, 8 + rows : wide] = pick(row < 5, hb, 0.0)
        S[0, at, 8 + rows : wide] = pick(row < 4, pltpu.roll(hr, 4, 0), 0.0)
        S[1, at, 8 + rows : wide] = pick(row < 3, pltpu.roll(hb, 3, 0), 0.0)
        for ref, to in ((s, S), (k, K)):
            a, b = ref[2 * p], ref[2 * p + 1]
            to[0, at, 8 : 8 + rows] = pick(even_own, a, b)
            to[1, at, 8 : 8 + rows] = pick(even_own, b, a)
        return carry

    lax.fori_loop(0, own, fill, 0)

    def halo(to, at, ref, first, second):
        def part(rows_of):
            a = zero8 if first is None else rows_of(first)
            b = zero8 if second is None else rows_of(second)
            return a, b

        def put(start, a, b, mask):
            to[0, at, start : start + a.shape[0]] = pick(mask, a, b)
            to[1, at, start : start + a.shape[0]] = pick(mask, b, a)

        a, b = part(lambda j: pick(row >= 4, pltpu.roll(ref[j, rows : rows + 8], 4, 0), 0.0))
        put(0, a, b, even)
        a, b = part(lambda j: pick(row < 4, pltpu.roll(ref[j, rows : rows + 8], 4, 0), 0.0))
        put(8 + rows, a, b, even)
        big = jnp.zeros((rows, lanes), F32)
        a = big if first is None else ref[first, 0:rows]
        b = big if second is None else ref[second, 0:rows]
        put(8, a, b, even_own)

    halo(S, 1, from_down, 0, 1)
    halo(S, 2, from_down, 2, 3)
    halo(K, 0, from_down, None, 4)
    halo(K, 1, from_down, 5, 6)
    halo(K, 2, from_down, 7, 8)
    halo(S, HP + own, from_up, 0, 1)
    halo(S, HP + own + 1, from_up, 2, 3)
    halo(K, HP + own, from_up, 4, 5)
    halo(K, HP + own + 1, from_up, 6, 7)
    halo(K, HP + own + 2, from_up, 8, None)
    relax_level(K, S, U, W, D, R, own, 4, 0)
    store_field(U, field, own, even_own)
    zero = jnp.zeros((rows, lanes), F32)
    for colour in (0, 1):
        for at in (0, 1, own + 2, own + 3):
            R[colour, at] = zero
    source, mean, half, count = coarsen(
        K, R, Z, Zk, even_own, own, range(-1, own + 1), 2, range(own))
    for q in range(count):
        at = (half + 8) * q
        source_out[q] = source[at : at + half]
    for q in range(own):
        mean_out[q] = mean[half * q : half * (q + 1)]
    row_messages(source, mean, half, count, 0, 1, own + 2, to_low, to_high)


def widen(own_rows, mine_low, mine_high, got_low, got_high):
    rows, lanes = own_rows.shape
    row = row_index(lanes)
    low = pltpu.roll(got_low[0:8], 3, 0)
    low = pick(row >= 4, low, 0.0) + pick(row == 7, pltpu.roll(mine_low[0:8], 7, 0), 0.0)
    high = pick(row < 4, pltpu.roll(got_high[0:8], 7, 0), 0.0)
    high = high + pick(row == 0, mine_high[0:8], 0.0)
    first = pick(row == 0, got_low[0:8], 0.0)
    last = pick(row == 7, pltpu.roll(got_high[0:8], 7, 0), 0.0)
    if rows == 8:
        return jnp.concatenate([low, own_rows + first + last, high], axis=0)
    return jnp.concatenate(
        [low, own_rows[0:8] + first, own_rows[8 : rows - 8], own_rows[rows - 8 :] + last, high]
        if rows > 16 else
        [low, own_rows[0:8] + first, own_rows[8:16] + last, high], axis=0)


def widen_mean(own_rows, got_low, got_high):
    rows, lanes = own_rows.shape
    row = row_index(lanes)
    low = pick(row >= 3, pltpu.roll(got_low[8:16], 3, 0), 0.0)
    high = pick(row < 5, got_high[8:16], 0.0)
    return jnp.concatenate([low, own_rows, high], axis=0)


def middle_planes_kernel(source, mean, to_low, to_high, from_low, from_high,
                         S, K, to_down, to_up):
    planes = mean.shape[0]
    for q in range(planes + 2):
        value = widen(source[q], to_low[q], to_high[q], from_low[q], from_high[q])
        S[q] = value
        if q < 6:
            to_down[q] = value
        if q >= planes - 4:
            to_up[q - planes + 4] = value
    for q in range(planes):
        value = widen_mean(mean[q], from_low[q + 1], from_high[q + 1])
        K[q] = value
        if q < 6:
            to_down[6 + q] = value
        if q >= planes - 6:
            to_up[12 + q - planes] = value


def middle_kernel(s, k, from_down, from_up,
                  field, source_out, mean_out, to_low, to_high,
                  K, S, U, W, D, R, Z, Zk):
    planes, wide, lanes = k.shape
    own = planes // 2
    rows = wide - 16
    even = even_mask(wide, lanes)
    even_own = even_mask(rows, lanes)
    zero = jnp.zeros((wide, lanes), F32)

    def source_plane(i):
        if i < -5 or i > planes + 4:
            return zero
        if i < -1:
            return from_down[i + 5]
        if i == -1:
            return from_down[4] + s[0]
        if i == 0:
            return s[1] + from_down[5]
        if i < planes - 1:
            return s[i + 1]
        if i == planes - 1:
            return s[planes] + from_up[0]
        if i == planes:
            return from_up[1] + s[planes + 1]
        return from_up[i - planes + 1]

    def mean_plane(i):
        if i < 0:
            return from_down[12 + i]
        if i < planes:
            return k[i]
        return from_up[6 + i - planes]

    for p in range(-HP, own + HP):
        for to, plane in ((S, source_plane), (K, mean_plane)):
            a, b = plane(2 * p), plane(2 * p + 1)
            to[0, HP + p] = pick(even, a, b)
            to[1, HP + p] = pick(even, b, a)
    relax_level(K, S, U, W, D, R, own, 5, 1)
    store_field(U, field, own, even_own)
    source, mean, half, count = coarsen(
        K, R, Z, Zk, even_own, own, range(own), 1, range(-1, own + 1))
    for q in range(count):
        at = (half + 8) * q
        source_out[q] = source[at : at + half]
    for q in range(own + 2):
        mean_out[q] = mean[half * q : half * (q + 1)]
    row_messages(source, mean, half, count, 1, 0, own + 2, to_low, to_high)


def coarse_planes_kernel(source, mean, to_low, to_high, from_low, from_high,
                         S, K, to_down, to_up):
    planes = source.shape[0]
    for q in range(planes):
        value = widen(source[q], to_low[q + 1], to_high[q + 1], from_low[q + 1], from_high[q + 1])
        S[q] = value
        if q < 4:
            to_down[q] = value
        if q >= planes - 4:
            to_up[q - planes + 4] = value
    for q in range(planes + 2):
        value = widen_mean(mean[q], from_low[q], from_high[q])
        if 1 <= q <= planes:
            K[q - 1] = value
        if 1 <= q <= 5:
            to_down[3 + q] = value
        if planes - 4 <= q <= planes:
            to_up[8 + q - planes] = value


def coarse_kernel(s, k, from_down, from_up, field, rest, K, S, U, W, D, R):
    planes, wide, lanes = k.shape
    own = planes // 2
    rows = wide - 16
    even = even_mask(wide, lanes)
    even_own = even_mask(rows, lanes)
    zero = jnp.zeros((wide, lanes), F32)

    def source_plane(i):
        if i < -4 or i > planes + 3:
            return zero
        if i < 0:
            return from_down[4 + i]
        return s[i] if i < planes else from_up[i - planes]

    def mean_plane(i):
        if i < -5 or i > planes + 4:
            return zero
        if i < 0:
            return from_down[9 + i]
        return k[i] if i < planes else from_up[4 + i - planes]

    for p in range(-HP, own + HP):
        for to, plane in ((S, source_plane), (K, mean_plane)):
            a, b = plane(2 * p), plane(2 * p + 1)
            to[0, HP + p] = pick(even, a, b)
            to[1, HP + p] = pick(even, b, a)
    relax_level(K, S, U, W, D, R, own, 4, 0)
    store_field(U, field, own, even_own)
    for p in range(own):
        red, black = R[0, p + 2], R[1, p + 2]
        rest[2 * p] = pick(even_own, red, black)
        rest[2 * p + 1] = pick(even_own, black, red)


def call(kernel, outs, scratch, *args, in_specs=None, name=None):
    extra = {} if in_specs is None else {"in_specs": in_specs, "grid": (1,)}
    if in_specs is not None:
        extra["out_specs"] = [pl.BlockSpec(o, lambda i, n=len(o): (0,) * n) for o in outs]
    return pl.pallas_call(
        kernel,
        out_shape=[jax.ShapeDtypeStruct(o, F32) for o in outs],
        scratch_shapes=[pltpu.VMEM(shape, F32) for shape in scratch],
        name=name,
        **extra,
    )(*args)


def level_scratch(own, wide, lanes, r_pairs):
    pairs = own + 2 * HP
    return [
        (2, pairs, wide, lanes),
        (2, pairs, wide, lanes),
        (2, pairs, wide, lanes),
        (12, pairs, wide, lanes),
        (2, pairs, wide, lanes),
        (2, r_pairs, wide - 16, lanes),
    ]


def exchange(to_low, to_high, axis):
    size = lax.axis_size(axis)
    up = [(i, i + 1) for i in range(size - 1)]
    down = [(i + 1, i) for i in range(size - 1)]
    return lax.ppermute(to_high, axis, up), lax.ppermute(to_low, axis, down)


def body(right_side, coefficient):
    s, k = right_side, coefficient
    planes, rows, lanes = s.shape
    own = planes // 2
    wide = rows + 16

    low = pl.BlockSpec((planes, 8, lanes), lambda i: (0, 0, 0))
    high = pl.BlockSpec((planes, 8, lanes), lambda i: (0, rows // 8 - 1, 0))
    message = (2, own, 8, lanes)
    to_low, to_high = call(pack_rows_kernel, [message] * 2, [], s, s, k, k,
                           in_specs=[low, high, low, high], name="pack_rows")
    from_low, from_high = exchange(to_low, to_high, "inner")
    message = (9, rows + 8, lanes)
    to_down, to_up = call(pack_planes_kernel, [message] * 2, [], s, k, from_low, from_high,
                          name="pack_planes")
    from_down, from_up = exchange(to_down, to_up, "outer")

    count, half = own + 2, rows // 2
    message = (own + 2, 16, lanes // 2)
    field0, source, mean, to_low, to_high = call(
        fine_kernel,
        [s.shape, (count, half, lanes // 2), (own, half, lanes // 2), message, message],
        level_scratch(own, wide, lanes, own + 4)
        + [((half + 8) * count, lanes), (half * own, lanes)],
        s, k, from_low, from_high, from_down, from_up, name="fine_level")

    planes, rows, lanes = own, half, lanes // 2
    own, wide = planes // 2, rows + 16
    from_low, from_high = exchange(to_low, to_high, "inner")
    message = (12, wide, lanes)
    s1, k1, to_down, to_up = call(
        middle_planes_kernel, [(planes + 2, wide, lanes), (planes, wide, lanes), message, message], [],
        source, mean, to_low, to_high, from_low, from_high, name="middle_planes")
    from_down, from_up = exchange(to_down, to_up, "outer")
    half = rows // 2
    message = (own + 2, 16, lanes // 2)
    field1, source, mean, to_low, to_high = call(
        middle_kernel,
        [(planes, rows, lanes), (own, half, lanes // 2), (own + 2, half, lanes // 2), message, message],
        level_scratch(own, wide, lanes, own + 2)
        + [((half + 8) * own, lanes), (half * (own + 2), lanes)],
        s1, k1, from_down, from_up, name="middle_level")

    planes, rows, lanes = own, half, lanes // 2
    own, wide = planes // 2, rows + 16
    from_low, from_high = exchange(to_low, to_high, "inner")
    message = (9, wide, lanes)
    s2, k2, to_down, to_up = call(
        coarse_planes_kernel, [(planes, wide, lanes), (planes, wide, lanes), message, message], [],
        source, mean, to_low, to_high, from_low, from_high, name="coarse_planes")
    from_down, from_up = exchange(to_down, to_up, "outer")
    field2, rest = call(
        coarse_kernel, [(planes, rows, lanes)] * 2, level_scratch(own, wide, lanes, own + 4),
        s2, k2, from_down, from_up, name="coarse_level")
    return field0, field1, field2, rest


def solution(mesh):
    spec = P("outer", "inner", None)
    return jax.shard_map(body, mesh=mesh, in_specs=(spec, spec), out_specs=(spec,) * 4, check_vma=False)
```

```python
import jax
import jax.numpy as jnp
from jax import lax
from jax.experimental import pallas as pl
from jax.experimental.pallas import tpu as pltpu
from jax.sharding import PartitionSpec as P

F32 = jnp.float32
HP = 3
HIGHEST = lax.Precision.HIGHEST


def tiled(tile, rows, lanes):
    wide = jnp.concatenate([tile] * (lanes // 128), axis=1)
    return jnp.concatenate([wide] * (rows // 8), axis=0)


def even_mask(rows, lanes):
    row = lax.broadcasted_iota(jnp.int32, (8, 128), 0)
    lane = lax.broadcasted_iota(jnp.int32, (8, 128), 1)
    return tiled((row + lane) & 1, rows, lanes) == 0


def pick(mask, a, b):
    return jnp.where(mask, a, b)


def row_index(lanes):
    return lax.broadcasted_iota(jnp.int32, (8, lanes), 0)


def lane_edge(value, at_start):
    lanes = value.shape[1]
    lane = lax.broadcasted_iota(jnp.int32, (value.shape[0], 128), 1)
    if at_start:
        edge = pick(lane == 0, 0.0, value[:, :128])
        return edge if lanes == 128 else jnp.concatenate([edge, value[:, 128:]], axis=1)
    edge = pick(lane == 127, 0.0, value[:, lanes - 128 :])
    return edge if lanes == 128 else jnp.concatenate([value[:, : lanes - 128], edge], axis=1)


def neighbours(ref, colour, p, pairs, even):
    other = 1 - colour
    x = ref[other, p]
    if isinstance(p, int):
        below, above = ref[other, max(p - 1, 0)], ref[other, min(p + 1, pairs - 1)]
    else:
        below = ref[other, jnp.maximum(p - 1, 0)]
        above = ref[other, jnp.minimum(p + 1, pairs - 1)]
    far = pick(even, below, above) if colour == 0 else pick(even, above, below)
    rows, lanes = x.shape
    return (
        x,
        far,
        pltpu.roll(x, 1, 0),
        pltpu.roll(x, rows - 1, 0),
        pltpu.roll(x, 1, 1),
        pltpu.roll(x, lanes - 1, 1),
    )


def span(own, layers):
    extra = (layers + 1) // 2
    return HP - extra, HP + own + extra


def over(first, last, step, unrolled):
    if unrolled:
        for p in range(first, last):
            step(p, 0)
    else:
        lax.fori_loop(first, last, step, 0)


def relax_level(K, S, U, W, D, R, own, depth, residual_layers, inset, unrolled):
    _, pairs, rows, lanes = K.shape
    even = even_mask(rows, lanes)

    def setup(colour, layers):
        first, last = span(own, layers)

        def step(p, carry):
            near = list(neighbours(K, colour, p, pairs, even))
            near[4] = lane_edge(near[4], True)
            near[5] = lane_edge(near[5], False)
            centre = K[colour, p]
            total = near[0]
            for value in near[1:]:
                total = total + value
            diag = 3.0 * centre + 0.5 * total
            inverse = pick(centre > 0.0, 1.0 / diag, 0.0)
            half = 0.5 * inverse
            for i, value in enumerate(near):
                weight = (centre + value) * half
                if i == 4:
                    weight = lane_edge(weight, True)
                if i == 5:
                    weight = lane_edge(weight, False)
                W[colour * 6 + i, p] = weight
            D[colour, p] = diag
            start = S[colour, p] * inverse
            S[colour, p] = start
            if colour == 0:
                U[0, p] = start
            return carry

        over(first, last, step, unrolled)
        zero = jnp.zeros((rows, lanes), F32)
        for p in list(range(first)) + list(range(last, pairs)):
            U[colour, p] = zero

    def relaxed(colour, p):
        near = neighbours(U, colour, p, pairs, even)
        total = S[colour, p]
        for i, value in enumerate(near):
            total = total + W[colour * 6 + i, p] * value
        return total

    def half_sweep(colour, layers):
        first, last = span(own, layers)

        def step(p, carry):
            U[colour, p] = relaxed(colour, p)
            return carry

        over(first, last, step, unrolled)

    setup(0, depth)
    setup(1, depth - 1)
    half_sweep(1, depth - 1)
    half_sweep(0, depth - 2)
    half_sweep(1, depth - 3)
    first, last = span(own, residual_layers)

    def left(p, carry):
        for colour in (0, 1):
            rest = D[colour, p] * (relaxed(colour, p) - U[colour, p])
            R[colour, p - first + R_PAD[residual_layers]] = rest[inset : rows - inset]
        return carry

    over(first, last, left, unrolled)


R_PAD = {0: 2, 1: 0}


def store_field(U, out, own, even):
    rows = out.shape[1]
    first = (U.shape[2] - rows) // 2
    for p in range(own):
        red = U[0, HP + p, first : first + rows]
        black = U[1, HP + p, first : first + rows]
        out[2 * p] = pick(even, red, black)
        out[2 * p + 1] = pick(even, black, red)


def restrict_planes(R, at, even):
    red, black = R[0, at], R[1, at]
    odd_below = pick(even, R[1, at - 1], R[0, at - 1])
    even_above = pick(even, R[0, at + 1], R[1, at + 1])
    return (3.0 * (red + black) + (odd_below + even_above)) * 0.125


def row_restriction(rows, ends):
    half = rows // 2
    shape = (half + 8 if ends else half, rows)
    j = lax.broadcasted_iota(jnp.int32, shape, 0)
    m = lax.broadcasted_iota(jnp.int32, shape, 1)
    inner = (m == 2 * j) | (m == 2 * j + 1)
    outer = (m == 2 * j - 1) | (m == 2 * j + 2)
    main = pick(inner, 0.375, pick(outer, 0.125, 0.0)).astype(F32)
    if not ends:
        return main
    edge = pick(((j == half) & (m == 0)) | ((j == half + 1) & (m == rows - 1)), 0.125, 0.0)
    return pick(j < half, main, edge).astype(F32)


def row_sum(rows):
    j = 2 * lax.broadcasted_iota(jnp.int32, (rows // 2, rows), 0)
    m = lax.broadcasted_iota(jnp.int32, (rows // 2, rows), 1)
    return pick((m == j) | (m == j + 1), 1.0, 0.0).astype(F32)


def product(a, b):
    return jnp.dot(a, b, precision=HIGHEST, preferred_element_type=F32)


def lane_restriction(lanes):
    m = lax.broadcasted_iota(jnp.int32, (lanes, lanes // 2), 0)
    i = 2 * lax.broadcasted_iota(jnp.int32, (lanes, lanes // 2), 1)
    inner = (m == i) | (m == i + 1)
    outer = (m == i - 1) | (m == i + 2)
    return pick(inner, 1.5, pick(outer, 0.5, 0.0)).astype(F32)


def lane_mean(lanes):
    m = lax.broadcasted_iota(jnp.int32, (lanes, lanes // 2), 0)
    i = 2 * lax.broadcasted_iota(jnp.int32, (lanes, lanes // 2), 1)
    return pick((m == i) | (m == i + 1), 0.125, 0.0).astype(F32)


def pack_rows_kernel(s_low, s_high, k_low, k_high, to_low, to_high):
    lanes = s_low.shape[2]
    even = even_mask(8, lanes)

    def step(p, carry):
        def pair(ref):
            a, b = ref[2 * p], ref[2 * p + 1]
            return pick(even, a, b), pick(even, b, a)

        sr, sb = pair(s_low)
        kr, kb = pair(k_low)
        to_low[0, p] = jnp.concatenate([kr[0:4], sr[0:4]], axis=0)
        to_low[1, p] = jnp.concatenate([kb[0:5], sb[0:3]], axis=0)
        sr, sb = pair(s_high)
        kr, kb = pair(k_high)
        to_high[0, p] = jnp.concatenate([kr[4:8], sr[4:8]], axis=0)
        to_high[1, p] = jnp.concatenate([kb[3:8], sb[5:8]], axis=0)
        return carry

    lax.fori_loop(0, s_low.shape[0] // 2, step, 0)


def pack_planes_kernel(s, k, from_low, from_high, to_down, to_up):
    planes, rows, lanes = s.shape
    even = even_mask(8, lanes)

    def edges(p, of_k):
        lr, lb = from_low[0, p], from_low[1, p]
        hr, hb = from_high[0, p], from_high[1, p]
        if of_k:
            red = jnp.concatenate([lr[0:4], hr[0:4]], axis=0)
            black = jnp.concatenate([lb[1:5], hb[0:4]], axis=0)
        else:
            red = jnp.concatenate([lr[4:8], hr[4:8]], axis=0)
            black = jnp.concatenate([lb[4:8], hb[5:8], hb[7:8]], axis=0)
        return pick(even, red, black), pick(even, black, red)

    def put(out, at, ref, plane, of_k):
        out[at, 0:rows] = ref[plane]
        out[at, rows : rows + 8] = edges(plane // 2, of_k)[plane % 2]

    for j in range(4):
        put(to_down, j, s, j, False)
        put(to_up, j, s, planes - 4 + j, False)
    for j in range(5):
        put(to_down, 4 + j, k, j, True)
        put(to_up, 4 + j, k, planes - 5 + j, True)


def mean_kernel(k, out, Z):
    planes, rows, lanes = k.shape
    half = rows // 2
    for q in range(planes // 2):
        Z[half * q : half * (q + 1)] = product(row_sum(rows), k[2 * q] + k[2 * q + 1])
    mean = product(Z[...], lane_mean(lanes))
    for q in range(planes // 2):
        out[q] = mean[half * q : half * (q + 1)]


def fine_kernel(s, k, from_low, from_high, from_down, from_up,
                field, source_out, to_low, to_high,
                K, S, U, W, D, R, Z):
    planes, rows, lanes = s.shape
    own = planes // 2
    wide = rows + 16
    even = even_mask(8, lanes)
    even_own = even_mask(rows, lanes)
    row = row_index(lanes)
    zero8 = jnp.zeros((8, lanes), F32)
    zero = jnp.zeros((wide, lanes), F32)

    def fill(p, carry):
        at = HP + p
        lr, lb = from_low[0, p], from_low[1, p]
        hr, hb = from_high[0, p], from_high[1, p]
        K[0, at, 0:8] = pick(row >= 4, pltpu.roll(lr, 4, 0), 0.0)
        K[1, at, 0:8] = pick(row >= 3, pltpu.roll(lb, 3, 0), 0.0)
        S[0, at, 0:8] = pick(row >= 4, lr, 0.0)
        S[1, at, 0:8] = pick(row >= 5, lb, 0.0)
        K[0, at, 8 + rows : wide] = pick(row < 4, hr, 0.0)
        K[1, at, 8 + rows : wide] = pick(row < 5, hb, 0.0)
        S[0, at, 8 + rows : wide] = pick(row < 4, pltpu.roll(hr, 4, 0), 0.0)
        S[1, at, 8 + rows : wide] = pick(row < 3, pltpu.roll(hb, 3, 0), 0.0)
        for ref, to in ((s, S), (k, K)):
            a, b = ref[2 * p], ref[2 * p + 1]
            to[0, at, 8 : 8 + rows] = pick(even_own, a, b)
            to[1, at, 8 : 8 + rows] = pick(even_own, b, a)
        return carry

    lax.fori_loop(0, own, fill, 0)

    def halo(to, at, ref, first, second):
        def part(rows_of):
            a = zero8 if first is None else rows_of(first)
            b = zero8 if second is None else rows_of(second)
            return a, b

        def put(start, a, b, mask):
            to[0, at, start : start + a.shape[0]] = pick(mask, a, b)
            to[1, at, start : start + a.shape[0]] = pick(mask, b, a)

        a, b = part(lambda j: pick(row >= 4, pltpu.roll(ref[j, rows : rows + 8], 4, 0), 0.0))
        put(0, a, b, even)
        a, b = part(lambda j: pick(row < 4, pltpu.roll(ref[j, rows : rows + 8], 4, 0), 0.0))
        put(8 + rows, a, b, even)
        big = jnp.zeros((rows, lanes), F32)
        a = big if first is None else ref[first, 0:rows]
        b = big if second is None else ref[second, 0:rows]
        put(8, a, b, even_own)

    halo(S, 1, from_down, 0, 1)
    halo(S, 2, from_down, 2, 3)
    halo(K, 0, from_down, None, 4)
    halo(K, 1, from_down, 5, 6)
    halo(K, 2, from_down, 7, 8)
    halo(S, HP + own, from_up, 0, 1)
    halo(S, HP + own + 1, from_up, 2, 3)
    halo(K, HP + own, from_up, 4, 5)
    halo(K, HP + own + 1, from_up, 6, 7)
    halo(K, HP + own + 2, from_up, 8, None)
    relax_level(K, S, U, W, D, R, own, 4, 0, 8, False)
    store_field(U, field, own, even_own)
    zero = jnp.zeros((rows, lanes), F32)
    for colour in (0, 1):
        for at in (0, 1, own + 2, own + 3):
            R[colour, at] = zero
    half = rows // 2
    block = half + 8
    for q in range(own + 2):
        Z[block * q : block * (q + 1)] = product(
            row_restriction(rows, True), restrict_planes(R, q + 1, even_own))
    source = product(Z[...], lane_restriction(lanes))
    row = lax.broadcasted_iota(jnp.int32, (half, lanes // 2), 0)
    for q in range(own + 2):
        at = block * q
        rows_of = source[at : at + half]
        source_out[q] = rows_of
        to_low[q] = pick(row == half - 1, source[at + half : at + half + 1], rows_of)
        to_high[q] = pick(row == 0, source[at + half + 1 : at + half + 2], rows_of)


def mean_planes_kernel(own_rows, from_low, from_high, K, to_down, to_up):
    planes, rows, _ = own_rows.shape
    for q in range(planes):
        for out, at in ((K, q), (to_down, q), (to_up, q - planes + 6)):
            if 0 <= at < out.shape[0]:
                out[at, 0:rows] = from_low[q]
                out[at, rows : 2 * rows] = own_rows[q]
                out[at, 2 * rows : 3 * rows] = from_high[q]


def source_planes_kernel(own_rows, to_low, to_high, from_low, from_high, S, to_down, to_up):
    planes, rows, lanes = own_rows.shape
    row = lax.broadcasted_iota(jnp.int32, (rows, lanes), 0)
    first, last = row == 0, row == rows - 1
    for q in range(planes):
        got_low, got_high = from_low[q], from_high[q]
        low = pick(first, 0.0, got_low) + pick(last, to_low[q], 0.0)
        mine = own_rows[q] + pick(first, got_low, 0.0) + pick(last, got_high, 0.0)
        high = pick(last, 0.0, got_high) + pick(first, to_high[q], 0.0)
        for out, at in ((S, q), (to_down, q), (to_up, q - planes + 6)):
            if 0 <= at < out.shape[0]:
                out[at, 0:rows] = low
                out[at, rows : 2 * rows] = mine
                out[at, 2 * rows : 3 * rows] = high


def middle_kernel(s, k, from_down, from_up, k_down, k_up,
                  field, s_next, k_next, to_down, to_up,
                  K, S, U, W, D, R, Z, Zk):
    planes, wide, lanes = k.shape
    own = planes // 2
    even = even_mask(wide, lanes)
    zero = jnp.zeros((wide, lanes), F32)

    def source_plane(i):
        if i < -5 or i > planes + 4:
            return zero
        if i < -1:
            return from_down[i + 5]
        if i == -1:
            return from_down[4] + s[0]
        if i == 0:
            return s[1] + from_down[5]
        if i < planes - 1:
            return s[i + 1]
        if i == planes - 1:
            return s[planes] + from_up[0]
        if i == planes:
            return from_up[1] + s[planes + 1]
        return from_up[i - planes + 1]

    def mean_plane(i):
        if i < 0:
            return k_down[6 + i]
        if i < planes:
            return k[i]
        return k_up[i - planes]

    for p in range(-HP, own + HP):
        for to, plane in ((S, source_plane), (K, mean_plane)):
            a, b = plane(2 * p), plane(2 * p + 1)
            to[0, HP + p] = pick(even, a, b)
            to[1, HP + p] = pick(even, b, a)
    relax_level(K, S, U, W, D, R, own, 5, 1, 0, True)
    rows = field.shape[1]
    store_field(U, field, own, even_mask(rows, lanes))
    half = wide // 2
    for q in range(own):
        Z[half * q : half * (q + 1)] = product(
            row_restriction(wide, False), restrict_planes(R, q + 1, even))
    for q in range(own + 2):
        total = K[0, HP - 1 + q] + K[1, HP - 1 + q]
        Zk[half * q : half * (q + 1)] = product(row_sum(wide), total)
    source = product(Z[...], lane_restriction(lanes))
    mean = product(Zk[...], lane_mean(lanes))
    for q in range(own):
        value = source[half * q : half * (q + 1)]
        s_next[q] = value
        if q < 4:
            to_down[q] = value
        if q >= own - 4:
            to_up[q - own + 4] = value
    for q in range(own + 2):
        value = mean[half * q : half * (q + 1)]
        if 1 <= q <= own:
            k_next[q - 1] = value
        if 1 <= q <= 5:
            to_down[3 + q] = value
        if own - 4 <= q <= own:
            to_up[8 + q - own] = value


def coarse_kernel(s, k, from_down, from_up, field, rest, K, S, U, W, D, R):
    planes, wide, lanes = k.shape
    own = planes // 2
    rows = field.shape[1]
    even = even_mask(wide, lanes)
    even_own = even_mask(rows, lanes)
    zero = jnp.zeros((wide, lanes), F32)

    def source_plane(i):
        if i < -4 or i > planes + 3:
            return zero
        if i < 0:
            return from_down[4 + i]
        return s[i] if i < planes else from_up[i - planes]

    def mean_plane(i):
        if i < -5 or i > planes + 4:
            return zero
        if i < 0:
            return from_down[9 + i]
        return k[i] if i < planes else from_up[4 + i - planes]

    for p in range(-HP, own + HP):
        for to, plane in ((S, source_plane), (K, mean_plane)):
            a, b = plane(2 * p), plane(2 * p + 1)
            to[0, HP + p] = pick(even, a, b)
            to[1, HP + p] = pick(even, b, a)
    relax_level(K, S, U, W, D, R, own, 4, 0, (wide - rows) // 2, True)
    store_field(U, field, own, even_own)
    for p in range(own):
        red, black = R[0, p + 2], R[1, p + 2]
        rest[2 * p] = pick(even_own, red, black)
        rest[2 * p + 1] = pick(even_own, black, red)


def call(kernel, outs, scratch, *args, in_specs=None, name=None):
    extra = {} if in_specs is None else {"in_specs": in_specs, "grid": (1,)}
    if in_specs is not None:
        extra["out_specs"] = [pl.BlockSpec(o, lambda i, n=len(o): (0,) * n) for o in outs]
    return pl.pallas_call(
        kernel,
        out_shape=[jax.ShapeDtypeStruct(o, F32) for o in outs],
        scratch_shapes=[pltpu.VMEM(shape, F32) for shape in scratch],
        name=name,
        **extra,
    )(*args)


def level_scratch(own, wide, lanes, r_pairs, r_rows):
    pairs = own + 2 * HP
    block = (2, pairs, wide, lanes)
    return [block, block, block, (12, pairs, wide, lanes), block, (2, r_pairs, r_rows, lanes)]


def exchange(to_low, to_high, axis):
    size = lax.axis_size(axis)
    up = [(i, i + 1) for i in range(size - 1)]
    down = [(i + 1, i) for i in range(size - 1)]
    return lax.ppermute(to_high, axis, up), lax.ppermute(to_low, axis, down)


def body(right_side, coefficient):
    s, k = right_side, coefficient
    planes, rows, lanes = s.shape
    own = planes // 2
    wide = rows + 16

    low = pl.BlockSpec((planes, 8, lanes), lambda i: (0, 0, 0))
    high = pl.BlockSpec((planes, 8, lanes), lambda i: (0, rows // 8 - 1, 0))
    message = (2, own, 8, lanes)
    to_low, to_high = call(pack_rows_kernel, [message] * 2, [], s, s, k, k,
                           in_specs=[low, high, low, high], name="pack_rows")
    from_low, from_high = exchange(to_low, to_high, "inner")
    half, next_lanes = rows // 2, lanes // 2
    (mean,) = call(mean_kernel, [(own, half, next_lanes)], [(half * own, lanes)], k, name="mean")
    message = (9, rows + 8, lanes)
    to_down, to_up = call(pack_planes_kernel, [message] * 2, [], s, k, from_low, from_high,
                          name="pack_planes")
    mean, to_down, to_up = lax.optimization_barrier((mean, to_down, to_up))
    from_down, from_up = exchange(to_down, to_up, "outer")
    mean_low, mean_high = exchange(mean, mean, "inner")

    count = own + 2
    message = (count, half, next_lanes)
    field0, source, to_low, to_high = call(
        fine_kernel, [s.shape, message, message, message],
        level_scratch(own, wide, lanes, own + 4, rows) + [((half + 8) * count, lanes)],
        s, k, from_low, from_high, from_down, from_up, name="fine_level")

    planes, rows, lanes = own, half, next_lanes
    own, wide = planes // 2, 3 * rows
    mean_low, mean_high, to_low, to_high = lax.optimization_barrier((mean_low, mean_high, to_low, to_high))
    from_low, from_high = exchange(to_low, to_high, "inner")
    message = (6, wide, lanes)
    k1, to_down, to_up = call(
        mean_planes_kernel, [(planes, wide, lanes), message, message], [],
        mean, mean_low, mean_high, name="mean_planes")
    k_down, k_up = exchange(to_down, to_up, "outer")
    s1, to_down, to_up = call(
        source_planes_kernel, [(planes + 2, wide, lanes), message, message], [],
        source, to_low, to_high, from_low, from_high, name="source_planes")
    from_down, from_up = exchange(to_down, to_up, "outer")
    half, next_lanes = wide // 2, lanes // 2
    block, message = (own, half, next_lanes), (9, half, next_lanes)
    field1, s2, k2, to_down, to_up = call(
        middle_kernel, [(planes, rows, lanes), block, block, message, message],
        level_scratch(own, wide, lanes, own + 2, wide) + [(half * own, lanes), (half * (own + 2), lanes)],
        s1, k1, from_down, from_up, k_down, k_up, name="middle_level")

    planes, rows, wide, lanes = own, rows // 2, half, next_lanes
    own = planes // 2
    from_down, from_up = exchange(to_down, to_up, "outer")
    field2, rest = call(
        coarse_kernel, [(planes, rows, lanes)] * 2, level_scratch(own, wide, lanes, own + 4, rows),
        s2, k2, from_down, from_up, name="coarse_level")
    return field0, field1, field2, rest


def solution(mesh):
    spec = P("outer", "inner", None)
    return jax.shard_map(body, mesh=mesh, in_specs=(spec, spec), out_specs=(spec,) * 4, check_vma=False)
```

```python
import jax
import jax.numpy as jnp
from jax import lax
from jax.experimental import pallas as pl
from jax.experimental.pallas import tpu as pltpu
from jax.sharding import PartitionSpec as P

F32 = jnp.float32
HP = 3
HIGHEST = lax.Precision.HIGHEST


def tiled(tile, rows, lanes):
    wide = jnp.concatenate([tile] * (lanes // 128), axis=1)
    return jnp.concatenate([wide] * (rows // 8), axis=0)


def even_mask(rows, lanes):
    row = lax.broadcasted_iota(jnp.int32, (8, 128), 0)
    lane = lax.broadcasted_iota(jnp.int32, (8, 128), 1)
    return tiled((row + lane) & 1, rows, lanes) == 0


def pick(mask, a, b):
    return jnp.where(mask, a, b)


def row_index(lanes):
    return lax.broadcasted_iota(jnp.int32, (8, lanes), 0)


def lane_edge(value, at_start):
    lanes = value.shape[1]
    lane = lax.broadcasted_iota(jnp.int32, (value.shape[0], 128), 1)
    if at_start:
        edge = pick(lane == 0, 0.0, value[:, :128])
        return edge if lanes == 128 else jnp.concatenate([edge, value[:, 128:]], axis=1)
    edge = pick(lane == 127, 0.0, value[:, lanes - 128 :])
    return edge if lanes == 128 else jnp.concatenate([value[:, : lanes - 128], edge], axis=1)


def neighbours(ref, colour, p, pairs, even):
    other = 1 - colour
    x = ref[other, p]
    if isinstance(p, int):
        below, above = ref[other, max(p - 1, 0)], ref[other, min(p + 1, pairs - 1)]
    else:
        below = ref[other, jnp.maximum(p - 1, 0)]
        above = ref[other, jnp.minimum(p + 1, pairs - 1)]
    far = pick(even, below, above) if colour == 0 else pick(even, above, below)
    rows, lanes = x.shape
    return (
        x,
        far,
        pltpu.roll(x, 1, 0),
        pltpu.roll(x, rows - 1, 0),
        pltpu.roll(x, 1, 1),
        pltpu.roll(x, lanes - 1, 1),
    )


def span(own, layers):
    extra = (layers + 1) // 2
    return HP - extra, HP + own + extra


def over(first, last, step, unrolled):
    if unrolled:
        for p in range(first, last):
            step(p, 0)
    else:
        lax.fori_loop(first, last, step, 0)


def relax_level(K, S, U, W, D, R, own, depth, residual_layers, inset, unrolled):
    _, pairs, rows, lanes = K.shape
    even = even_mask(rows, lanes)

    def setup(colour, layers):
        first, last = span(own, layers)

        def step(p, carry):
            near = list(neighbours(K, colour, p, pairs, even))
            near[4] = lane_edge(near[4], True)
            near[5] = lane_edge(near[5], False)
            centre = K[colour, p]
            total = near[0]
            for value in near[1:]:
                total = total + value
            diag = 3.0 * centre + 0.5 * total
            inverse = pick(centre > 0.0, 1.0 / diag, 0.0)
            half = 0.5 * inverse
            for i, value in enumerate(near):
                weight = (centre + value) * half
                if i == 4:
                    weight = lane_edge(weight, True)
                if i == 5:
                    weight = lane_edge(weight, False)
                W[colour * 6 + i, p] = weight
            D[colour, p] = diag
            start = S[colour, p] * inverse
            S[colour, p] = start
            if colour == 0:
                U[0, p] = start
            return carry

        over(first, last, step, unrolled)
        zero = jnp.zeros((rows, lanes), F32)
        for p in list(range(first)) + list(range(last, pairs)):
            U[colour, p] = zero

    def relaxed(colour, p):
        near = neighbours(U, colour, p, pairs, even)
        total = S[colour, p]
        for i, value in enumerate(near):
            total = total + W[colour * 6 + i, p] * value
        return total

    def half_sweep(colour, layers):
        first, last = span(own, layers)

        def step(p, carry):
            U[colour, p] = relaxed(colour, p)
            return carry

        over(first, last, step, unrolled)

    setup(0, depth)
    setup(1, depth - 1)
    half_sweep(1, depth - 1)
    half_sweep(0, depth - 2)
    half_sweep(1, depth - 3)
    first, last = span(own, residual_layers)

    def left(p, carry):
        for colour in (0, 1):
            rest = D[colour, p] * (relaxed(colour, p) - U[colour, p])
            R[colour, p - first + R_PAD[residual_layers]] = rest[inset : rows - inset]
        return carry

    over(first, last, left, unrolled)


R_PAD = {0: 2, 1: 0}


def store_field(U, out, own, even):
    rows = out.shape[1]
    first = (U.shape[2] - rows) // 2
    for p in range(own):
        red = U[0, HP + p, first : first + rows]
        black = U[1, HP + p, first : first + rows]
        out[2 * p] = pick(even, red, black)
        out[2 * p + 1] = pick(even, black, red)


def restrict_planes(R, at, even):
    red, black = R[0, at], R[1, at]
    odd_below = pick(even, R[1, at - 1], R[0, at - 1])
    even_above = pick(even, R[0, at + 1], R[1, at + 1])
    return (3.0 * (red + black) + (odd_below + even_above)) * 0.125


def row_restriction(rows, ends):
    half = rows // 2
    shape = (half + 8 if ends else half, rows)
    j = lax.broadcasted_iota(jnp.int32, shape, 0)
    m = lax.broadcasted_iota(jnp.int32, shape, 1)
    inner = (m == 2 * j) | (m == 2 * j + 1)
    outer = (m == 2 * j - 1) | (m == 2 * j + 2)
    main = pick(inner, 0.375, pick(outer, 0.125, 0.0)).astype(F32)
    if not ends:
        return main
    edge = pick(((j == half) & (m == 0)) | ((j == half + 1) & (m == rows - 1)), 0.125, 0.0)
    return pick(j < half, main, edge).astype(F32)


def row_sum(rows):
    j = 2 * lax.broadcasted_iota(jnp.int32, (rows // 2, rows), 0)
    m = lax.broadcasted_iota(jnp.int32, (rows // 2, rows), 1)
    return pick((m == j) | (m == j + 1), 1.0, 0.0).astype(F32)


def product(a, b):
    return jnp.dot(a, b, precision=HIGHEST, preferred_element_type=F32)


def lane_restriction(lanes):
    m = lax.broadcasted_iota(jnp.int32, (lanes, lanes // 2), 0)
    i = 2 * lax.broadcasted_iota(jnp.int32, (lanes, lanes // 2), 1)
    inner = (m == i) | (m == i + 1)
    outer = (m == i - 1) | (m == i + 2)
    return pick(inner, 1.5, pick(outer, 0.5, 0.0)).astype(F32)


def lane_mean(lanes):
    m = lax.broadcasted_iota(jnp.int32, (lanes, lanes // 2), 0)
    i = 2 * lax.broadcasted_iota(jnp.int32, (lanes, lanes // 2), 1)
    return pick((m == i) | (m == i + 1), 0.125, 0.0).astype(F32)


def pack_rows_kernel(s_low, s_high, k_low, k_high, to_low, to_high):
    lanes = s_low.shape[2]
    even = even_mask(8, lanes)

    def step(p, carry):
        def pair(ref):
            a, b = ref[2 * p], ref[2 * p + 1]
            return pick(even, a, b), pick(even, b, a)

        sr, sb = pair(s_low)
        kr, kb = pair(k_low)
        to_low[0, p] = jnp.concatenate([kr[0:4], sr[0:4]], axis=0)
        to_low[1, p] = jnp.concatenate([kb[0:5], sb[0:3]], axis=0)
        sr, sb = pair(s_high)
        kr, kb = pair(k_high)
        to_high[0, p] = jnp.concatenate([kr[4:8], sr[4:8]], axis=0)
        to_high[1, p] = jnp.concatenate([kb[3:8], sb[5:8]], axis=0)
        return carry

    lax.fori_loop(0, s_low.shape[0] // 2, step, 0)


def pack_planes_kernel(s, k, from_low, from_high, to_down, to_up):
    planes, rows, lanes = s.shape
    even = even_mask(8, lanes)

    def edges(p, of_k):
        lr, lb = from_low[0, p], from_low[1, p]
        hr, hb = from_high[0, p], from_high[1, p]
        if of_k:
            red = jnp.concatenate([lr[0:4], hr[0:4]], axis=0)
            black = jnp.concatenate([lb[1:5], hb[0:4]], axis=0)
        else:
            red = jnp.concatenate([lr[4:8], hr[4:8]], axis=0)
            black = jnp.concatenate([lb[4:8], hb[5:8], hb[7:8]], axis=0)
        return pick(even, red, black), pick(even, black, red)

    def put(out, at, ref, plane, of_k):
        out[at, 0:rows] = ref[plane]
        out[at, rows : rows + 8] = edges(plane // 2, of_k)[plane % 2]

    for j in range(4):
        put(to_down, j, s, j, False)
        put(to_up, j, s, planes - 4 + j, False)
    for j in range(5):
        put(to_down, 4 + j, k, j, True)
        put(to_up, 4 + j, k, planes - 5 + j, True)


def mean_kernel(k, out, Z):
    planes, rows, lanes = k.shape
    half = rows // 2
    for q in range(planes // 2):
        Z[half * q : half * (q + 1)] = product(row_sum(rows), k[2 * q] + k[2 * q + 1])
    mean = product(Z[...], lane_mean(lanes))
    for q in range(planes // 2):
        out[q] = mean[half * q : half * (q + 1)]


def fine_kernel(s, k, from_low, from_high, from_down, from_up,
                field, source_out, to_low, to_high,
                K, S, U, W, D, R, Z):
    planes, rows, lanes = s.shape
    own = planes // 2
    wide = rows + 16
    even = even_mask(8, lanes)
    even_own = even_mask(rows, lanes)
    row = row_index(lanes)
    zero8 = jnp.zeros((8, lanes), F32)
    zero = jnp.zeros((wide, lanes), F32)

    def fill(p, carry):
        at = HP + p
        lr, lb = from_low[0, p], from_low[1, p]
        hr, hb = from_high[0, p], from_high[1, p]
        K[0, at, 0:8] = pick(row >= 4, pltpu.roll(lr, 4, 0), 0.0)
        K[1, at, 0:8] = pick(row >= 3, pltpu.roll(lb, 3, 0), 0.0)
        S[0, at, 0:8] = pick(row >= 4, lr, 0.0)
        S[1, at, 0:8] = pick(row >= 5, lb, 0.0)
        K[0, at, 8 + rows : wide] = pick(row < 4, hr, 0.0)
        K[1, at, 8 + rows : wide] = pick(row < 5, hb, 0.0)
        S[0, at, 8 + rows : wide] = pick(row < 4, pltpu.roll(hr, 4, 0), 0.0)
        S[1, at, 8 + rows : wide] = pick(row < 3, pltpu.roll(hb, 3, 0), 0.0)
        for ref, to in ((s, S), (k, K)):
            a, b = ref[2 * p], ref[2 * p + 1]
            to[0, at, 8 : 8 + rows] = pick(even_own, a, b)
            to[1, at, 8 : 8 + rows] = pick(even_own, b, a)
        return carry

    lax.fori_loop(0, own, fill, 0)

    def halo(to, at, ref, first, second):
        def part(rows_of):
            a = zero8 if first is None else rows_of(first)
            b = zero8 if second is None else rows_of(second)
            return a, b

        def put(start, a, b, mask):
            to[0, at, start : start + a.shape[0]] = pick(mask, a, b)
            to[1, at, start : start + a.shape[0]] = pick(mask, b, a)

        a, b = part(lambda j: pick(row >= 4, pltpu.roll(ref[j, rows : rows + 8], 4, 0), 0.0))
        put(0, a, b, even)
        a, b = part(lambda j: pick(row < 4, pltpu.roll(ref[j, rows : rows + 8], 4, 0), 0.0))
        put(8 + rows, a, b, even)
        big = jnp.zeros((rows, lanes), F32)
        a = big if first is None else ref[first, 0:rows]
        b = big if second is None else ref[second, 0:rows]
        put(8, a, b, even_own)

    halo(S, 1, from_down, 0, 1)
    halo(S, 2, from_down, 2, 3)
    halo(K, 0, from_down, None, 4)
    halo(K, 1, from_down, 5, 6)
    halo(K, 2, from_down, 7, 8)
    halo(S, HP + own, from_up, 0, 1)
    halo(S, HP + own + 1, from_up, 2, 3)
    halo(K, HP + own, from_up, 4, 5)
    halo(K, HP + own + 1, from_up, 6, 7)
    halo(K, HP + own + 2, from_up, 8, None)
    relax_level(K, S, U, W, D, R, own, 4, 0, 8, False)
    store_field(U, field, own, even_own)
    zero = jnp.zeros((rows, lanes), F32)
    for colour in (0, 1):
        for at in (0, 1, own + 2, own + 3):
            R[colour, at] = zero
    half = rows // 2
    block = half + 8
    for q in range(own + 2):
        Z[block * q : block * (q + 1)] = product(
            row_restriction(rows, True), restrict_planes(R, q + 1, even_own))
    source = product(Z[...], lane_restriction(lanes))
    row = lax.broadcasted_iota(jnp.int32, (half, lanes // 2), 0)
    for q in range(own + 2):
        at = block * q
        rows_of = source[at : at + half]
        source_out[q] = rows_of
        to_low[q] = pick(row == half - 1, source[at + half : at + half + 1], rows_of)
        to_high[q] = pick(row == 0, source[at + half + 1 : at + half + 2], rows_of)


def mean_planes_kernel(own_rows, from_low, from_high, K, to_down, to_up):
    planes, rows, _ = own_rows.shape
    for q in range(planes):
        for out, at in ((K, q), (to_down, q), (to_up, q - planes + 6)):
            if 0 <= at < out.shape[0]:
                out[at, 0:rows] = from_low[q]
                out[at, rows : 2 * rows] = own_rows[q]
                out[at, 2 * rows : 3 * rows] = from_high[q]


def source_planes_kernel(own_rows, to_low, to_high, from_low, from_high, S, to_down, to_up):
    planes, rows, lanes = own_rows.shape
    row = lax.broadcasted_iota(jnp.int32, (rows, lanes), 0)
    first, last = row == 0, row == rows - 1
    for q in range(planes):
        got_low, got_high = from_low[q], from_high[q]
        low = pick(first, 0.0, got_low) + pick(last, to_low[q], 0.0)
        mine = own_rows[q] + pick(first, got_low, 0.0) + pick(last, got_high, 0.0)
        high = pick(last, 0.0, got_high) + pick(first, to_high[q], 0.0)
        for out, at in ((S, q), (to_down, q), (to_up, q - planes + 6)):
            if 0 <= at < out.shape[0]:
                out[at, 0:rows] = low
                out[at, rows : 2 * rows] = mine
                out[at, 2 * rows : 3 * rows] = high


def middle_kernel(s, k, from_down, from_up, k_down, k_up,
                  field, s_next, k_next, to_down, to_up,
                  K, S, U, W, D, R, Z, Zk):
    planes, wide, lanes = k.shape
    own = planes // 2
    even = even_mask(wide, lanes)
    zero = jnp.zeros((wide, lanes), F32)

    def source_plane(i):
        if i < -5 or i > planes + 4:
            return zero
        if i < -1:
            return from_down[i + 5]
        if i == -1:
            return from_down[4] + s[0]
        if i == 0:
            return s[1] + from_down[5]
        if i < planes - 1:
            return s[i + 1]
        if i == planes - 1:
            return s[planes] + from_up[0]
        if i == planes:
            return from_up[1] + s[planes + 1]
        return from_up[i - planes + 1]

    def mean_plane(i):
        if i < 0:
            return k_down[6 + i]
        if i < planes:
            return k[i]
        return k_up[i - planes]

    for p in range(-HP, own + HP):
        for to, plane in ((S, source_plane), (K, mean_plane)):
            a, b = plane(2 * p), plane(2 * p + 1)
            to[0, HP + p] = pick(even, a, b)
            to[1, HP + p] = pick(even, b, a)
    relax_level(K, S, U, W, D, R, own, 5, 1, 0, True)
    rows = field.shape[1]
    store_field(U, field, own, even_mask(rows, lanes))
    half = wide // 2
    for q in range(own):
        Z[half * q : half * (q + 1)] = product(
            row_restriction(wide, False), restrict_planes(R, q + 1, even))
    for q in range(own + 2):
        total = K[0, HP - 1 + q] + K[1, HP - 1 + q]
        Zk[half * q : half * (q + 1)] = product(row_sum(wide), total)
    source = product(Z[...], lane_restriction(lanes))
    mean = product(Zk[...], lane_mean(lanes))
    for q in range(own):
        value = source[half * q : half * (q + 1)]
        s_next[q] = value
        if q < 4:
            to_down[q] = value
        if q >= own - 4:
            to_up[q - own + 4] = value
    for q in range(own + 2):
        value = mean[half * q : half * (q + 1)]
        if 1 <= q <= own:
            k_next[q - 1] = value
        if 1 <= q <= 5:
            to_down[3 + q] = value
        if own - 4 <= q <= own:
            to_up[8 + q - own] = value


def coarse_kernel(s, k, from_down, from_up, field, rest, K, S, U, W, D, R):
    planes, wide, lanes = k.shape
    own = planes // 2
    rows = field.shape[1]
    even = even_mask(wide, lanes)
    even_own = even_mask(rows, lanes)
    zero = jnp.zeros((wide, lanes), F32)

    def source_plane(i):
        if i < -4 or i > planes + 3:
            return zero
        if i < 0:
            return from_down[4 + i]
        return s[i] if i < planes else from_up[i - planes]

    def mean_plane(i):
        if i < -5 or i > planes + 4:
            return zero
        if i < 0:
            return from_down[9 + i]
        return k[i] if i < planes else from_up[4 + i - planes]

    for p in range(-HP, own + HP):
        for to, plane in ((S, source_plane), (K, mean_plane)):
            a, b = plane(2 * p), plane(2 * p + 1)
            to[0, HP + p] = pick(even, a, b)
            to[1, HP + p] = pick(even, b, a)
    relax_level(K, S, U, W, D, R, own, 4, 0, (wide - rows) // 2, True)
    store_field(U, field, own, even_own)
    for p in range(own):
        red, black = R[0, p + 2], R[1, p + 2]
        rest[2 * p] = pick(even_own, red, black)
        rest[2 * p + 1] = pick(even_own, black, red)


def limit(scratch):
    words = 0
    for shape in scratch:
        size = 1
        for n in shape:
            size *= n
        words += size
    return 4 * words + (12 << 20)


def call(kernel, outs, scratch, *args, in_specs=None, name=None, results=()):
    extra = {}
    if in_specs is None:
        args = [pltpu.with_memory_space_constraint(a, pltpu.VMEM) for a in args]
    else:
        extra = {"in_specs": in_specs, "grid": (1,)}
        extra["out_specs"] = [pl.BlockSpec(memory_space=pltpu.VMEM) for _ in outs]
    return pl.pallas_call(
        kernel,
        out_shape=[jax.ShapeDtypeStruct(o, F32) if i in results else pltpu.VMEM(o, F32)
                   for i, o in enumerate(outs)],
        scratch_shapes=[pltpu.VMEM(shape, F32) for shape in scratch],
        compiler_params=pltpu.CompilerParams(vmem_limit_bytes=limit(scratch)),
        name=name,
        **extra,
    )(*args)


def level_scratch(own, wide, lanes, r_pairs, r_rows):
    pairs = own + 2 * HP
    block = (2, pairs, wide, lanes)
    return [block, block, block, (12, pairs, wide, lanes), block, (2, r_pairs, r_rows, lanes)]


def exchange(to_low, to_high, axis):
    size = lax.axis_size(axis)
    up = [(i, i + 1) for i in range(size - 1)]
    down = [(i + 1, i) for i in range(size - 1)]
    return lax.ppermute(to_high, axis, up), lax.ppermute(to_low, axis, down)


def body(right_side, coefficient):
    s, k = right_side, coefficient
    planes, rows, lanes = s.shape
    own = planes // 2
    wide = rows + 16

    low = pl.BlockSpec((planes, 8, lanes), lambda i: (0, 0, 0))
    high = pl.BlockSpec((planes, 8, lanes), lambda i: (0, rows // 8 - 1, 0))
    message = (2, own, 8, lanes)
    to_low, to_high = call(pack_rows_kernel, [message] * 2, [], s, s, k, k,
                           in_specs=[low, high, low, high], name="pack_rows")
    from_low, from_high = exchange(to_low, to_high, "inner")
    half, next_lanes = rows // 2, lanes // 2
    (mean,) = call(mean_kernel, [(own, half, next_lanes)], [(half * own, lanes)], k, name="mean")
    message = (9, rows + 8, lanes)
    to_down, to_up = call(pack_planes_kernel, [message] * 2, [], s, k, from_low, from_high,
                          name="pack_planes")
    mean, to_down, to_up = lax.optimization_barrier((mean, to_down, to_up))
    from_down, from_up = exchange(to_down, to_up, "outer")
    mean_low, mean_high = exchange(mean, mean, "inner")

    count = own + 2
    message = (count, half, next_lanes)
    field0, source, to_low, to_high = call(
        fine_kernel, [s.shape, message, message, message],
        level_scratch(own, wide, lanes, own + 4, rows) + [((half + 8) * count, lanes)],
        s, k, from_low, from_high, from_down, from_up, name="fine_level")

    planes, rows, lanes = own, half, next_lanes
    own, wide = planes // 2, 3 * rows
    mean_low, mean_high, to_low, to_high = lax.optimization_barrier((mean_low, mean_high, to_low, to_high))
    from_low, from_high = exchange(to_low, to_high, "inner")
    message = (6, wide, lanes)
    k1, to_down, to_up = call(
        mean_planes_kernel, [(planes, wide, lanes), message, message], [],
        mean, mean_low, mean_high, name="mean_planes")
    k_down, k_up = exchange(to_down, to_up, "outer")
    s1, to_down, to_up = call(
        source_planes_kernel, [(planes + 2, wide, lanes), message, message], [],
        source, to_low, to_high, from_low, from_high, name="source_planes")
    from_down, from_up = exchange(to_down, to_up, "outer")
    half, next_lanes = wide // 2, lanes // 2
    block, message = (own, half, next_lanes), (9, half, next_lanes)
    field1, s2, k2, to_down, to_up = call(
        middle_kernel, [(planes, rows, lanes), block, block, message, message],
        level_scratch(own, wide, lanes, own + 2, wide) + [(half * own, lanes), (half * (own + 2), lanes)],
        s1, k1, from_down, from_up, k_down, k_up, name="middle_level")

    planes, rows, wide, lanes = own, rows // 2, half, next_lanes
    own = planes // 2
    from_down, from_up = exchange(to_down, to_up, "outer")
    field2, rest = call(
        coarse_kernel, [(planes, rows, lanes)] * 2, level_scratch(own, wide, lanes, own + 4, rows),
        s2, k2, from_down, from_up, name="coarse_level")
    return field0, field1, field2, rest


def solution(mesh):
    spec = P("outer", "inner", None)
    return jax.shard_map(body, mesh=mesh, in_specs=(spec, spec), out_specs=(spec,) * 4, check_vma=False)
```

```python
import jax
import jax.numpy as jnp
from jax import lax
from jax.experimental import pallas as pl
from jax.experimental.pallas import tpu as pltpu
from jax.sharding import PartitionSpec as P

F32 = jnp.float32
HP = 3
HIGHEST = lax.Precision.HIGHEST


def tiled(tile, rows, lanes):
    wide = jnp.concatenate([tile] * (lanes // 128), axis=1)
    return jnp.concatenate([wide] * (rows // 8), axis=0)


def even_mask(rows, lanes):
    row = lax.broadcasted_iota(jnp.int32, (8, 128), 0)
    lane = lax.broadcasted_iota(jnp.int32, (8, 128), 1)
    return tiled((row + lane) & 1, rows, lanes) == 0


def pick(mask, a, b):
    return jnp.where(mask, a, b)


def row_index(lanes):
    return lax.broadcasted_iota(jnp.int32, (8, lanes), 0)


def lane_edge(value, at_start):
    lanes = value.shape[1]
    lane = lax.broadcasted_iota(jnp.int32, (value.shape[0], 128), 1)
    if at_start:
        edge = pick(lane == 0, 0.0, value[:, :128])
        return edge if lanes == 128 else jnp.concatenate([edge, value[:, 128:]], axis=1)
    edge = pick(lane == 127, 0.0, value[:, lanes - 128 :])
    return edge if lanes == 128 else jnp.concatenate([value[:, : lanes - 128], edge], axis=1)


def neighbours(ref, colour, p, pairs, even):
    other = 1 - colour
    x = ref[other, p]
    if isinstance(p, int):
        below, above = ref[other, max(p - 1, 0)], ref[other, min(p + 1, pairs - 1)]
    else:
        below = ref[other, jnp.maximum(p - 1, 0)]
        above = ref[other, jnp.minimum(p + 1, pairs - 1)]
    far = pick(even, below, above) if colour == 0 else pick(even, above, below)
    rows, lanes = x.shape
    return (
        x,
        far,
        pltpu.roll(x, 1, 0),
        pltpu.roll(x, rows - 1, 0),
        pltpu.roll(x, 1, 1),
        pltpu.roll(x, lanes - 1, 1),
    )


def span(own, layers):
    extra = (layers + 1) // 2
    return HP - extra, HP + own + extra


def over(first, last, step, unrolled):
    if unrolled:
        for p in range(first, last):
            step(p, 0)
    else:
        lax.fori_loop(first, last, step, 0)


def relax_level(K, S, U, W, D, R, own, depth, residual_layers, inset, unrolled):
    _, pairs, rows, lanes = K.shape
    even = even_mask(rows, lanes)

    def setup(colour, layers):
        first, last = span(own, layers)

        def step(p, carry):
            near = list(neighbours(K, colour, p, pairs, even))
            near[4] = lane_edge(near[4], True)
            near[5] = lane_edge(near[5], False)
            centre = K[colour, p]
            total = near[0]
            for value in near[1:]:
                total = total + value
            diag = 3.0 * centre + 0.5 * total
            inverse = pick(centre > 0.0, 1.0 / diag, 0.0)
            half = 0.5 * inverse
            for i, value in enumerate(near):
                weight = (centre + value) * half
                if i == 4:
                    weight = lane_edge(weight, True)
                if i == 5:
                    weight = lane_edge(weight, False)
                W[colour * 6 + i, p] = weight
            D[colour, p] = diag
            start = S[colour, p] * inverse
            S[colour, p] = start
            if colour == 0:
                U[0, p] = start
            return carry

        over(first, last, step, unrolled)
        zero = jnp.zeros((rows, lanes), F32)
        for p in list(range(first)) + list(range(last, pairs)):
            U[colour, p] = zero

    def relaxed(colour, p):
        near = neighbours(U, colour, p, pairs, even)
        total = S[colour, p]
        for i, value in enumerate(near):
            total = total + W[colour * 6 + i, p] * value
        return total

    def half_sweep(colour, layers):
        first, last = span(own, layers)

        def step(p, carry):
            U[colour, p] = relaxed(colour, p)
            return carry

        over(first, last, step, unrolled)

    setup(0, depth)
    setup(1, depth - 1)
    half_sweep(1, depth - 1)
    half_sweep(0, depth - 2)
    half_sweep(1, depth - 3)
    first, last = span(own, residual_layers)

    def left(p, carry):
        for colour in (0, 1):
            rest = D[colour, p] * (relaxed(colour, p) - U[colour, p])
            R[colour, p - first + R_PAD[residual_layers]] = rest[inset : rows - inset]
        return carry

    over(first, last, left, unrolled)


R_PAD = {0: 2, 1: 0}


def store_field(U, out, own, even):
    rows = out.shape[1]
    first = (U.shape[2] - rows) // 2
    for p in range(own):
        red = U[0, HP + p, first : first + rows]
        black = U[1, HP + p, first : first + rows]
        out[2 * p] = pick(even, red, black)
        out[2 * p + 1] = pick(even, black, red)


def restrict_planes(R, at, even):
    red, black = R[0, at], R[1, at]
    odd_below = pick(even, R[1, at - 1], R[0, at - 1])
    even_above = pick(even, R[0, at + 1], R[1, at + 1])
    return (3.0 * (red + black) + (odd_below + even_above)) * 0.125


def row_restriction(rows, ends):
    half = rows // 2
    shape = (half + 8 if ends else half, rows)
    j = lax.broadcasted_iota(jnp.int32, shape, 0)
    m = lax.broadcasted_iota(jnp.int32, shape, 1)
    inner = (m == 2 * j) | (m == 2 * j + 1)
    outer = (m == 2 * j - 1) | (m == 2 * j + 2)
    main = pick(inner, 0.375, pick(outer, 0.125, 0.0)).astype(F32)
    if not ends:
        return main
    edge = pick(((j == half) & (m == 0)) | ((j == half + 1) & (m == rows - 1)), 0.125, 0.0)
    return pick(j < half, main, edge).astype(F32)


def row_sum(rows):
    j = 2 * lax.broadcasted_iota(jnp.int32, (rows // 2, rows), 0)
    m = lax.broadcasted_iota(jnp.int32, (rows // 2, rows), 1)
    return pick((m == j) | (m == j + 1), 1.0, 0.0).astype(F32)


def product(a, b):
    return jnp.dot(a, b, precision=HIGHEST, preferred_element_type=F32)


def lane_restriction(lanes):
    m = lax.broadcasted_iota(jnp.int32, (lanes, lanes // 2), 0)
    i = 2 * lax.broadcasted_iota(jnp.int32, (lanes, lanes // 2), 1)
    inner = (m == i) | (m == i + 1)
    outer = (m == i - 1) | (m == i + 2)
    return pick(inner, 1.5, pick(outer, 0.5, 0.0)).astype(F32)


def lane_mean(lanes):
    m = lax.broadcasted_iota(jnp.int32, (lanes, lanes // 2), 0)
    i = 2 * lax.broadcasted_iota(jnp.int32, (lanes, lanes // 2), 1)
    return pick((m == i) | (m == i + 1), 0.125, 0.0).astype(F32)


def pack_rows_kernel(s_low, s_high, k_low, k_high, to_low, to_high):
    lanes = s_low.shape[2]
    even = even_mask(8, lanes)

    def step(p, carry):
        def pair(ref):
            a, b = ref[2 * p], ref[2 * p + 1]
            return pick(even, a, b), pick(even, b, a)

        sr, sb = pair(s_low)
        kr, kb = pair(k_low)
        to_low[0, p] = jnp.concatenate([kr[0:4], sr[0:4]], axis=0)
        to_low[1, p] = jnp.concatenate([kb[0:5], sb[0:3]], axis=0)
        sr, sb = pair(s_high)
        kr, kb = pair(k_high)
        to_high[0, p] = jnp.concatenate([kr[4:8], sr[4:8]], axis=0)
        to_high[1, p] = jnp.concatenate([kb[3:8], sb[5:8]], axis=0)
        return carry

    lax.fori_loop(0, s_low.shape[0] // 2, step, 0)


def pack_planes_kernel(s, k, from_low, from_high, to_down, to_up):
    planes, rows, lanes = s.shape
    even = even_mask(8, lanes)

    def edges(p, of_k):
        lr, lb = from_low[0, p], from_low[1, p]
        hr, hb = from_high[0, p], from_high[1, p]
        if of_k:
            red = jnp.concatenate([lr[0:4], hr[0:4]], axis=0)
            black = jnp.concatenate([lb[1:5], hb[0:4]], axis=0)
        else:
            red = jnp.concatenate([lr[4:8], hr[4:8]], axis=0)
            black = jnp.concatenate([lb[4:8], hb[5:8], hb[7:8]], axis=0)
        return pick(even, red, black), pick(even, black, red)

    def put(out, at, ref, plane, of_k):
        out[at, 0:rows] = ref[plane]
        out[at, rows : rows + 8] = edges(plane // 2, of_k)[plane % 2]

    for j in range(4):
        put(to_down, j, s, j, False)
        put(to_up, j, s, planes - 4 + j, False)
    for j in range(5):
        put(to_down, 4 + j, k, j, True)
        put(to_up, 4 + j, k, planes - 5 + j, True)


def mean_kernel(k, out, Z):
    planes, rows, lanes = k.shape
    half = rows // 2
    for q in range(planes // 2):
        Z[half * q : half * (q + 1)] = product(row_sum(rows), k[2 * q] + k[2 * q + 1])
    mean = product(Z[...], lane_mean(lanes))
    for q in range(planes // 2):
        out[q] = mean[half * q : half * (q + 1)]


def fine_kernel(s, k, from_low, from_high, from_down, from_up,
                field, source_out, to_low, to_high,
                K, S, U, W, D, R, Z):
    planes, rows, lanes = s.shape
    own = planes // 2
    wide = rows + 16
    even = even_mask(8, lanes)
    even_own = even_mask(rows, lanes)
    row = row_index(lanes)
    zero8 = jnp.zeros((8, lanes), F32)
    zero = jnp.zeros((wide, lanes), F32)

    def fill(p, carry):
        at = HP + p
        lr, lb = from_low[0, p], from_low[1, p]
        hr, hb = from_high[0, p], from_high[1, p]
        K[0, at, 0:8] = pick(row >= 4, pltpu.roll(lr, 4, 0), 0.0)
        K[1, at, 0:8] = pick(row >= 3, pltpu.roll(lb, 3, 0), 0.0)
        S[0, at, 0:8] = pick(row >= 4, lr, 0.0)
        S[1, at, 0:8] = pick(row >= 5, lb, 0.0)
        K[0, at, 8 + rows : wide] = pick(row < 4, hr, 0.0)
        K[1, at, 8 + rows : wide] = pick(row < 5, hb, 0.0)
        S[0, at, 8 + rows : wide] = pick(row < 4, pltpu.roll(hr, 4, 0), 0.0)
        S[1, at, 8 + rows : wide] = pick(row < 3, pltpu.roll(hb, 3, 0), 0.0)
        for ref, to in ((s, S), (k, K)):
            a, b = ref[2 * p], ref[2 * p + 1]
            to[0, at, 8 : 8 + rows] = pick(even_own, a, b)
            to[1, at, 8 : 8 + rows] = pick(even_own, b, a)
        return carry

    lax.fori_loop(0, own, fill, 0)

    def halo(to, at, ref, first, second):
        def part(rows_of):
            a = zero8 if first is None else rows_of(first)
            b = zero8 if second is None else rows_of(second)
            return a, b

        def put(start, a, b, mask):
            to[0, at, start : start + a.shape[0]] = pick(mask, a, b)
            to[1, at, start : start + a.shape[0]] = pick(mask, b, a)

        a, b = part(lambda j: pick(row >= 4, pltpu.roll(ref[j, rows : rows + 8], 4, 0), 0.0))
        put(0, a, b, even)
        a, b = part(lambda j: pick(row < 4, pltpu.roll(ref[j, rows : rows + 8], 4, 0), 0.0))
        put(8 + rows, a, b, even)
        big = jnp.zeros((rows, lanes), F32)
        a = big if first is None else ref[first, 0:rows]
        b = big if second is None else ref[second, 0:rows]
        put(8, a, b, even_own)

    halo(S, 1, from_down, 0, 1)
    halo(S, 2, from_down, 2, 3)
    halo(K, 0, from_down, None, 4)
    halo(K, 1, from_down, 5, 6)
    halo(K, 2, from_down, 7, 8)
    halo(S, HP + own, from_up, 0, 1)
    halo(S, HP + own + 1, from_up, 2, 3)
    halo(K, HP + own, from_up, 4, 5)
    halo(K, HP + own + 1, from_up, 6, 7)
    halo(K, HP + own + 2, from_up, 8, None)
    relax_level(K, S, U, W, D, R, own, 4, 0, 8, True)
    store_field(U, field, own, even_own)
    zero = jnp.zeros((rows, lanes), F32)
    for colour in (0, 1):
        for at in (0, 1, own + 2, own + 3):
            R[colour, at] = zero
    half = rows // 2
    block = half + 8
    for q in range(own + 2):
        Z[block * q : block * (q + 1)] = product(
            row_restriction(rows, True), restrict_planes(R, q + 1, even_own))
    source = product(Z[...], lane_restriction(lanes))
    row = lax.broadcasted_iota(jnp.int32, (half, lanes // 2), 0)
    for q in range(own + 2):
        at = block * q
        rows_of = source[at : at + half]
        source_out[q] = rows_of
        to_low[q] = pick(row == half - 1, source[at + half : at + half + 1], rows_of)
        to_high[q] = pick(row == 0, source[at + half + 1 : at + half + 2], rows_of)


def mean_planes_kernel(own_rows, from_low, from_high, K, to_down, to_up):
    planes, rows, _ = own_rows.shape
    for q in range(planes):
        for out, at in ((K, q), (to_down, q), (to_up, q - planes + 6)):
            if 0 <= at < out.shape[0]:
                out[at, 0:rows] = from_low[q]
                out[at, rows : 2 * rows] = own_rows[q]
                out[at, 2 * rows : 3 * rows] = from_high[q]


def source_planes_kernel(own_rows, to_low, to_high, from_low, from_high, S, to_down, to_up):
    planes, rows, lanes = own_rows.shape
    row = lax.broadcasted_iota(jnp.int32, (rows, lanes), 0)
    first, last = row == 0, row == rows - 1
    for q in range(planes):
        got_low, got_high = from_low[q], from_high[q]
        low = pick(first, 0.0, got_low) + pick(last, to_low[q], 0.0)
        mine = own_rows[q] + pick(first, got_low, 0.0) + pick(last, got_high, 0.0)
        high = pick(last, 0.0, got_high) + pick(first, to_high[q], 0.0)
        for out, at in ((S, q), (to_down, q), (to_up, q - planes + 6)):
            if 0 <= at < out.shape[0]:
                out[at, 0:rows] = low
                out[at, rows : 2 * rows] = mine
                out[at, 2 * rows : 3 * rows] = high


def middle_kernel(s, k, from_down, from_up, k_down, k_up,
                  field, s_next, k_next, to_down, to_up,
                  K, S, U, W, D, R, Z, Zk):
    planes, wide, lanes = k.shape
    own = planes // 2
    even = even_mask(wide, lanes)
    zero = jnp.zeros((wide, lanes), F32)

    def source_plane(i):
        if i < -5 or i > planes + 4:
            return zero
        if i < -1:
            return from_down[i + 5]
        if i == -1:
            return from_down[4] + s[0]
        if i == 0:
            return s[1] + from_down[5]
        if i < planes - 1:
            return s[i + 1]
        if i == planes - 1:
            return s[planes] + from_up[0]
        if i == planes:
            return from_up[1] + s[planes + 1]
        return from_up[i - planes + 1]

    def mean_plane(i):
        if i < 0:
            return k_down[6 + i]
        if i < planes:
            return k[i]
        return k_up[i - planes]

    for p in range(-HP, own + HP):
        for to, plane in ((S, source_plane), (K, mean_plane)):
            a, b = plane(2 * p), plane(2 * p + 1)
            to[0, HP + p] = pick(even, a, b)
            to[1, HP + p] = pick(even, b, a)
    relax_level(K, S, U, W, D, R, own, 5, 1, 0, True)
    rows = field.shape[1]
    store_field(U, field, own, even_mask(rows, lanes))
    half = wide // 2
    for q in range(own):
        Z[half * q : half * (q + 1)] = product(
            row_restriction(wide, False), restrict_planes(R, q + 1, even))
    for q in range(own + 2):
        total = K[0, HP - 1 + q] + K[1, HP - 1 + q]
        Zk[half * q : half * (q + 1)] = product(row_sum(wide), total)
    source = product(Z[...], lane_restriction(lanes))
    mean = product(Zk[...], lane_mean(lanes))
    for q in range(own):
        value = source[half * q : half * (q + 1)]
        s_next[q] = value
        if q < 4:
            to_down[q] = value
        if q >= own - 4:
            to_up[q - own + 4] = value
    for q in range(own + 2):
        value = mean[half * q : half * (q + 1)]
        if 1 <= q <= own:
            k_next[q - 1] = value
        if 1 <= q <= 5:
            to_down[3 + q] = value
        if own - 4 <= q <= own:
            to_up[8 + q - own] = value


def coarse_kernel(s, k, from_down, from_up, field, rest, K, S, U, W, D, R):
    planes, wide, lanes = k.shape
    own = planes // 2
    rows = field.shape[1]
    even = even_mask(wide, lanes)
    even_own = even_mask(rows, lanes)
    zero = jnp.zeros((wide, lanes), F32)

    def source_plane(i):
        if i < -4 or i > planes + 3:
            return zero
        if i < 0:
            return from_down[4 + i]
        return s[i] if i < planes else from_up[i - planes]

    def mean_plane(i):
        if i < -5 or i > planes + 4:
            return zero
        if i < 0:
            return from_down[9 + i]
        return k[i] if i < planes else from_up[4 + i - planes]

    for p in range(-HP, own + HP):
        for to, plane in ((S, source_plane), (K, mean_plane)):
            a, b = plane(2 * p), plane(2 * p + 1)
            to[0, HP + p] = pick(even, a, b)
            to[1, HP + p] = pick(even, b, a)
    relax_level(K, S, U, W, D, R, own, 4, 0, (wide - rows) // 2, True)
    store_field(U, field, own, even_own)
    for p in range(own):
        red, black = R[0, p + 2], R[1, p + 2]
        rest[2 * p] = pick(even_own, red, black)
        rest[2 * p + 1] = pick(even_own, black, red)


def limit(scratch):
    words = 0
    for shape in scratch:
        size = 1
        for n in shape:
            size *= n
        words += size
    return 4 * words + (12 << 20)


def call(kernel, outs, scratch, *args, in_specs=None, name=None, results=()):
    extra = {}
    if in_specs is None:
        args = [pltpu.with_memory_space_constraint(a, pltpu.VMEM) for a in args]
    else:
        extra = {"in_specs": in_specs, "grid": (1,)}
        extra["out_specs"] = [pl.BlockSpec(memory_space=pltpu.VMEM) for _ in outs]
    return pl.pallas_call(
        kernel,
        out_shape=[jax.ShapeDtypeStruct(o, F32) if i in results else pltpu.VMEM(o, F32)
                   for i, o in enumerate(outs)],
        scratch_shapes=[pltpu.VMEM(shape, F32) for shape in scratch],
        compiler_params=pltpu.CompilerParams(vmem_limit_bytes=limit(scratch)),
        name=name,
        **extra,
    )(*args)


def level_scratch(own, wide, lanes, r_pairs, r_rows):
    pairs = own + 2 * HP
    block = (2, pairs, wide, lanes)
    return [block, block, block, (12, pairs, wide, lanes), block, (2, r_pairs, r_rows, lanes)]


def exchange(to_low, to_high, axis):
    size = lax.axis_size(axis)
    up = [(i, i + 1) for i in range(size - 1)]
    down = [(i + 1, i) for i in range(size - 1)]
    return lax.ppermute(to_high, axis, up), lax.ppermute(to_low, axis, down)


def body(right_side, coefficient):
    s, k = right_side, coefficient
    planes, rows, lanes = s.shape
    own = planes // 2
    wide = rows + 16

    low = pl.BlockSpec((planes, 8, lanes), lambda i: (0, 0, 0))
    high = pl.BlockSpec((planes, 8, lanes), lambda i: (0, rows // 8 - 1, 0))
    message = (2, own, 8, lanes)
    to_low, to_high = call(pack_rows_kernel, [message] * 2, [], s, s, k, k,
                           in_specs=[low, high, low, high], name="pack_rows")
    from_low, from_high = exchange(to_low, to_high, "inner")
    half, next_lanes = rows // 2, lanes // 2
    (mean,) = call(mean_kernel, [(own, half, next_lanes)], [(half * own, lanes)], k, name="mean")
    message = (9, rows + 8, lanes)
    to_down, to_up = call(pack_planes_kernel, [message] * 2, [], s, k, from_low, from_high,
                          name="pack_planes")
    mean, to_down, to_up = lax.optimization_barrier((mean, to_down, to_up))
    from_down, from_up = exchange(to_down, to_up, "outer")
    mean_low, mean_high = exchange(mean, mean, "inner")

    count = own + 2
    message = (count, half, next_lanes)
    field0, source, to_low, to_high = call(
        fine_kernel, [s.shape, message, message, message],
        level_scratch(own, wide, lanes, own + 4, rows) + [((half + 8) * count, lanes)],
        s, k, from_low, from_high, from_down, from_up, name="fine_level")

    planes, rows, lanes = own, half, next_lanes
    own, wide = planes // 2, 3 * rows
    mean_low, mean_high, to_low, to_high = lax.optimization_barrier((mean_low, mean_high, to_low, to_high))
    from_low, from_high = exchange(to_low, to_high, "inner")
    message = (6, wide, lanes)
    k1, to_down, to_up = call(
        mean_planes_kernel, [(planes, wide, lanes), message, message], [],
        mean, mean_low, mean_high, name="mean_planes")
    k_down, k_up = exchange(to_down, to_up, "outer")
    s1, to_down, to_up = call(
        source_planes_kernel, [(planes + 2, wide, lanes), message, message], [],
        source, to_low, to_high, from_low, from_high, name="source_planes")
    from_down, from_up = exchange(to_down, to_up, "outer")
    half, next_lanes = wide // 2, lanes // 2
    block, message = (own, half, next_lanes), (9, half, next_lanes)
    field1, s2, k2, to_down, to_up = call(
        middle_kernel, [(planes, rows, lanes), block, block, message, message],
        level_scratch(own, wide, lanes, own + 2, wide) + [(half * own, lanes), (half * (own + 2), lanes)],
        s1, k1, from_down, from_up, k_down, k_up, name="middle_level")

    planes, rows, wide, lanes = own, rows // 2, half, next_lanes
    own = planes // 2
    from_down, from_up = exchange(to_down, to_up, "outer")
    field2, rest = call(
        coarse_kernel, [(planes, rows, lanes)] * 2, level_scratch(own, wide, lanes, own + 4, rows),
        s2, k2, from_down, from_up, name="coarse_level")
    return field0, field1, field2, rest


def solution(mesh):
    spec = P("outer", "inner", None)
    return jax.shard_map(body, mesh=mesh, in_specs=(spec, spec), out_specs=(spec,) * 4, check_vma=False)
```

```python
import jax
import jax.numpy as jnp
from jax import lax
from jax.experimental import pallas as pl
from jax.experimental.pallas import tpu as pltpu
from jax.sharding import PartitionSpec as P

F32 = jnp.float32
HP = 3
HIGHEST = lax.Precision.HIGHEST


def tiled(tile, rows, lanes):
    wide = jnp.concatenate([tile] * (lanes // 128), axis=1)
    return jnp.concatenate([wide] * (rows // 8), axis=0)


def even_mask(rows, lanes):
    row = lax.broadcasted_iota(jnp.int32, (8, 128), 0)
    lane = lax.broadcasted_iota(jnp.int32, (8, 128), 1)
    return tiled((row + lane) & 1, rows, lanes) == 0


def pick(mask, a, b):
    return jnp.where(mask, a, b)


def odd_on(axis):
    return lax.axis_index(axis) % 2 == 1


def choose(odd, a, b):
    return lax.select(jnp.full(a.shape, odd), a, b)


class Got:
    def __init__(self, a, b, odd, upper):
        self.first, self.second = (a, b) if upper else (b, a)
        self.odd = odd
        self.shape = a.shape

    def __getitem__(self, at):
        return choose(self.odd, self.first[at], self.second[at])


def got_pair(a, b, axis):
    odd = odd_on(axis)
    return Got(a, b, odd, False), Got(a, b, odd, True)


class Send:
    def __init__(self, a, b, axis):
        self.a, self.b, self.odd = a, b, odd_on(axis)

    def put(self, at, low, high):
        self.a[at] = choose(self.odd, high, low)
        self.b[at] = choose(self.odd, low, high)


def row_index(lanes):
    return lax.broadcasted_iota(jnp.int32, (8, lanes), 0)


def lane_edge(value, at_start):
    lanes = value.shape[1]
    lane = lax.broadcasted_iota(jnp.int32, (value.shape[0], 128), 1)
    if at_start:
        edge = pick(lane == 0, 0.0, value[:, :128])
        return edge if lanes == 128 else jnp.concatenate([edge, value[:, 128:]], axis=1)
    edge = pick(lane == 127, 0.0, value[:, lanes - 128 :])
    return edge if lanes == 128 else jnp.concatenate([value[:, : lanes - 128], edge], axis=1)


def neighbours(ref, colour, p, pairs, even):
    other = 1 - colour
    x = ref[other, p]
    if isinstance(p, int):
        below, above = ref[other, max(p - 1, 0)], ref[other, min(p + 1, pairs - 1)]
    else:
        below = ref[other, jnp.maximum(p - 1, 0)]
        above = ref[other, jnp.minimum(p + 1, pairs - 1)]
    far = pick(even, below, above) if colour == 0 else pick(even, above, below)
    rows, lanes = x.shape
    return (
        x,
        far,
        pltpu.roll(x, 1, 0),
        pltpu.roll(x, rows - 1, 0),
        pltpu.roll(x, 1, 1),
        pltpu.roll(x, lanes - 1, 1),
    )


def span(own, layers):
    extra = (layers + 1) // 2
    return HP - extra, HP + own + extra


def over(first, last, step, unrolled):
    if unrolled:
        for p in range(first, last):
            step(p, 0)
    else:
        lax.fori_loop(first, last, step, 0)


def relax_level(K, S, U, W, D, R, own, depth, residual_layers, inset, unrolled):
    _, pairs, rows, lanes = K.shape
    even = even_mask(rows, lanes)

    def setup(colour, layers):
        first, last = span(own, layers)

        def step(p, carry):
            near = list(neighbours(K, colour, p, pairs, even))
            near[4] = lane_edge(near[4], True)
            near[5] = lane_edge(near[5], False)
            centre = K[colour, p]
            total = near[0]
            for value in near[1:]:
                total = total + value
            diag = 3.0 * centre + 0.5 * total
            inverse = pick(centre > 0.0, 1.0 / diag, 0.0)
            half = 0.5 * inverse
            for i, value in enumerate(near):
                weight = (centre + value) * half
                if i == 4:
                    weight = lane_edge(weight, True)
                if i == 5:
                    weight = lane_edge(weight, False)
                W[colour * 6 + i, p] = weight
            D[colour, p] = diag
            start = S[colour, p] * inverse
            S[colour, p] = start
            if colour == 0:
                U[0, p] = start
            return carry

        over(first, last, step, unrolled)
        zero = jnp.zeros((rows, lanes), F32)
        for p in list(range(first)) + list(range(last, pairs)):
            U[colour, p] = zero

    def relaxed(colour, p):
        near = neighbours(U, colour, p, pairs, even)
        total = S[colour, p]
        for i, value in enumerate(near):
            total = total + W[colour * 6 + i, p] * value
        return total

    def half_sweep(colour, layers):
        first, last = span(own, layers)

        def step(p, carry):
            U[colour, p] = relaxed(colour, p)
            return carry

        over(first, last, step, unrolled)

    setup(0, depth)
    setup(1, depth - 1)
    half_sweep(1, depth - 1)
    half_sweep(0, depth - 2)
    half_sweep(1, depth - 3)
    first, last = span(own, residual_layers)

    def left(p, carry):
        for colour in (0, 1):
            rest = D[colour, p] * (relaxed(colour, p) - U[colour, p])
            R[colour, p - first + R_PAD[residual_layers]] = rest[inset : rows - inset]
        return carry

    over(first, last, left, unrolled)


R_PAD = {0: 2, 1: 0}


def store_field(U, out, own, even):
    rows = out.shape[1]
    first = (U.shape[2] - rows) // 2
    for p in range(own):
        red = U[0, HP + p, first : first + rows]
        black = U[1, HP + p, first : first + rows]
        out[2 * p] = pick(even, red, black)
        out[2 * p + 1] = pick(even, black, red)


def restrict_planes(R, at, even):
    red, black = R[0, at], R[1, at]
    odd_below = pick(even, R[1, at - 1], R[0, at - 1])
    even_above = pick(even, R[0, at + 1], R[1, at + 1])
    return (3.0 * (red + black) + (odd_below + even_above)) * 0.125


def row_restriction(rows, ends):
    half = rows // 2
    shape = (half + 8 if ends else half, rows)
    j = lax.broadcasted_iota(jnp.int32, shape, 0)
    m = lax.broadcasted_iota(jnp.int32, shape, 1)
    inner = (m == 2 * j) | (m == 2 * j + 1)
    outer = (m == 2 * j - 1) | (m == 2 * j + 2)
    main = pick(inner, 0.375, pick(outer, 0.125, 0.0)).astype(F32)
    if not ends:
        return main
    edge = pick(((j == half) & (m == 0)) | ((j == half + 1) & (m == rows - 1)), 0.125, 0.0)
    return pick(j < half, main, edge).astype(F32)


def row_sum(rows):
    j = 2 * lax.broadcasted_iota(jnp.int32, (rows // 2, rows), 0)
    m = lax.broadcasted_iota(jnp.int32, (rows // 2, rows), 1)
    return pick((m == j) | (m == j + 1), 1.0, 0.0).astype(F32)


def product(a, b):
    return jnp.dot(a, b, precision=HIGHEST, preferred_element_type=F32)


def lane_restriction(lanes):
    m = lax.broadcasted_iota(jnp.int32, (lanes, lanes // 2), 0)
    i = 2 * lax.broadcasted_iota(jnp.int32, (lanes, lanes // 2), 1)
    inner = (m == i) | (m == i + 1)
    outer = (m == i - 1) | (m == i + 2)
    return pick(inner, 1.5, pick(outer, 0.5, 0.0)).astype(F32)


def lane_mean(lanes):
    m = lax.broadcasted_iota(jnp.int32, (lanes, lanes // 2), 0)
    i = 2 * lax.broadcasted_iota(jnp.int32, (lanes, lanes // 2), 1)
    return pick((m == i) | (m == i + 1), 0.125, 0.0).astype(F32)


def pack_rows_kernel(s_low, s_high, k_low, k_high, to_a, to_b):
    lanes = s_low.shape[2]
    even = even_mask(8, lanes)
    send = Send(to_a, to_b, "inner")
    cat = lambda *parts: jnp.concatenate(parts, axis=0)

    def step(p, carry):
        def pair(ref):
            a, b = ref[2 * p], ref[2 * p + 1]
            return pick(even, a, b), pick(even, b, a)

        ls, lk, hs, hk = pair(s_low), pair(k_low), pair(s_high), pair(k_high)
        send.put((0, p), cat(lk[0][0:4], ls[0][0:4]), cat(hk[0][4:8], hs[0][4:8]))
        send.put((1, p), cat(lk[1][0:5], ls[1][0:3]), cat(hk[1][3:8], hs[1][5:8]))
        return carry

    lax.fori_loop(0, s_low.shape[0] // 2, step, 0, unroll=True)


def pack_planes_kernel(s, k, from_a, from_b, to_a, to_b):
    planes, rows, lanes = s.shape
    even = even_mask(8, lanes)
    from_low, from_high = got_pair(from_a, from_b, "inner")
    send = Send(to_a, to_b, "outer")

    def edges(p, of_k):
        lr, lb = from_low[0, p], from_low[1, p]
        hr, hb = from_high[0, p], from_high[1, p]
        if of_k:
            red = jnp.concatenate([lr[0:4], hr[0:4]], axis=0)
            black = jnp.concatenate([lb[1:5], hb[0:4]], axis=0)
        else:
            red = jnp.concatenate([lr[4:8], hr[4:8]], axis=0)
            black = jnp.concatenate([lb[4:8], hb[5:8], hb[7:8]], axis=0)
        return pick(even, red, black), pick(even, black, red)

    def put(at, ref, down, up, of_k):
        send.put((at, slice(0, rows)), ref[down], ref[up])
        send.put((at, slice(rows, rows + 8)),
                 edges(down // 2, of_k)[down % 2], edges(up // 2, of_k)[up % 2])

    for j in range(4):
        put(j, s, j, planes - 4 + j, False)
    for j in range(5):
        put(4 + j, k, j, planes - 5 + j, True)


def mean_kernel(k, out, Z):
    planes, rows, lanes = k.shape
    half = rows // 2
    for q in range(planes // 2):
        Z[half * q : half * (q + 1)] = product(row_sum(rows), k[2 * q] + k[2 * q + 1])
    mean = product(Z[...], lane_mean(lanes))
    for q in range(planes // 2):
        out[q] = mean[half * q : half * (q + 1)]


def fine_kernel(s, k, row_a, row_b, plane_a, plane_b,
                field, source_out, to_a, to_b,
                K, S, U, W, D, R, Z):
    from_low, from_high = got_pair(row_a, row_b, "inner")
    from_down, from_up = got_pair(plane_a, plane_b, "outer")
    send = Send(to_a, to_b, "inner")
    planes, rows, lanes = s.shape
    own = planes // 2
    wide = rows + 16
    even = even_mask(8, lanes)
    even_own = even_mask(rows, lanes)
    row = row_index(lanes)
    zero8 = jnp.zeros((8, lanes), F32)
    zero = jnp.zeros((wide, lanes), F32)

    def fill(p, carry):
        at = HP + p
        lr, lb = from_low[0, p], from_low[1, p]
        hr, hb = from_high[0, p], from_high[1, p]
        K[0, at, 0:8] = pick(row >= 4, pltpu.roll(lr, 4, 0), 0.0)
        K[1, at, 0:8] = pick(row >= 3, pltpu.roll(lb, 3, 0), 0.0)
        S[0, at, 0:8] = pick(row >= 4, lr, 0.0)
        S[1, at, 0:8] = pick(row >= 5, lb, 0.0)
        K[0, at, 8 + rows : wide] = pick(row < 4, hr, 0.0)
        K[1, at, 8 + rows : wide] = pick(row < 5, hb, 0.0)
        S[0, at, 8 + rows : wide] = pick(row < 4, pltpu.roll(hr, 4, 0), 0.0)
        S[1, at, 8 + rows : wide] = pick(row < 3, pltpu.roll(hb, 3, 0), 0.0)
        for ref, to in ((s, S), (k, K)):
            a, b = ref[2 * p], ref[2 * p + 1]
            to[0, at, 8 : 8 + rows] = pick(even_own, a, b)
            to[1, at, 8 : 8 + rows] = pick(even_own, b, a)
        return carry

    lax.fori_loop(0, own, fill, 0)

    def halo(to, at, ref, first, second):
        def part(rows_of):
            a = zero8 if first is None else rows_of(first)
            b = zero8 if second is None else rows_of(second)
            return a, b

        def put(start, a, b, mask):
            to[0, at, start : start + a.shape[0]] = pick(mask, a, b)
            to[1, at, start : start + a.shape[0]] = pick(mask, b, a)

        a, b = part(lambda j: pick(row >= 4, pltpu.roll(ref[j, rows : rows + 8], 4, 0), 0.0))
        put(0, a, b, even)
        a, b = part(lambda j: pick(row < 4, pltpu.roll(ref[j, rows : rows + 8], 4, 0), 0.0))
        put(8 + rows, a, b, even)
        big = jnp.zeros((rows, lanes), F32)
        a = big if first is None else ref[first, 0:rows]
        b = big if second is None else ref[second, 0:rows]
        put(8, a, b, even_own)

    halo(S, 1, from_down, 0, 1)
    halo(S, 2, from_down, 2, 3)
    halo(K, 0, from_down, None, 4)
    halo(K, 1, from_down, 5, 6)
    halo(K, 2, from_down, 7, 8)
    halo(S, HP + own, from_up, 0, 1)
    halo(S, HP + own + 1, from_up, 2, 3)
    halo(K, HP + own, from_up, 4, 5)
    halo(K, HP + own + 1, from_up, 6, 7)
    halo(K, HP + own + 2, from_up, 8, None)
    relax_level(K, S, U, W, D, R, own, 4, 0, 8, True)
    store_field(U, field, own, even_own)
    zero = jnp.zeros((rows, lanes), F32)
    for colour in (0, 1):
        for at in (0, 1, own + 2, own + 3):
            R[colour, at] = zero
    half = rows // 2
    block = half + 8
    for q in range(own + 2):
        Z[block * q : block * (q + 1)] = product(
            row_restriction(rows, True), restrict_planes(R, q + 1, even_own))
    source = product(Z[...], lane_restriction(lanes))
    row = lax.broadcasted_iota(jnp.int32, (half, lanes // 2), 0)
    for q in range(own + 2):
        at = block * q
        rows_of = source[at : at + half]
        source_out[q] = rows_of
        send.put(q, pick(row == half - 1, source[at + half : at + half + 1], rows_of),
                 pick(row == 0, source[at + half + 1 : at + half + 2], rows_of))


def widen_planes(K, send, planes, of):
    for q in range(planes):
        K[q] = of(q)
    for j in range(6):
        send.put(j, K[j], K[planes - 6 + j])


def mean_planes_kernel(own_rows, from_a, from_b, K, to_a, to_b):
    from_low, from_high = got_pair(from_a, from_b, "inner")

    def of(q):
        return jnp.concatenate([from_low[q], own_rows[q], from_high[q]], axis=0)

    widen_planes(K, Send(to_a, to_b, "outer"), own_rows.shape[0], of)


def source_planes_kernel(own_rows, sent_a, sent_b, from_a, from_b, S, to_a, to_b):
    planes, rows, lanes = own_rows.shape
    row = lax.broadcasted_iota(jnp.int32, (rows, lanes), 0)
    first, last = row == 0, row == rows - 1
    to_low, to_high = got_pair(sent_a, sent_b, "inner")
    from_low, from_high = got_pair(from_a, from_b, "inner")

    def of(q):
        got_low, got_high = from_low[q], from_high[q]
        low = pick(first, 0.0, got_low) + pick(last, to_low[q], 0.0)
        mine = own_rows[q] + pick(first, got_low, 0.0) + pick(last, got_high, 0.0)
        high = pick(last, 0.0, got_high) + pick(first, to_high[q], 0.0)
        return jnp.concatenate([low, mine, high], axis=0)

    widen_planes(S, Send(to_a, to_b, "outer"), planes, of)


def middle_kernel(s, k, source_a, source_b, mean_a, mean_b,
                  field, s_next, k_next, to_a, to_b,
                  K, S, U, W, D, R, Z, Zk):
    from_down, from_up = got_pair(source_a, source_b, "outer")
    k_down, k_up = got_pair(mean_a, mean_b, "outer")
    send = Send(to_a, to_b, "outer")
    planes, wide, lanes = k.shape
    own = planes // 2
    even = even_mask(wide, lanes)
    zero = jnp.zeros((wide, lanes), F32)

    def source_plane(i):
        if i < -5 or i > planes + 4:
            return zero
        if i < -1:
            return from_down[i + 5]
        if i == -1:
            return from_down[4] + s[0]
        if i == 0:
            return s[1] + from_down[5]
        if i < planes - 1:
            return s[i + 1]
        if i == planes - 1:
            return s[planes] + from_up[0]
        if i == planes:
            return from_up[1] + s[planes + 1]
        return from_up[i - planes + 1]

    def mean_plane(i):
        if i < 0:
            return k_down[6 + i]
        if i < planes:
            return k[i]
        return k_up[i - planes]

    for p in range(-HP, own + HP):
        for to, plane in ((S, source_plane), (K, mean_plane)):
            a, b = plane(2 * p), plane(2 * p + 1)
            to[0, HP + p] = pick(even, a, b)
            to[1, HP + p] = pick(even, b, a)
    relax_level(K, S, U, W, D, R, own, 5, 1, 0, True)
    rows = field.shape[1]
    store_field(U, field, own, even_mask(rows, lanes))
    half = wide // 2
    for q in range(own):
        Z[half * q : half * (q + 1)] = product(
            row_restriction(wide, False), restrict_planes(R, q + 1, even))
    for q in range(own + 2):
        total = K[0, HP - 1 + q] + K[1, HP - 1 + q]
        Zk[half * q : half * (q + 1)] = product(row_sum(wide), total)
    source = product(Z[...], lane_restriction(lanes))
    mean = product(Zk[...], lane_mean(lanes))
    for q in range(own):
        s_next[q] = source[half * q : half * (q + 1)]
        k_next[q] = mean[half * (q + 1) : half * (q + 2)]
    for j in range(4):
        send.put(j, s_next[j], s_next[own - 4 + j])
    for j in range(5):
        send.put(4 + j, mean[half * (1 + j) : half * (2 + j)],
                 mean[half * (own - 4 + j) : half * (own - 3 + j)])


def coarse_kernel(s, k, from_a, from_b, field, rest, K, S, U, W, D, R):
    from_down, from_up = got_pair(from_a, from_b, "outer")
    planes, wide, lanes = k.shape
    own = planes // 2
    rows = field.shape[1]
    even = even_mask(wide, lanes)
    even_own = even_mask(rows, lanes)
    zero = jnp.zeros((wide, lanes), F32)

    def source_plane(i):
        if i < -4 or i > planes + 3:
            return zero
        if i < 0:
            return from_down[4 + i]
        return s[i] if i < planes else from_up[i - planes]

    def mean_plane(i):
        if i < -5 or i > planes + 4:
            return zero
        if i < 0:
            return from_down[9 + i]
        return k[i] if i < planes else from_up[4 + i - planes]

    for p in range(-HP, own + HP):
        for to, plane in ((S, source_plane), (K, mean_plane)):
            a, b = plane(2 * p), plane(2 * p + 1)
            to[0, HP + p] = pick(even, a, b)
            to[1, HP + p] = pick(even, b, a)
    relax_level(K, S, U, W, D, R, own, 4, 0, (wide - rows) // 2, True)
    store_field(U, field, own, even_own)
    for p in range(own):
        red, black = R[0, p + 2], R[1, p + 2]
        rest[2 * p] = pick(even_own, red, black)
        rest[2 * p + 1] = pick(even_own, black, red)


def limit(scratch):
    words = 0
    for shape in scratch:
        size = 1
        for n in shape:
            size *= n
        words += size
    return 4 * words + (12 << 20)


def call(kernel, outs, scratch, *args, in_specs=None, name=None, results=False):
    extra = {}
    if in_specs is None:
        args = [pltpu.with_memory_space_constraint(a, pltpu.VMEM) for a in args]
    else:
        args = [pltpu.with_memory_space_constraint(a, pltpu.HBM) for a in args]
        extra = {"in_specs": in_specs, "grid": (1,)}
        extra["out_specs"] = [pl.BlockSpec(memory_space=pltpu.VMEM) for _ in outs]
    if results:
        extra = {"out_specs": [pl.BlockSpec(memory_space=pltpu.VMEM) for _ in outs]}
    return pl.pallas_call(
        kernel,
        out_shape=[jax.ShapeDtypeStruct(o, F32) if results else pltpu.VMEM(o, F32) for o in outs],
        scratch_shapes=[pltpu.VMEM(shape, F32) for shape in scratch],
        compiler_params=pltpu.CompilerParams(vmem_limit_bytes=limit(scratch)),
        name=name,
        **extra,
    )(*args)


def level_scratch(own, wide, lanes, r_pairs, r_rows):
    pairs = own + 2 * HP
    block = (2, pairs, wide, lanes)
    return [block, block, block, (12, pairs, wide, lanes), block, (2, r_pairs, r_rows, lanes)]


def exchange(a, b, axis):
    size = lax.axis_size(axis)

    def swapped(x, first):
        pairs = [(i, i + 1) for i in range(first, size - 1, 2)]
        return lax.ppermute(x, axis, pairs + [(j, i) for i, j in pairs])

    return swapped(a, 1), swapped(b, 0)


def body(right_side, coefficient):
    s, k = right_side, coefficient
    planes, rows, lanes = s.shape
    own = planes // 2
    wide = rows + 16

    low = pl.BlockSpec((planes, 8, lanes), lambda i: (0, 0, 0))
    high = pl.BlockSpec((planes, 8, lanes), lambda i: (0, rows // 8 - 1, 0))
    message = (2, own, 8, lanes)
    sent = call(pack_rows_kernel, [message] * 2, [], s, s, k, k,
                in_specs=[low, high, low, high], name="pack_rows")
    row_halo = exchange(*sent, "inner")
    half, next_lanes = rows // 2, lanes // 2
    (mean,) = call(mean_kernel, [(own, half, next_lanes)], [(half * own, lanes)], k, name="mean")
    message = (9, rows + 8, lanes)
    to_a, to_b = call(pack_planes_kernel, [message] * 2, [], s, k, *row_halo, name="pack_planes")
    mean, to_a, to_b = lax.optimization_barrier((mean, to_a, to_b))
    plane_halo = exchange(to_a, to_b, "outer")
    mean_halo = exchange(mean, mean, "inner")

    count = own + 2
    message = (count, half, next_lanes)
    field0, source, to_a, to_b = call(
        fine_kernel, [s.shape, message, message, message],
        level_scratch(own, wide, lanes, own + 4, rows) + [((half + 8) * count, lanes)],
        s, k, *row_halo, *plane_halo, name="fine_level")

    planes, rows, lanes = own, half, next_lanes
    own, wide = planes // 2, 3 * rows
    *mean_halo, to_a, to_b = lax.optimization_barrier((*mean_halo, to_a, to_b))
    row_halo = exchange(to_a, to_b, "inner")
    message = (6, wide, lanes)
    k1, *sent = call(
        mean_planes_kernel, [(planes, wide, lanes), message, message], [],
        mean, *mean_halo, name="mean_planes")
    mean_halo = exchange(*sent, "outer")
    s1, *sent = call(
        source_planes_kernel, [(planes + 2, wide, lanes), message, message], [],
        source, to_a, to_b, *row_halo, name="source_planes")
    source_halo = exchange(*sent, "outer")
    half, next_lanes = wide // 2, lanes // 2
    block, message = (own, half, next_lanes), (9, half, next_lanes)
    field1, s2, k2, *sent = call(
        middle_kernel, [(planes, rows, lanes), block, block, message, message],
        level_scratch(own, wide, lanes, own + 2, wide) + [(half * own, lanes), (half * (own + 2), lanes)],
        s1, k1, *source_halo, *mean_halo, name="middle_level")

    planes, rows, wide, lanes = own, rows // 2, half, next_lanes
    own = planes // 2
    field2, rest = call(
        coarse_kernel, [(planes, rows, lanes)] * 2, level_scratch(own, wide, lanes, own + 4, rows),
        s2, k2, *exchange(*sent, "outer"), name="coarse_level", results=True)
    return field0, field1, field2, rest


def solution(mesh):
    spec = P("outer", "inner", None)
    return jax.shard_map(body, mesh=mesh, in_specs=(spec, spec), out_specs=(spec,) * 4, check_vma=False)
```

```python
import jax
import jax.numpy as jnp
from jax import lax
from jax.experimental import pallas as pl
from jax.experimental.pallas import tpu as pltpu
from jax.sharding import PartitionSpec as P

F32 = jnp.float32
HP = 3
HIGHEST = lax.Precision.HIGHEST


def tiled(tile, rows, lanes):
    wide = jnp.concatenate([tile] * (lanes // 128), axis=1)
    return jnp.concatenate([wide] * (rows // 8), axis=0)


def even_mask(rows, lanes):
    row = lax.broadcasted_iota(jnp.int32, (8, 128), 0)
    lane = lax.broadcasted_iota(jnp.int32, (8, 128), 1)
    return tiled((row + lane) & 1, rows, lanes) == 0


def pick(mask, a, b):
    return jnp.where(mask, a, b)


def odd_on(axis):
    return lax.axis_index(axis) % 2 == 1


def choose(odd, a, b):
    return lax.select(jnp.full(a.shape, odd), a, b)


class Got:
    def __init__(self, a, b, odd, upper):
        self.first, self.second = (a, b) if upper else (b, a)
        self.odd = odd
        self.shape = a.shape

    def __getitem__(self, at):
        return choose(self.odd, self.first[at], self.second[at])


def got_pair(a, b, axis):
    odd = odd_on(axis)
    return Got(a, b, odd, False), Got(a, b, odd, True)


class Send:
    def __init__(self, a, b, axis):
        self.a, self.b, self.odd = a, b, odd_on(axis)

    def put(self, at, low, high):
        self.a[at] = choose(self.odd, high, low)
        self.b[at] = choose(self.odd, low, high)


def row_index(lanes):
    return lax.broadcasted_iota(jnp.int32, (8, lanes), 0)


def lane_edge(value, at_start):
    lanes = value.shape[1]
    lane = lax.broadcasted_iota(jnp.int32, (value.shape[0], 128), 1)
    if at_start:
        edge = pick(lane == 0, 0.0, value[:, :128])
        return edge if lanes == 128 else jnp.concatenate([edge, value[:, 128:]], axis=1)
    edge = pick(lane == 127, 0.0, value[:, lanes - 128 :])
    return edge if lanes == 128 else jnp.concatenate([value[:, : lanes - 128], edge], axis=1)


def neighbours(ref, colour, p, pairs, even):
    other = 1 - colour
    x = ref[other, p]
    if isinstance(p, int):
        below, above = ref[other, max(p - 1, 0)], ref[other, min(p + 1, pairs - 1)]
    else:
        below = ref[other, jnp.maximum(p - 1, 0)]
        above = ref[other, jnp.minimum(p + 1, pairs - 1)]
    far = pick(even, below, above) if colour == 0 else pick(even, above, below)
    rows, lanes = x.shape
    return (
        x,
        far,
        pltpu.roll(x, 1, 0),
        pltpu.roll(x, rows - 1, 0),
        pltpu.roll(x, 1, 1),
        pltpu.roll(x, lanes - 1, 1),
    )


def span(own, layers):
    extra = (layers + 1) // 2
    return range(HP - extra, HP + own + extra)


class Store:
    def __init__(self, ref, start=0, early=None, held=()):
        self.ref, self.start = ref, start
        self.early = {key: early for key in held}

    def place(self, at):
        first, p, *rest = at
        early = self.early.get((first, p))
        if early is not None:
            return early.ref, (first, p - early.start, *rest)
        return self.ref, (first, p - self.start, *rest)

    def __getitem__(self, at):
        ref, at = self.place(at)
        return ref[at]

    def __setitem__(self, at, value):
        self.early.pop((at[0], at[1]), None)
        ref, at = self.place(at)
        ref[at] = value


class Level:
    def __init__(self, K, S, U, W, D, own, shape):
        self.K, self.S, self.U, self.W, self.D, self.own = K, S, U, W, D, own
        self.pairs = own + 2 * HP
        self.rows, self.lanes = shape
        self.even = even_mask(self.rows, self.lanes)

    def setup(self, colour, pairs, inverse_out=None):
        for p in pairs:
            near = list(neighbours(self.K, colour, p, self.pairs, self.even))
            near[4] = lane_edge(near[4], True)
            near[5] = lane_edge(near[5], False)
            centre = self.K[colour, p]
            total = near[0]
            for value in near[1:]:
                total = total + value
            diag = 3.0 * centre + 0.5 * total
            inverse = pick(centre > 0.0, 1.0 / diag, 0.0)
            half = 0.5 * inverse
            for i, value in enumerate(near):
                weight = (centre + value) * half
                if i == 4:
                    weight = lane_edge(weight, True)
                if i == 5:
                    weight = lane_edge(weight, False)
                self.W[colour * 6 + i, p] = weight
            self.D[colour, p] = diag
            if inverse_out is not None:
                inverse_out[colour, p] = inverse
            else:
                self.begin(colour, p, inverse)

    def begin(self, colour, p, inverse):
        start = self.S[colour, p] * inverse
        self.S[colour, p] = start
        if colour == 0:
            self.U[0, p] = start

    def clear(self, colour, pairs):
        zero = jnp.zeros((self.rows, self.lanes), F32)
        for p in range(self.pairs):
            if p not in pairs:
                self.U[colour, p] = zero

    def relaxed(self, colour, p):
        near = neighbours(self.U, colour, p, self.pairs, self.even)
        total = self.S[colour, p]
        for i, value in enumerate(near):
            total = total + self.W[colour * 6 + i, p] * value
        return total

    def sweep(self, colour, pairs):
        for p in pairs:
            self.U[colour, p] = self.relaxed(colour, p)

    def residual(self, R, pairs, pad, inset):
        for i, p in enumerate(pairs):
            for colour in (0, 1):
                rest = self.D[colour, p] * (self.relaxed(colour, p) - self.U[colour, p])
                R[colour, i + pad] = rest[inset : self.rows - inset]

    def all_setup(self, depth, inverse_out=None):
        for colour in (0, 1):
            self.setup(colour, span(self.own, depth - colour), inverse_out)

    def all_clear(self, depth):
        for colour in (0, 1):
            self.clear(colour, span(self.own, depth - colour))

    def all_sweeps(self, depth):
        for i, colour in enumerate((1, 0, 1)):
            self.sweep(colour, span(self.own, depth - 1 - i))


def without(pairs, inner):
    return [p for p in pairs if p not in inner]


def inner_span(own, margin):
    return range(HP + margin, HP + own - margin)


def store_field(U, out, own, even, wide):
    rows = out.shape[1]
    first = (wide - rows) // 2
    for p in range(own):
        red = U[0, HP + p, first : first + rows]
        black = U[1, HP + p, first : first + rows]
        out[2 * p] = pick(even, red, black)
        out[2 * p + 1] = pick(even, black, red)


def restrict_planes(R, at, even):
    red, black = R[0, at], R[1, at]
    odd_below = pick(even, R[1, at - 1], R[0, at - 1])
    even_above = pick(even, R[0, at + 1], R[1, at + 1])
    return (3.0 * (red + black) + (odd_below + even_above)) * 0.125


def row_restriction(rows, ends):
    half = rows // 2
    shape = (half + 8 if ends else half, rows)
    j = lax.broadcasted_iota(jnp.int32, shape, 0)
    m = lax.broadcasted_iota(jnp.int32, shape, 1)
    inner = (m == 2 * j) | (m == 2 * j + 1)
    outer = (m == 2 * j - 1) | (m == 2 * j + 2)
    main = pick(inner, 0.375, pick(outer, 0.125, 0.0)).astype(F32)
    if not ends:
        return main
    edge = pick(((j == half) & (m == 0)) | ((j == half + 1) & (m == rows - 1)), 0.125, 0.0)
    return pick(j < half, main, edge).astype(F32)


def row_sum(rows):
    j = 2 * lax.broadcasted_iota(jnp.int32, (rows // 2, rows), 0)
    m = lax.broadcasted_iota(jnp.int32, (rows // 2, rows), 1)
    return pick((m == j) | (m == j + 1), 1.0, 0.0).astype(F32)


def product(a, b):
    return jnp.dot(a, b, precision=HIGHEST, preferred_element_type=F32)


def lane_restriction(lanes):
    m = lax.broadcasted_iota(jnp.int32, (lanes, lanes // 2), 0)
    i = 2 * lax.broadcasted_iota(jnp.int32, (lanes, lanes // 2), 1)
    inner = (m == i) | (m == i + 1)
    outer = (m == i - 1) | (m == i + 2)
    return pick(inner, 1.5, pick(outer, 0.5, 0.0)).astype(F32)


def lane_mean(lanes):
    m = lax.broadcasted_iota(jnp.int32, (lanes, lanes // 2), 0)
    i = 2 * lax.broadcasted_iota(jnp.int32, (lanes, lanes // 2), 1)
    return pick((m == i) | (m == i + 1), 0.125, 0.0).astype(F32)


def pack_rows_kernel(s_low, s_high, k_low, k_high, to_a, to_b):
    lanes = s_low.shape[2]
    even = even_mask(8, lanes)
    send = Send(to_a, to_b, "inner")
    cat = lambda *parts: jnp.concatenate(parts, axis=0)

    def step(p, carry):
        def pair(ref):
            a, b = ref[2 * p], ref[2 * p + 1]
            return pick(even, a, b), pick(even, b, a)

        ls, lk, hs, hk = pair(s_low), pair(k_low), pair(s_high), pair(k_high)
        send.put((0, p), cat(lk[0][0:4], ls[0][0:4]), cat(hk[0][4:8], hs[0][4:8]))
        send.put((1, p), cat(lk[1][0:5], ls[1][0:3]), cat(hk[1][3:8], hs[1][5:8]))
        return carry

    lax.fori_loop(0, s_low.shape[0] // 2, step, 0, unroll=True)


def pack_planes_kernel(s, k, from_a, from_b, to_a, to_b):
    planes, rows, lanes = s.shape
    even = even_mask(8, lanes)
    from_low, from_high = got_pair(from_a, from_b, "inner")
    send = Send(to_a, to_b, "outer")

    def edges(p, of_k):
        lr, lb = from_low[0, p], from_low[1, p]
        hr, hb = from_high[0, p], from_high[1, p]
        if of_k:
            red = jnp.concatenate([lr[0:4], hr[0:4]], axis=0)
            black = jnp.concatenate([lb[1:5], hb[0:4]], axis=0)
        else:
            red = jnp.concatenate([lr[4:8], hr[4:8]], axis=0)
            black = jnp.concatenate([lb[4:8], hb[5:8], hb[7:8]], axis=0)
        return pick(even, red, black), pick(even, black, red)

    def put(at, ref, down, up, of_k):
        send.put((at, slice(0, rows)), ref[down], ref[up])
        send.put((at, slice(rows, rows + 8)),
                 edges(down // 2, of_k)[down % 2], edges(up // 2, of_k)[up % 2])

    for j in range(4):
        put(j, s, j, planes - 4 + j, False)
    for j in range(5):
        put(4 + j, k, j, planes - 5 + j, True)


def mean_kernel(k, out, Z):
    planes, rows, lanes = k.shape
    half = rows // 2
    for q in range(planes // 2):
        Z[half * q : half * (q + 1)] = product(row_sum(rows), k[2 * q] + k[2 * q + 1])
    mean = product(Z[...], lane_mean(lanes))
    for q in range(planes // 2):
        out[q] = mean[half * q : half * (q + 1)]


def fine_prepare_kernel(s, k, row_a, row_b, *arrays):
    planes, rows, lanes = s.shape
    own = planes // 2
    wide = rows + 16
    from_low, from_high = got_pair(row_a, row_b, "inner")
    even_own = even_mask(rows, lanes)
    row = row_index(lanes)
    K, S, U, W, D = [Store(ref, HP) for ref in arrays]

    def fill(p):
        at = HP + p
        lr, lb = from_low[0, p], from_low[1, p]
        hr, hb = from_high[0, p], from_high[1, p]
        K[0, at, 0:8] = pick(row >= 4, pltpu.roll(lr, 4, 0), 0.0)
        K[1, at, 0:8] = pick(row >= 3, pltpu.roll(lb, 3, 0), 0.0)
        S[0, at, 0:8] = pick(row >= 4, lr, 0.0)
        S[1, at, 0:8] = pick(row >= 5, lb, 0.0)
        K[0, at, 8 + rows : wide] = pick(row < 4, hr, 0.0)
        K[1, at, 8 + rows : wide] = pick(row < 5, hb, 0.0)
        S[0, at, 8 + rows : wide] = pick(row < 4, pltpu.roll(hr, 4, 0), 0.0)
        S[1, at, 8 + rows : wide] = pick(row < 3, pltpu.roll(hb, 3, 0), 0.0)
        for ref, to in ((s, S), (k, K)):
            a, b = ref[2 * p], ref[2 * p + 1]
            to[0, at, 8 : 8 + rows] = pick(even_own, a, b)
            to[1, at, 8 : 8 + rows] = pick(even_own, b, a)

    for p in range(own):
        fill(p)
    level = Level(K, S, U, W, D, own, (wide, lanes))
    level.setup(0, inner_span(own, 1))
    level.setup(1, inner_span(own, 1))
    level.sweep(1, inner_span(own, 2))
    level.sweep(0, inner_span(own, 3))


def fine_kernel(plane_a, plane_b, K0, S0, U0, W0, D0,
                field, source_out, to_a, to_b, K1, S1, U1, W1, D1, R, Z):
    from_down, from_up = got_pair(plane_a, plane_b, "outer")
    send = Send(to_a, to_b, "inner")
    planes, rows, lanes = field.shape
    own = planes // 2
    wide = rows + 16
    even = even_mask(8, lanes)
    even_own = even_mask(rows, lanes)
    row = row_index(lanes)
    zero8 = jnp.zeros((8, lanes), F32)

    def store(ref, early, firsts, pairs):
        return Store(ref, 0, Store(early, HP), [(i, p) for i in firsts for p in pairs])

    inside = inner_span(own, 1)
    K = store(K1, K0, (0, 1), inner_span(own, 0))
    S = store(S1, S0, (0, 1), inner_span(own, 0))
    W = store(W1, W0, range(12), inside)
    D = store(D1, D0, (0, 1), inside)
    U = store(U1, U0, (0,), inside)
    U.early.update({(1, p): Store(U0, HP) for p in inner_span(own, 2)})

    def halo(to, at, ref, first, second):
        def part(rows_of):
            a = zero8 if first is None else rows_of(first)
            b = zero8 if second is None else rows_of(second)
            return a, b

        def put(start, a, b, mask):
            to[0, at, start : start + a.shape[0]] = pick(mask, a, b)
            to[1, at, start : start + a.shape[0]] = pick(mask, b, a)

        a, b = part(lambda j: pick(row >= 4, pltpu.roll(ref[j, rows : rows + 8], 4, 0), 0.0))
        put(0, a, b, even)
        a, b = part(lambda j: pick(row < 4, pltpu.roll(ref[j, rows : rows + 8], 4, 0), 0.0))
        put(8 + rows, a, b, even)
        big = jnp.zeros((rows, lanes), F32)
        a = big if first is None else ref[first, 0:rows]
        b = big if second is None else ref[second, 0:rows]
        put(8, a, b, even_own)

    halo(S, 1, from_down, 0, 1)
    halo(S, 2, from_down, 2, 3)
    halo(K, 0, from_down, None, 4)
    halo(K, 1, from_down, 5, 6)
    halo(K, 2, from_down, 7, 8)
    halo(S, HP + own, from_up, 0, 1)
    halo(S, HP + own + 1, from_up, 2, 3)
    halo(K, HP + own, from_up, 4, 5)
    halo(K, HP + own + 1, from_up, 6, 7)
    halo(K, HP + own + 2, from_up, 8, None)
    level = Level(K, S, U, W, D, own, (wide, lanes))
    for colour in (0, 1):
        level.setup(colour, without(span(own, 4 - colour), inner_span(own, 1)))
    level.all_clear(4)
    level.sweep(1, without(span(own, 3), inner_span(own, 2)))
    level.sweep(0, without(span(own, 2), inner_span(own, 3)))
    level.sweep(1, span(own, 1))
    level.residual(R, span(own, 0), 2, 8)
    store_field(U, field, own, even_own, wide)
    zero = jnp.zeros((rows, lanes), F32)
    for colour in (0, 1):
        for at in (0, 1, own + 2, own + 3):
            R[colour, at] = zero
    half = rows // 2
    block = half + 8
    for q in range(own + 2):
        Z[block * q : block * (q + 1)] = product(
            row_restriction(rows, True), restrict_planes(R, q + 1, even_own))
    source = product(Z[...], lane_restriction(lanes))
    row = lax.broadcasted_iota(jnp.int32, (half, lanes // 2), 0)
    for q in range(own + 2):
        at = block * q
        rows_of = source[at : at + half]
        source_out[q] = rows_of
        send.put(q, pick(row == half - 1, source[at + half : at + half + 1], rows_of),
                 pick(row == 0, source[at + half + 1 : at + half + 2], rows_of))


def widen_planes(K, send, planes, of):
    for q in range(planes):
        K[q] = of(q)
    for j in range(6):
        send.put(j, K[j], K[planes - 6 + j])


def mean_planes_kernel(own_rows, from_a, from_b, K, to_a, to_b):
    from_low, from_high = got_pair(from_a, from_b, "inner")

    def of(q):
        return jnp.concatenate([from_low[q], own_rows[q], from_high[q]], axis=0)

    widen_planes(K, Send(to_a, to_b, "outer"), own_rows.shape[0], of)


def middle_setup_kernel(k, from_a, from_b, K, W, D, I):
    from_down, from_up = got_pair(from_a, from_b, "outer")
    _, pairs, wide, lanes = K.shape
    planes = k.shape[0]
    even = even_mask(wide, lanes)

    def plane(i):
        if i < 0:
            return from_down[6 + i]
        return k[i] if i < planes else from_up[i - planes]

    for p in range(pairs):
        a, b = plane(2 * (p - HP)), plane(2 * (p - HP) + 1)
        K[0, p] = pick(even, a, b)
        K[1, p] = pick(even, b, a)
    Level(K, None, None, W, D, pairs - 2 * HP, (wide, lanes)).all_setup(5, I)


def source_planes_kernel(own_rows, sent_a, sent_b, from_a, from_b, S, to_a, to_b):
    planes, rows, lanes = own_rows.shape
    row = lax.broadcasted_iota(jnp.int32, (rows, lanes), 0)
    first, last = row == 0, row == rows - 1
    to_low, to_high = got_pair(sent_a, sent_b, "inner")
    from_low, from_high = got_pair(from_a, from_b, "inner")

    def of(q):
        got_low, got_high = from_low[q], from_high[q]
        low = pick(first, 0.0, got_low) + pick(last, to_low[q], 0.0)
        mine = own_rows[q] + pick(first, got_low, 0.0) + pick(last, got_high, 0.0)
        high = pick(last, 0.0, got_high) + pick(first, to_high[q], 0.0)
        return jnp.concatenate([low, mine, high], axis=0)

    widen_planes(S, Send(to_a, to_b, "outer"), planes, of)


def middle_kernel(s, source_a, source_b, K, W, D, I,
                  field, s_next, k_next, to_a, to_b,
                  S, U, R, Z, Zk):
    from_down, from_up = got_pair(source_a, source_b, "outer")
    send = Send(to_a, to_b, "outer")
    planes = field.shape[0]
    _, pairs, wide, lanes = K.shape
    own = planes // 2
    even = even_mask(wide, lanes)
    zero = jnp.zeros((wide, lanes), F32)

    def source_plane(i):
        if i < -5 or i > planes + 4:
            return zero
        if i < -1:
            return from_down[i + 5]
        if i == -1:
            return from_down[4] + s[0]
        if i == 0:
            return s[1] + from_down[5]
        if i < planes - 1:
            return s[i + 1]
        if i == planes - 1:
            return s[planes] + from_up[0]
        if i == planes:
            return from_up[1] + s[planes + 1]
        return from_up[i - planes + 1]

    level = Level(K, S, U, W, D, own, (wide, lanes))
    for p in range(-HP, own + HP):
        a, b = source_plane(2 * p), source_plane(2 * p + 1)
        S[0, HP + p] = pick(even, a, b)
        S[1, HP + p] = pick(even, b, a)
    for colour in (0, 1):
        for p in span(own, 5 - colour):
            level.begin(colour, p, I[colour, p])
    level.all_clear(5)
    level.all_sweeps(5)
    level.residual(R, span(own, 1), 0, 0)
    rows = field.shape[1]
    store_field(U, field, own, even_mask(rows, lanes), wide)
    half = wide // 2
    for q in range(own):
        Z[half * q : half * (q + 1)] = product(
            row_restriction(wide, False), restrict_planes(R, q + 1, even))
    for q in range(own + 2):
        total = K[0, HP - 1 + q] + K[1, HP - 1 + q]
        Zk[half * q : half * (q + 1)] = product(row_sum(wide), total)
    source = product(Z[...], lane_restriction(lanes))
    mean = product(Zk[...], lane_mean(lanes))
    for q in range(own):
        s_next[q] = source[half * q : half * (q + 1)]
        k_next[q] = mean[half * (q + 1) : half * (q + 2)]
    for j in range(4):
        send.put(j, s_next[j], s_next[own - 4 + j])
    for j in range(5):
        send.put(4 + j, mean[half * (1 + j) : half * (2 + j)],
                 mean[half * (own - 4 + j) : half * (own - 3 + j)])


def coarse_kernel(s, k, from_a, from_b, field, rest, K, S, U, W, D, R):
    from_down, from_up = got_pair(from_a, from_b, "outer")
    planes, wide, lanes = k.shape
    own = planes // 2
    rows = field.shape[1]
    even = even_mask(wide, lanes)
    even_own = even_mask(rows, lanes)
    zero = jnp.zeros((wide, lanes), F32)

    def source_plane(i):
        if i < -4 or i > planes + 3:
            return zero
        if i < 0:
            return from_down[4 + i]
        return s[i] if i < planes else from_up[i - planes]

    def mean_plane(i):
        if i < -5 or i > planes + 4:
            return zero
        if i < 0:
            return from_down[9 + i]
        return k[i] if i < planes else from_up[4 + i - planes]

    for p in range(-HP, own + HP):
        for to, plane in ((S, source_plane), (K, mean_plane)):
            a, b = plane(2 * p), plane(2 * p + 1)
            to[0, HP + p] = pick(even, a, b)
            to[1, HP + p] = pick(even, b, a)
    level = Level(K, S, U, W, D, own, (wide, lanes))
    level.all_setup(4)
    level.all_clear(4)
    level.all_sweeps(4)
    level.residual(R, span(own, 0), 2, (wide - rows) // 2)
    store_field(U, field, own, even_own, wide)
    for p in range(own):
        red, black = R[0, p + 2], R[1, p + 2]
        rest[2 * p] = pick(even_own, red, black)
        rest[2 * p + 1] = pick(even_own, black, red)


def limit(scratch):
    words = 0
    for shape in scratch:
        size = 1
        for n in shape:
            size *= n
        words += size
    return 4 * words + (12 << 20)


def call(kernel, outs, scratch, *args, in_specs=None, name=None, results=False):
    extra = {}
    if in_specs is None:
        args = [pltpu.with_memory_space_constraint(a, pltpu.VMEM) for a in args]
    else:
        args = [pltpu.with_memory_space_constraint(a, pltpu.HBM) for a in args]
        extra = {"in_specs": in_specs, "grid": (1,)}
        extra["out_specs"] = [pl.BlockSpec(memory_space=pltpu.VMEM) for _ in outs]
    if results:
        extra = {"out_specs": [pl.BlockSpec(memory_space=pltpu.VMEM) for _ in outs]}
    return pl.pallas_call(
        kernel,
        out_shape=[jax.ShapeDtypeStruct(o, F32) if results else pltpu.VMEM(o, F32) for o in outs],
        scratch_shapes=[pltpu.VMEM(shape, F32) for shape in scratch],
        compiler_params=pltpu.CompilerParams(vmem_limit_bytes=limit(scratch)),
        name=name,
        **extra,
    )(*args)


def level_arrays(own, wide, lanes):
    block = (2, own + 2 * HP, wide, lanes)
    return [block, block, block, (12, *block[1:]), block]


def exchange(a, b, axis):
    size = lax.axis_size(axis)

    def swapped(x, first):
        pairs = [(i, i + 1) for i in range(first, size - 1, 2)]
        return lax.ppermute(x, axis, pairs + [(j, i) for i, j in pairs])

    return swapped(a, 1), swapped(b, 0)


def body(right_side, coefficient):
    s, k = right_side, coefficient
    planes, rows, lanes = s.shape
    own = planes // 2
    wide = rows + 16

    low = pl.BlockSpec((planes, 8, lanes), lambda i: (0, 0, 0))
    high = pl.BlockSpec((planes, 8, lanes), lambda i: (0, rows // 8 - 1, 0))
    message = (2, own, 8, lanes)
    sent = call(pack_rows_kernel, [message] * 2, [], s, s, k, k,
                in_specs=[low, high, low, high], name="pack_rows")
    row_halo = exchange(*sent, "inner")
    half, next_lanes = rows // 2, lanes // 2
    (mean,) = call(mean_kernel, [(own, half, next_lanes)], [(half * own, lanes)], k, name="mean")
    message = (9, rows + 8, lanes)
    to_a, to_b = call(pack_planes_kernel, [message] * 2, [], s, k, *row_halo, name="pack_planes")
    mean, to_a, to_b = lax.optimization_barrier((mean, to_a, to_b))
    plane_halo = exchange(to_a, to_b, "outer")
    arrays = level_arrays(own, wide, lanes)
    early = [(a[0], own, wide, lanes) for a in arrays]
    prepared = call(fine_prepare_kernel, early, [], s, k, *row_halo, name="fine_prepare")
    mean, *prepared = lax.optimization_barrier((mean, *prepared))
    mean_halo = exchange(mean, mean, "inner")

    count = own + 2
    message = (count, half, next_lanes)
    field0, source, to_a, to_b = call(
        fine_kernel, [s.shape, message, message, message],
        [*arrays, (2, own + 4, rows, lanes), ((half + 8) * count, lanes)],
        *plane_halo, *prepared, name="fine_level")

    planes, rows, lanes = own, half, next_lanes
    own, wide = planes // 2, 3 * rows
    *mean_halo, to_a, to_b = lax.optimization_barrier((*mean_halo, to_a, to_b))
    row_halo = exchange(to_a, to_b, "inner")
    message = (6, wide, lanes)
    k1, *sent = call(
        mean_planes_kernel, [(planes, wide, lanes), message, message], [],
        mean, *mean_halo, name="mean_planes")
    mean_halo = exchange(*sent, "outer")
    K, S, U, W, D = level_arrays(own, wide, lanes)
    constants = call(middle_setup_kernel, [K, W, D, K], [], k1, *mean_halo, name="middle_setup")
    message = (6, wide, lanes)
    s1, *sent = call(
        source_planes_kernel, [(planes + 2, wide, lanes), message, message], [],
        source, to_a, to_b, *row_halo, name="source_planes")
    source_halo = exchange(*sent, "outer")
    half, next_lanes = wide // 2, lanes // 2
    block, message = (own, half, next_lanes), (9, half, next_lanes)
    field1, s2, k2, *sent = call(
        middle_kernel, [(planes, rows, lanes), block, block, message, message],
        [S, U, (2, own + 2, wide, lanes), (half * own, lanes), (half * (own + 2), lanes)],
        s1, *source_halo, *constants, name="middle_level")

    planes, rows, wide, lanes = own, rows // 2, half, next_lanes
    own = planes // 2
    field2, rest = call(
        coarse_kernel, [(planes, rows, lanes)] * 2,
        [*level_arrays(own, wide, lanes), (2, own + 4, rows, lanes)],
        s2, k2, *exchange(*sent, "outer"), name="coarse_level", results=True)
    return field0, field1, field2, rest


def solution(mesh):
    spec = P("outer", "inner", None)
    return jax.shard_map(body, mesh=mesh, in_specs=(spec, spec), out_specs=(spec,) * 4, check_vma=False)
```

```python
import jax
import jax.numpy as jnp
from jax import lax
from jax.experimental import pallas as pl
from jax.experimental.pallas import tpu as pltpu
from jax.sharding import PartitionSpec as P

F32 = jnp.float32
HP = 3
HIGHEST = lax.Precision.HIGHEST


def tiled(tile, rows, lanes):
    wide = jnp.concatenate([tile] * (lanes // 128), axis=1)
    return jnp.concatenate([wide] * (rows // 8), axis=0)


def even_mask(rows, lanes):
    row = lax.broadcasted_iota(jnp.int32, (8, 128), 0)
    lane = lax.broadcasted_iota(jnp.int32, (8, 128), 1)
    return tiled((row + lane) & 1, rows, lanes) == 0


def pick(mask, a, b):
    return jnp.where(mask, a, b)


def odd_on(axis):
    return lax.axis_index(axis) % 2 == 1


def choose(odd, a, b):
    return lax.select(jnp.full(a.shape, odd), a, b)


class Got:
    def __init__(self, a, b, odd, upper):
        self.first, self.second = (a, b) if upper else (b, a)
        self.odd = odd
        self.shape = a.shape

    def __getitem__(self, at):
        return choose(self.odd, self.first[at], self.second[at])


def got_pair(a, b, axis):
    odd = odd_on(axis)
    return Got(a, b, odd, False), Got(a, b, odd, True)


class Send:
    def __init__(self, a, b, axis):
        self.a, self.b, self.odd = a, b, odd_on(axis)

    def put(self, at, low, high):
        self.a[at] = choose(self.odd, high, low)
        self.b[at] = choose(self.odd, low, high)


def row_index(lanes):
    return lax.broadcasted_iota(jnp.int32, (8, lanes), 0)


def lane_edge(value, at_start):
    lanes = value.shape[1]
    lane = lax.broadcasted_iota(jnp.int32, (value.shape[0], 128), 1)
    if at_start:
        edge = pick(lane == 0, 0.0, value[:, :128])
        return edge if lanes == 128 else jnp.concatenate([edge, value[:, 128:]], axis=1)
    edge = pick(lane == 127, 0.0, value[:, lanes - 128 :])
    return edge if lanes == 128 else jnp.concatenate([value[:, : lanes - 128], edge], axis=1)


def neighbours(ref, colour, p, pairs, even):
    other = 1 - colour
    x = ref[other, p]
    if isinstance(p, int):
        below, above = ref[other, max(p - 1, 0)], ref[other, min(p + 1, pairs - 1)]
    else:
        below = ref[other, jnp.maximum(p - 1, 0)]
        above = ref[other, jnp.minimum(p + 1, pairs - 1)]
    far = pick(even, below, above) if colour == 0 else pick(even, above, below)
    rows, lanes = x.shape
    return (
        x,
        far,
        pltpu.roll(x, 1, 0),
        pltpu.roll(x, rows - 1, 0),
        pltpu.roll(x, 1, 1),
        pltpu.roll(x, lanes - 1, 1),
    )


def span(own, layers):
    extra = (layers + 1) // 2
    return range(HP - extra, HP + own + extra)


class Store:
    def __init__(self, ref, start=0, early=None, held=()):
        self.ref, self.start = ref, start
        self.early = {key: early for key in held}

    def place(self, at):
        first, p, *rest = at
        early = self.early.get((first, p))
        if early is not None:
            return early.ref, (first, p - early.start, *rest)
        return self.ref, (first, p - self.start, *rest)

    def __getitem__(self, at):
        ref, at = self.place(at)
        return ref[at]

    def __setitem__(self, at, value):
        self.early.pop((at[0], at[1]), None)
        ref, at = self.place(at)
        ref[at] = value


class Level:
    def __init__(self, K, S, U, W, D, own, shape):
        self.K, self.S, self.U, self.W, self.D, self.own = K, S, U, W, D, own
        self.pairs = own + 2 * HP
        self.rows, self.lanes = shape
        self.even = even_mask(self.rows, self.lanes)

    def setup(self, colour, pairs, inverse_out=None):
        for p in pairs:
            near = list(neighbours(self.K, colour, p, self.pairs, self.even))
            near[4] = lane_edge(near[4], True)
            near[5] = lane_edge(near[5], False)
            centre = self.K[colour, p]
            total = near[0]
            for value in near[1:]:
                total = total + value
            diag = 3.0 * centre + 0.5 * total
            inverse = pick(centre > 0.0, 1.0 / diag, 0.0)
            half = 0.5 * inverse
            for i, value in enumerate(near):
                weight = (centre + value) * half
                if i == 4:
                    weight = lane_edge(weight, True)
                if i == 5:
                    weight = lane_edge(weight, False)
                self.W[colour * 6 + i, p] = weight
            self.D[colour, p] = diag
            if inverse_out is not None:
                inverse_out[colour, p] = inverse
            else:
                self.begin(colour, p, inverse)

    def begin(self, colour, p, inverse):
        start = self.S[colour, p] * inverse
        self.S[colour, p] = start
        if colour == 0:
            self.U[0, p] = start

    def clear(self, colour, pairs):
        zero = jnp.zeros((self.rows, self.lanes), F32)
        for p in range(self.pairs):
            if p not in pairs:
                self.U[colour, p] = zero

    def relaxed(self, colour, p):
        near = neighbours(self.U, colour, p, self.pairs, self.even)
        total = self.S[colour, p]
        for i, value in enumerate(near):
            total = total + self.W[colour * 6 + i, p] * value
        return total

    def sweep(self, colour, pairs):
        for p in pairs:
            self.U[colour, p] = self.relaxed(colour, p)

    def residual(self, R, pairs, pad, inset):
        for i, p in enumerate(pairs):
            for colour in (0, 1):
                rest = self.D[colour, p] * (self.relaxed(colour, p) - self.U[colour, p])
                R[colour, i + pad] = rest[inset : self.rows - inset]

    def all_setup(self, depth, inverse_out=None):
        for colour in (0, 1):
            self.setup(colour, span(self.own, depth - colour), inverse_out)

    def all_clear(self, depth):
        for colour in (0, 1):
            self.clear(colour, span(self.own, depth - colour))

    def all_sweeps(self, depth):
        for i, colour in enumerate((1, 0, 1)):
            self.sweep(colour, span(self.own, depth - 1 - i))


def without(pairs, inner):
    return [p for p in pairs if p not in inner]


def inner_span(own, margin):
    return range(HP + margin, HP + own - margin)


def store_field(U, out, own, even, wide):
    rows = out.shape[1]
    first = (wide - rows) // 2
    for p in range(own):
        red = U[0, HP + p, first : first + rows]
        black = U[1, HP + p, first : first + rows]
        out[2 * p] = pick(even, red, black)
        out[2 * p + 1] = pick(even, black, red)


def restrict_planes(R, at, even):
    red, black = R[0, at], R[1, at]
    odd_below = pick(even, R[1, at - 1], R[0, at - 1])
    even_above = pick(even, R[0, at + 1], R[1, at + 1])
    return (3.0 * (red + black) + (odd_below + even_above)) * 0.125


def row_restriction(rows, ends):
    half = rows // 2
    shape = (half + 8 if ends else half, rows)
    j = lax.broadcasted_iota(jnp.int32, shape, 0)
    m = lax.broadcasted_iota(jnp.int32, shape, 1)
    inner = (m == 2 * j) | (m == 2 * j + 1)
    outer = (m == 2 * j - 1) | (m == 2 * j + 2)
    main = pick(inner, 0.375, pick(outer, 0.125, 0.0)).astype(F32)
    if not ends:
        return main
    edge = pick(((j == half) & (m == 0)) | ((j == half + 1) & (m == rows - 1)), 0.125, 0.0)
    return pick(j < half, main, edge).astype(F32)


def row_sum(rows):
    j = 2 * lax.broadcasted_iota(jnp.int32, (rows // 2, rows), 0)
    m = lax.broadcasted_iota(jnp.int32, (rows // 2, rows), 1)
    return pick((m == j) | (m == j + 1), 1.0, 0.0).astype(F32)


def product(a, b):
    return jnp.dot(a, b, precision=HIGHEST, preferred_element_type=F32)


def lane_restriction(lanes):
    m = lax.broadcasted_iota(jnp.int32, (lanes, lanes // 2), 0)
    i = 2 * lax.broadcasted_iota(jnp.int32, (lanes, lanes // 2), 1)
    inner = (m == i) | (m == i + 1)
    outer = (m == i - 1) | (m == i + 2)
    return pick(inner, 1.5, pick(outer, 0.5, 0.0)).astype(F32)


def lane_mean(lanes):
    m = lax.broadcasted_iota(jnp.int32, (lanes, lanes // 2), 0)
    i = 2 * lax.broadcasted_iota(jnp.int32, (lanes, lanes // 2), 1)
    return pick((m == i) | (m == i + 1), 0.125, 0.0).astype(F32)


def pack_rows_kernel(s_low, s_high, k_low, k_high, end_a, end_b, inner_a, inner_b):
    planes, _, lanes = s_low.shape
    own = planes // 2
    even = even_mask(8, lanes)
    ends, inner = Send(end_a, end_b, "inner"), Send(inner_a, inner_b, "inner")
    cat = lambda *parts: jnp.concatenate(parts, axis=0)

    for p in range(own):
        def pair(ref):
            a, b = ref[2 * p], ref[2 * p + 1]
            return pick(even, a, b), pick(even, b, a)

        ls, lk, hs, hk = pair(s_low), pair(k_low), pair(s_high), pair(k_high)
        send, at = (inner, p - 2) if 2 <= p < own - 2 else (ends, p if p < 2 else p - own + 4)
        send.put((0, at), cat(lk[0][0:4], ls[0][0:4]), cat(hk[0][4:8], hs[0][4:8]))
        send.put((1, at), cat(lk[1][0:5], ls[1][0:3]), cat(hk[1][3:8], hs[1][5:8]))


def rows_from(got, p, own):
    ends, inner = got
    if 2 <= p < own - 2:
        return inner[0, p - 2], inner[1, p - 2]
    at = p if p < 2 else p - own + 4
    return ends[0, at], ends[1, at]


def between(row, first, last):
    return (row >= first) & (row <= last)


def pack_planes_kernel(s, k, from_a, from_b, to_a, to_b):
    planes, rows, lanes = s.shape
    own = planes // 2
    even = even_mask(8, lanes)
    even_own = even_mask(rows, lanes)
    row = row_index(lanes)
    low, high = got_pair(from_a, from_b, "inner")
    send = Send(to_a, to_b, "outer")

    def edges(plane, of_k):
        lr, lb = rows_from((low, None), plane // 2, own)
        hr, hb = rows_from((high, None), plane // 2, own)
        if of_k:
            red = jnp.concatenate([lr[0:4], hr[0:4]], axis=0)
            black = jnp.concatenate([lb[1:5], hb[0:4]], axis=0)
        else:
            red = jnp.concatenate([lr[4:8], hr[4:8]], axis=0)
            black = jnp.concatenate([lb[4:8], hb[5:8], hb[7:8]], axis=0)
        return (pick(even, red, black), pick(even, black, red))[plane % 2]

    def corners(plane):
        tiles = []
        for d in (1, 2, 3):
            source = edges(plane(d), False)
            mean = pltpu.roll(edges(plane(5 - d), True), 4, 0)
            tiles.append(pick(between(row, d, 7 - d), source, mean))
        return tiles + [edges(plane(1), True)]

    for j in range(3):
        send.put(j, s[j], s[planes - 3 + j])
    for j in range(4):
        send.put(3 + j, k[j], k[planes - 4 + j])
    send.put(7, pick(even_own, pltpu.roll(k[4], 1, 1), s[3]),
             pick(even_own, s[planes - 4], pltpu.roll(k[planes - 5], 1, 1)))
    down, up = corners(lambda d: d - 1), corners(lambda d: planes - d)
    for i in range(4):
        send.put((8, slice(8 * i, 8 * i + 8)), down[i], up[i])


def mean_kernel(k, out, Z):
    planes, rows, lanes = k.shape
    half = rows // 2
    for q in range(planes // 2):
        Z[half * q : half * (q + 1)] = product(row_sum(rows), k[2 * q] + k[2 * q + 1])
    mean = product(Z[...], lane_mean(lanes))
    for q in range(planes // 2):
        out[q] = mean[half * q : half * (q + 1)]


def fine_prepare_kernel(s, k, end_a, end_b, inner_a, inner_b, *arrays):
    planes, rows, lanes = s.shape
    own = planes // 2
    wide = rows + 16
    from_low, from_high = zip(got_pair(end_a, end_b, "inner"), got_pair(inner_a, inner_b, "inner"))
    even_own = even_mask(rows, lanes)
    row = row_index(lanes)
    K, S, U, W, D = [Store(ref, HP) for ref in arrays]

    def fill(p):
        at = HP + p
        lr, lb = rows_from(from_low, p, own)
        hr, hb = rows_from(from_high, p, own)
        K[0, at, 0:8] = pick(row >= 4, pltpu.roll(lr, 4, 0), 0.0)
        K[1, at, 0:8] = pick(row >= 3, pltpu.roll(lb, 3, 0), 0.0)
        S[0, at, 0:8] = pick(row >= 4, lr, 0.0)
        S[1, at, 0:8] = pick(row >= 5, lb, 0.0)
        K[0, at, 8 + rows : wide] = pick(row < 4, hr, 0.0)
        K[1, at, 8 + rows : wide] = pick(row < 5, hb, 0.0)
        S[0, at, 8 + rows : wide] = pick(row < 4, pltpu.roll(hr, 4, 0), 0.0)
        S[1, at, 8 + rows : wide] = pick(row < 3, pltpu.roll(hb, 3, 0), 0.0)
        for ref, to in ((s, S), (k, K)):
            a, b = ref[2 * p], ref[2 * p + 1]
            to[0, at, 8 : 8 + rows] = pick(even_own, a, b)
            to[1, at, 8 : 8 + rows] = pick(even_own, b, a)

    for p in range(own):
        fill(p)
    level = Level(K, S, U, W, D, own, (wide, lanes))
    level.setup(0, inner_span(own, 1))
    level.setup(1, inner_span(own, 1))
    level.sweep(1, inner_span(own, 2))
    level.sweep(0, inner_span(own, 3))


def fine_kernel(plane_a, plane_b, K0, S0, U0, W0, D0,
                field, source_out, to_a, to_b, K1, S1, U1, W1, D1, R, Z):
    from_down, from_up = got_pair(plane_a, plane_b, "outer")
    send = Send(to_a, to_b, "inner")
    planes, rows, lanes = field.shape
    own = planes // 2
    wide = rows + 16
    even = even_mask(wide, lanes)
    even_own = even_mask(rows, lanes)
    row = row_index(lanes)
    def store(ref, early, firsts, pairs):
        return Store(ref, 0, Store(early, HP), [(i, p) for i in firsts for p in pairs])

    inside = inner_span(own, 1)
    K = store(K1, K0, (0, 1), inner_span(own, 0))
    S = store(S1, S0, (0, 1), inner_span(own, 0))
    W = store(W1, W0, range(12), inside)
    D = store(D1, D0, (0, 1), inside)
    U = store(U1, U0, (0,), inside)
    U.early.update({(1, p): Store(U0, HP) for p in inner_span(own, 2)})

    def framed(low_edge, middle, high_edge):
        return jnp.concatenate(
            [pick(row >= 4, low_edge, 0.0), middle, pick(row < 4, high_edge, 0.0)], axis=0)

    def source_at(got, d, up):
        if d == 4:
            mixed = got[7]
            middle = pick(even_own, 0.0, mixed) if up else pick(even_own, mixed, 0.0)
            edge = jnp.zeros((8, lanes), F32)
        else:
            middle = got[d - 1 if up else 3 - d]
            edge = pick(between(row, d, 7 - d), got[8, 8 * d - 8 : 8 * d], 0.0)
            edge = pltpu.roll(edge, 4, 0)
        return framed(edge, middle, edge)

    def mean_at(got, d, up):
        edge = jnp.zeros((8, lanes), F32)
        if d == 6:
            return jnp.zeros((wide, lanes), F32)
        if d == 5:
            mixed = pltpu.roll(got[7], lanes - 1, 1)
            middle = pick(even_own, 0.0, mixed) if up else pick(even_own, mixed, 0.0)
        else:
            middle = got[2 + d if up else 7 - d]
            if d == 1:
                edge = pltpu.roll(got[8, 24:32], 4, 0)
            else:
                edge = pick(between(row, 5 - d, 2 + d), 0.0, got[8, 8 * (4 - d) : 8 * (5 - d)])
        return framed(edge, middle, edge)

    for j in range(HP):
        for to, plane in ((K, mean_at), (S, source_at)):
            if to is S and j == 2:
                continue
            near, far = 2 * j + 1, 2 * j + 2
            a, b = plane(from_up, near, True), plane(from_up, far, True)
            to[0, HP + own + j] = pick(even, a, b)
            to[1, HP + own + j] = pick(even, b, a)
            a, b = plane(from_down, far, False), plane(from_down, near, False)
            to[0, HP - 1 - j] = pick(even, a, b)
            to[1, HP - 1 - j] = pick(even, b, a)
    level = Level(K, S, U, W, D, own, (wide, lanes))
    for colour in (0, 1):
        level.setup(colour, without(span(own, 4 - colour), inner_span(own, 1)))
    level.all_clear(4)
    level.sweep(1, without(span(own, 3), inner_span(own, 2)))
    level.sweep(0, without(span(own, 2), inner_span(own, 3)))
    level.sweep(1, span(own, 1))
    level.residual(R, span(own, 0), 2, 8)
    store_field(U, field, own, even_own, wide)
    zero = jnp.zeros((rows, lanes), F32)
    for colour in (0, 1):
        for at in (0, 1, own + 2, own + 3):
            R[colour, at] = zero
    half = rows // 2
    block = half + 8
    for q in range(own + 2):
        Z[block * q : block * (q + 1)] = product(
            row_restriction(rows, True), restrict_planes(R, q + 1, even_own))
    source = product(Z[...], lane_restriction(lanes))
    row = lax.broadcasted_iota(jnp.int32, (half, lanes // 2), 0)
    for q in range(own + 2):
        at = block * q
        rows_of = source[at : at + half]
        source_out[q] = rows_of
        send.put(q, pick(row == half - 1, source[at + half : at + half + 1], rows_of),
                 pick(row == 0, source[at + half + 1 : at + half + 2], rows_of))


def widen_planes(K, send, planes, of):
    for q in range(planes):
        K[q] = of(q)
    for j in range(6):
        send.put(j, K[j], K[planes - 6 + j])


def mean_planes_kernel(own_rows, from_a, from_b, K, to_a, to_b):
    from_low, from_high = got_pair(from_a, from_b, "inner")

    def of(q):
        return jnp.concatenate([from_low[q], own_rows[q], from_high[q]], axis=0)

    widen_planes(K, Send(to_a, to_b, "outer"), own_rows.shape[0], of)


def middle_setup_kernel(k, from_a, from_b, K, W, D, I):
    from_down, from_up = got_pair(from_a, from_b, "outer")
    _, pairs, wide, lanes = K.shape
    planes = k.shape[0]
    even = even_mask(wide, lanes)

    def plane(i):
        if i < 0:
            return from_down[6 + i]
        return k[i] if i < planes else from_up[i - planes]

    for p in range(pairs):
        a, b = plane(2 * (p - HP)), plane(2 * (p - HP) + 1)
        K[0, p] = pick(even, a, b)
        K[1, p] = pick(even, b, a)
    Level(K, None, None, W, D, pairs - 2 * HP, (wide, lanes)).all_setup(5, I)


def source_planes_kernel(own_rows, sent_a, sent_b, from_a, from_b, S, to_a, to_b):
    planes, rows, lanes = own_rows.shape
    row = lax.broadcasted_iota(jnp.int32, (rows, lanes), 0)
    first, last = row == 0, row == rows - 1
    to_low, to_high = got_pair(sent_a, sent_b, "inner")
    from_low, from_high = got_pair(from_a, from_b, "inner")

    def of(q):
        got_low, got_high = from_low[q], from_high[q]
        low = pick(first, 0.0, got_low) + pick(last, to_low[q], 0.0)
        mine = own_rows[q] + pick(first, got_low, 0.0) + pick(last, got_high, 0.0)
        high = pick(last, 0.0, got_high) + pick(first, to_high[q], 0.0)
        return jnp.concatenate([low, mine, high], axis=0)

    widen_planes(S, Send(to_a, to_b, "outer"), planes, of)


def middle_kernel(s, source_a, source_b, K, W, D, I,
                  field, s_next, k_next, to_a, to_b,
                  S, U, R, Z, Zk):
    from_down, from_up = got_pair(source_a, source_b, "outer")
    send = Send(to_a, to_b, "outer")
    planes = field.shape[0]
    _, pairs, wide, lanes = K.shape
    own = planes // 2
    even = even_mask(wide, lanes)
    zero = jnp.zeros((wide, lanes), F32)

    def source_plane(i):
        if i < -5 or i > planes + 4:
            return zero
        if i < -1:
            return from_down[i + 5]
        if i == -1:
            return from_down[4] + s[0]
        if i == 0:
            return s[1] + from_down[5]
        if i < planes - 1:
            return s[i + 1]
        if i == planes - 1:
            return s[planes] + from_up[0]
        if i == planes:
            return from_up[1] + s[planes + 1]
        return from_up[i - planes + 1]

    level = Level(K, S, U, W, D, own, (wide, lanes))
    for p in range(-HP, own + HP):
        a, b = source_plane(2 * p), source_plane(2 * p + 1)
        S[0, HP + p] = pick(even, a, b)
        S[1, HP + p] = pick(even, b, a)
    for colour in (0, 1):
        for p in span(own, 5 - colour):
            level.begin(colour, p, I[colour, p])
    level.all_clear(5)
    level.all_sweeps(5)
    level.residual(R, span(own, 1), 0, 0)
    rows = field.shape[1]
    store_field(U, field, own, even_mask(rows, lanes), wide)
    half = wide // 2
    for q in range(own):
        Z[half * q : half * (q + 1)] = product(
            row_restriction(wide, False), restrict_planes(R, q + 1, even))
    for q in range(own + 2):
        total = K[0, HP - 1 + q] + K[1, HP - 1 + q]
        Zk[half * q : half * (q + 1)] = product(row_sum(wide), total)
    source = product(Z[...], lane_restriction(lanes))
    mean = product(Zk[...], lane_mean(lanes))
    for q in range(own):
        s_next[q] = source[half * q : half * (q + 1)]
        k_next[q] = mean[half * (q + 1) : half * (q + 2)]
    for j in range(4):
        send.put(j, s_next[j], s_next[own - 4 + j])
    for j in range(5):
        send.put(4 + j, mean[half * (1 + j) : half * (2 + j)],
                 mean[half * (own - 4 + j) : half * (own - 3 + j)])


def coarse_kernel(s, k, from_a, from_b, field, rest, K, S, U, W, D, R):
    from_down, from_up = got_pair(from_a, from_b, "outer")
    planes, wide, lanes = k.shape
    own = planes // 2
    rows = field.shape[1]
    even = even_mask(wide, lanes)
    even_own = even_mask(rows, lanes)
    zero = jnp.zeros((wide, lanes), F32)

    def source_plane(i):
        if i < -4 or i > planes + 3:
            return zero
        if i < 0:
            return from_down[4 + i]
        return s[i] if i < planes else from_up[i - planes]

    def mean_plane(i):
        if i < -5 or i > planes + 4:
            return zero
        if i < 0:
            return from_down[9 + i]
        return k[i] if i < planes else from_up[4 + i - planes]

    for p in range(-HP, own + HP):
        for to, plane in ((S, source_plane), (K, mean_plane)):
            a, b = plane(2 * p), plane(2 * p + 1)
            to[0, HP + p] = pick(even, a, b)
            to[1, HP + p] = pick(even, b, a)
    level = Level(K, S, U, W, D, own, (wide, lanes))
    level.all_setup(4)
    level.all_clear(4)
    level.all_sweeps(4)
    level.residual(R, span(own, 0), 2, (wide - rows) // 2)
    store_field(U, field, own, even_own, wide)
    for p in range(own):
        red, black = R[0, p + 2], R[1, p + 2]
        rest[2 * p] = pick(even_own, red, black)
        rest[2 * p + 1] = pick(even_own, black, red)


def limit(scratch):
    words = 0
    for shape in scratch:
        size = 1
        for n in shape:
            size *= n
        words += size
    return 4 * words + (12 << 20)


def call(kernel, outs, scratch, *args, in_specs=None, name=None, results=False, cost=None):
    extra = {}
    if in_specs is None:
        args = [pltpu.with_memory_space_constraint(a, pltpu.VMEM) for a in args]
    else:
        args = [pltpu.with_memory_space_constraint(a, pltpu.HBM) for a in args]
        extra = {"in_specs": in_specs, "grid": (1,)}
        extra["out_specs"] = [pl.BlockSpec(memory_space=pltpu.VMEM) for _ in outs]
    if results:
        extra = {"out_specs": [pl.BlockSpec(memory_space=pltpu.VMEM) for _ in outs]}
    return pl.pallas_call(
        kernel,
        out_shape=[jax.ShapeDtypeStruct(o, F32) if results else pltpu.VMEM(o, F32) for o in outs],
        scratch_shapes=[pltpu.VMEM(shape, F32) for shape in scratch],
        compiler_params=pltpu.CompilerParams(vmem_limit_bytes=limit(scratch)),
        name=name,
        cost_estimate=cost,
        **extra,
    )(*args)


def level_arrays(own, wide, lanes):
    block = (2, own + 2 * HP, wide, lanes)
    return [block, block, block, (12, *block[1:]), block]


def exchange(a, b, axis):
    size = lax.axis_size(axis)

    def swapped(x, first):
        pairs = [(i, i + 1) for i in range(first, size - 1, 2)]
        return lax.ppermute(x, axis, pairs + [(j, i) for i, j in pairs])

    return swapped(a, 1), swapped(b, 0)


def body(right_side, coefficient):
    s, k = right_side, coefficient
    planes, rows, lanes = s.shape
    own = planes // 2
    wide = rows + 16

    low = pl.BlockSpec((planes, 8, lanes), lambda i: (0, 0, 0))
    high = pl.BlockSpec((planes, 8, lanes), lambda i: (0, rows // 8 - 1, 0))
    ends, inner = (2, 4, 8, lanes), (2, own - 4, 8, lanes)
    end_a, end_b, inner_a, inner_b = call(
        pack_rows_kernel, [ends, ends, inner, inner], [], s, s, k, k,
        in_specs=[low, high, low, high], name="pack_rows")
    end_halo = exchange(end_a, end_b, "inner")
    inner_halo = exchange(inner_a, inner_b, "inner")
    half, next_lanes = rows // 2, lanes // 2
    (mean,) = call(mean_kernel, [(own, half, next_lanes)], [(half * own, lanes)], k, name="mean")
    message = (9, rows, lanes)
    to_a, to_b = call(pack_planes_kernel, [message] * 2, [], s, k, *end_halo, name="pack_planes")
    mean, to_a, to_b = lax.optimization_barrier((mean, to_a, to_b))
    plane_halo = exchange(to_a, to_b, "outer")
    arrays = level_arrays(own, wide, lanes)
    early = [(a[0], own, wide, lanes) for a in arrays]
    prepared = call(fine_prepare_kernel, early, [], s, k, *end_halo, *inner_halo,
                    name="fine_prepare", cost=pl.CostEstimate(0, 100 << 20, 0))
    mean_halo = exchange(mean, mean, "inner")

    count = own + 2
    message = (count, half, next_lanes)
    field0, source, to_a, to_b = call(
        fine_kernel, [s.shape, message, message, message],
        [*arrays, (2, own + 4, rows, lanes), ((half + 8) * count, lanes)],
        *plane_halo, *prepared, name="fine_level")

    planes, rows, lanes = own, half, next_lanes
    own, wide = planes // 2, 3 * rows
    *mean_halo, to_a, to_b = lax.optimization_barrier((*mean_halo, to_a, to_b))
    row_halo = exchange(to_a, to_b, "inner")
    message = (6, wide, lanes)
    k1, *sent = call(
        mean_planes_kernel, [(planes, wide, lanes), message, message], [],
        mean, *mean_halo, name="mean_planes")
    mean_halo = exchange(*sent, "outer")
    K, S, U, W, D = level_arrays(own, wide, lanes)
    constants = call(middle_setup_kernel, [K, W, D, K], [], k1, *mean_halo, name="middle_setup")
    message = (6, wide, lanes)
    s1, *sent = call(
        source_planes_kernel, [(planes + 2, wide, lanes), message, message], [],
        source, to_a, to_b, *row_halo, name="source_planes")
    source_halo = exchange(*sent, "outer")
    half, next_lanes = wide // 2, lanes // 2
    block, message = (own, half, next_lanes), (9, half, next_lanes)
    field1, s2, k2, *sent = call(
        middle_kernel, [(planes, rows, lanes), block, block, message, message],
        [S, U, (2, own + 2, wide, lanes), (half * own, lanes), (half * (own + 2), lanes)],
        s1, *source_halo, *constants, name="middle_level")

    planes, rows, wide, lanes = own, rows // 2, half, next_lanes
    own = planes // 2
    field2, rest = call(
        coarse_kernel, [(planes, rows, lanes)] * 2,
        [*level_arrays(own, wide, lanes), (2, own + 4, rows, lanes)],
        s2, k2, *exchange(*sent, "outer"), name="coarse_level", results=True)
    return field0, field1, field2, rest


def solution(mesh):
    spec = P("outer", "inner", None)
    return jax.shard_map(body, mesh=mesh, in_specs=(spec, spec), out_specs=(spec,) * 4, check_vma=False)
```

```python
import jax
import jax.numpy as jnp
from jax import lax
from jax.experimental import pallas as pl
from jax.experimental.pallas import tpu as pltpu
from jax.sharding import PartitionSpec as P

F32 = jnp.float32
HP = 3


def tiled(tile, rows, lanes):
    wide = jnp.concatenate([tile] * (lanes // 128), axis=1)
    return jnp.concatenate([wide] * (rows // 8), axis=0)


def even_mask(rows, lanes):
    row = lax.broadcasted_iota(jnp.int32, (8, 128), 0)
    lane = lax.broadcasted_iota(jnp.int32, (8, 128), 1)
    return tiled((row + lane) & 1, rows, lanes) == 0


def pick(mask, a, b):
    return jnp.where(mask, a, b)


def odd_on(axis):
    return lax.axis_index(axis) % 2 == 1


def choose(odd, a, b):
    return lax.select(jnp.full(a.shape, odd), a, b)


class Got:
    def __init__(self, a, b, odd, upper):
        self.first, self.second = (a, b) if upper else (b, a)
        self.odd = odd
        self.shape = a.shape

    def __getitem__(self, at):
        return choose(self.odd, self.first[at], self.second[at])


def got_pair(a, b, axis):
    odd = odd_on(axis)
    return Got(a, b, odd, False), Got(a, b, odd, True)


class Send:
    def __init__(self, a, b, axis):
        self.a, self.b, self.odd = a, b, odd_on(axis)

    def put(self, at, low, high):
        self.a[at] = choose(self.odd, high, low)
        self.b[at] = choose(self.odd, low, high)


def row_index(lanes):
    return lax.broadcasted_iota(jnp.int32, (8, lanes), 0)


def lane_edge(value, at_start):
    lanes = value.shape[1]
    lane = lax.broadcasted_iota(jnp.int32, (value.shape[0], 128), 1)
    if at_start:
        edge = pick(lane == 0, 0.0, value[:, :128])
        return edge if lanes == 128 else jnp.concatenate([edge, value[:, 128:]], axis=1)
    edge = pick(lane == 127, 0.0, value[:, lanes - 128 :])
    return edge if lanes == 128 else jnp.concatenate([value[:, : lanes - 128], edge], axis=1)


def neighbours(ref, colour, p, pairs, even):
    other = 1 - colour
    x = ref[other, p]
    if isinstance(p, int):
        below, above = ref[other, max(p - 1, 0)], ref[other, min(p + 1, pairs - 1)]
    else:
        below = ref[other, jnp.maximum(p - 1, 0)]
        above = ref[other, jnp.minimum(p + 1, pairs - 1)]
    far = pick(even, below, above) if colour == 0 else pick(even, above, below)
    rows, lanes = x.shape
    return (
        x,
        far,
        pltpu.roll(x, 1, 0),
        pltpu.roll(x, rows - 1, 0),
        pltpu.roll(x, 1, 1),
        pltpu.roll(x, lanes - 1, 1),
    )


def span(own, layers):
    extra = (layers + 1) // 2
    return range(HP - extra, HP + own + extra)


class Store:
    def __init__(self, ref, start=0, early=None, held=()):
        self.ref, self.start = ref, start
        self.early = {key: early for key in held}

    def place(self, at):
        first, p, *rest = at
        early = self.early.get((first, p))
        if early is not None:
            return early.ref, (first, p - early.start, *rest)
        return self.ref, (first, p - self.start, *rest)

    def __getitem__(self, at):
        ref, at = self.place(at)
        return ref[at]

    def __setitem__(self, at, value):
        self.early.pop((at[0], at[1]), None)
        ref, at = self.place(at)
        ref[at] = value


class Level:
    def __init__(self, K, S, U, W, D, own, shape):
        self.K, self.S, self.U, self.W, self.D, self.own = K, S, U, W, D, own
        self.pairs = own + 2 * HP
        self.rows, self.lanes = shape
        self.even = even_mask(self.rows, self.lanes)

    def setup(self, colour, pairs, inverse_out=None):
        for p in pairs:
            near = list(neighbours(self.K, colour, p, self.pairs, self.even))
            near[4] = lane_edge(near[4], True)
            near[5] = lane_edge(near[5], False)
            centre = self.K[colour, p]
            total = near[0]
            for value in near[1:]:
                total = total + value
            diag = 3.0 * centre + 0.5 * total
            inverse = pick(centre > 0.0, 1.0 / diag, 0.0)
            half = 0.5 * inverse
            for i, value in enumerate(near):
                weight = (centre + value) * half
                if i == 4:
                    weight = lane_edge(weight, True)
                if i == 5:
                    weight = lane_edge(weight, False)
                self.W[colour * 6 + i, p] = weight
            self.D[colour, p] = diag
            if inverse_out is not None:
                inverse_out[colour, p] = inverse
            else:
                self.begin(colour, p, inverse)

    def begin(self, colour, p, inverse):
        start = self.S[colour, p] * inverse
        self.S[colour, p] = start
        if colour == 0:
            self.U[0, p] = start

    def clear(self, colour, pairs):
        zero = jnp.zeros((self.rows, self.lanes), F32)
        for p in range(self.pairs):
            if p not in pairs:
                self.U[colour, p] = zero

    def relaxed(self, colour, p):
        near = neighbours(self.U, colour, p, self.pairs, self.even)
        total = self.S[colour, p]
        for i, value in enumerate(near):
            total = total + self.W[colour * 6 + i, p] * value
        return total

    def sweep(self, colour, pairs):
        for p in pairs:
            self.U[colour, p] = self.relaxed(colour, p)

    def residual(self, R, pairs, pad, inset):
        for i, p in enumerate(pairs):
            for colour in (0, 1):
                rest = self.D[colour, p] * (self.relaxed(colour, p) - self.U[colour, p])
                R[colour, i + pad] = rest[inset : self.rows - inset]

    def all_setup(self, depth, inverse_out=None):
        for colour in (0, 1):
            self.setup(colour, span(self.own, depth - colour), inverse_out)

    def all_clear(self, depth):
        for colour in (0, 1):
            self.clear(colour, span(self.own, depth - colour))

    def all_sweeps(self, depth):
        for i, colour in enumerate((1, 0, 1)):
            self.sweep(colour, span(self.own, depth - 1 - i))


def without(pairs, inner):
    return [p for p in pairs if p not in inner]


def inner_span(own, margin):
    return range(HP + margin, HP + own - margin)


def store_field(U, out, own, even, wide):
    rows = out.shape[1]
    first = (wide - rows) // 2
    for p in range(own):
        red = U[0, HP + p, first : first + rows]
        black = U[1, HP + p, first : first + rows]
        out[2 * p] = pick(even, red, black)
        out[2 * p + 1] = pick(even, black, red)


def restrict_planes(R, at, even):
    red, black = R[0, at], R[1, at]
    odd_below = pick(even, R[1, at - 1], R[0, at - 1])
    even_above = pick(even, R[0, at + 1], R[1, at + 1])
    return (3.0 * (red + black) + (odd_below + even_above)) * 0.125


def row_restriction(rows, ends):
    half = rows // 2
    shape = (half + 8 if ends else half, rows)
    j = lax.broadcasted_iota(jnp.int32, shape, 0)
    m = lax.broadcasted_iota(jnp.int32, shape, 1)
    inner = (m == 2 * j) | (m == 2 * j + 1)
    outer = (m == 2 * j - 1) | (m == 2 * j + 2)
    main = pick(inner, 0.375, pick(outer, 0.125, 0.0)).astype(F32)
    if not ends:
        return main.astype(jnp.bfloat16)
    edge = pick(((j == half) & (m == 0)) | ((j == half + 1) & (m == rows - 1)), 0.125, 0.0)
    return pick(j < half, main, edge).astype(F32).astype(jnp.bfloat16)


def row_sum(rows):
    j = 2 * lax.broadcasted_iota(jnp.int32, (rows // 2, rows), 0)
    m = lax.broadcasted_iota(jnp.int32, (rows // 2, rows), 1)
    return pick((m == j) | (m == j + 1), 1.0, 0.0).astype(F32).astype(jnp.bfloat16)


def split(x):
    parts = []
    for _ in range(3):
        part = x.astype(jnp.bfloat16)
        parts.append(part)
        x = x - part.astype(F32)
    return parts


def product(a, b):
    if a.dtype == jnp.bfloat16:
        parts = [jnp.dot(a, part, preferred_element_type=F32) for part in split(b)]
    else:
        parts = [jnp.dot(part, b, preferred_element_type=F32) for part in split(a)]
    return (parts[2] + parts[1]) + parts[0]


def lane_restriction(lanes):
    m = lax.broadcasted_iota(jnp.int32, (lanes, lanes // 2), 0)
    i = 2 * lax.broadcasted_iota(jnp.int32, (lanes, lanes // 2), 1)
    inner = (m == i) | (m == i + 1)
    outer = (m == i - 1) | (m == i + 2)
    return pick(inner, 1.5, pick(outer, 0.5, 0.0)).astype(F32).astype(jnp.bfloat16)


def lane_mean(lanes):
    m = lax.broadcasted_iota(jnp.int32, (lanes, lanes // 2), 0)
    i = 2 * lax.broadcasted_iota(jnp.int32, (lanes, lanes // 2), 1)
    return pick((m == i) | (m == i + 1), 0.125, 0.0).astype(F32).astype(jnp.bfloat16)


def pack_rows_kernel(s_low, s_high, k_low, k_high, end_a, end_b, inner_a, inner_b):
    planes, _, lanes = s_low.shape
    own = planes // 2
    even = even_mask(8, lanes)
    ends, inner = Send(end_a, end_b, "inner"), Send(inner_a, inner_b, "inner")
    cat = lambda *parts: jnp.concatenate(parts, axis=0)

    for p in range(own):
        def pair(ref):
            a, b = ref[2 * p], ref[2 * p + 1]
            return pick(even, a, b), pick(even, b, a)

        ls, lk, hs, hk = pair(s_low), pair(k_low), pair(s_high), pair(k_high)
        send, at = (inner, p - 2) if 2 <= p < own - 2 else (ends, p if p < 2 else p - own + 4)
        send.put((0, at), cat(lk[0][0:4], ls[0][0:4]), cat(hk[0][4:8], hs[0][4:8]))
        send.put((1, at), cat(lk[1][0:5], ls[1][0:3]), cat(hk[1][3:8], hs[1][5:8]))


def rows_from(got, p, own):
    ends, inner = got
    if 2 <= p < own - 2:
        return inner[0, p - 2], inner[1, p - 2]
    at = p if p < 2 else p - own + 4
    return ends[0, at], ends[1, at]


def between(row, first, last):
    return (row >= first) & (row <= last)


def pack_planes_kernel(s, k, from_a, from_b, to_a, to_b):
    planes, rows, lanes = s.shape
    own = planes // 2
    even = even_mask(8, lanes)
    even_own = even_mask(rows, lanes)
    row = row_index(lanes)
    low, high = got_pair(from_a, from_b, "inner")
    send = Send(to_a, to_b, "outer")

    def edges(plane, of_k):
        lr, lb = rows_from((low, None), plane // 2, own)
        hr, hb = rows_from((high, None), plane // 2, own)
        if of_k:
            red = jnp.concatenate([lr[0:4], hr[0:4]], axis=0)
            black = jnp.concatenate([lb[1:5], hb[0:4]], axis=0)
        else:
            red = jnp.concatenate([lr[4:8], hr[4:8]], axis=0)
            black = jnp.concatenate([lb[4:8], hb[5:8], hb[7:8]], axis=0)
        return (pick(even, red, black), pick(even, black, red))[plane % 2]

    def corners(plane):
        tiles = []
        for d in (1, 2, 3):
            source = edges(plane(d), False)
            mean = pltpu.roll(edges(plane(5 - d), True), 4, 0)
            tiles.append(pick(between(row, d, 7 - d), source, mean))
        return tiles + [edges(plane(1), True)]

    for j in range(3):
        send.put(j, s[j], s[planes - 3 + j])
    for j in range(4):
        send.put(3 + j, k[j], k[planes - 4 + j])
    send.put(7, pick(even_own, pltpu.roll(k[4], 1, 1), s[3]),
             pick(even_own, s[planes - 4], pltpu.roll(k[planes - 5], 1, 1)))
    down, up = corners(lambda d: d - 1), corners(lambda d: planes - d)
    for i in range(4):
        send.put((8, slice(8 * i, 8 * i + 8)), down[i], up[i])


def mean_kernel(k, out, Z):
    planes, rows, lanes = k.shape
    half = rows // 2
    for q in range(planes // 2):
        Z[half * q : half * (q + 1)] = product(row_sum(rows), k[2 * q] + k[2 * q + 1])
    mean = product(Z[...], lane_mean(lanes))
    for q in range(planes // 2):
        out[q] = mean[half * q : half * (q + 1)]


def fine_prepare_kernel(s, k, end_a, end_b, inner_a, inner_b, *arrays):
    planes, rows, lanes = s.shape
    own = planes // 2
    wide = rows + 16
    from_low, from_high = zip(got_pair(end_a, end_b, "inner"), got_pair(inner_a, inner_b, "inner"))
    even_own = even_mask(rows, lanes)
    row = row_index(lanes)
    K, S, U, W, D = [Store(ref, HP) for ref in arrays]

    def fill(p):
        at = HP + p
        lr, lb = rows_from(from_low, p, own)
        hr, hb = rows_from(from_high, p, own)
        K[0, at, 0:8] = pick(row >= 4, pltpu.roll(lr, 4, 0), 0.0)
        K[1, at, 0:8] = pick(row >= 3, pltpu.roll(lb, 3, 0), 0.0)
        S[0, at, 0:8] = pick(row >= 4, lr, 0.0)
        S[1, at, 0:8] = pick(row >= 5, lb, 0.0)
        K[0, at, 8 + rows : wide] = pick(row < 4, hr, 0.0)
        K[1, at, 8 + rows : wide] = pick(row < 5, hb, 0.0)
        S[0, at, 8 + rows : wide] = pick(row < 4, pltpu.roll(hr, 4, 0), 0.0)
        S[1, at, 8 + rows : wide] = pick(row < 3, pltpu.roll(hb, 3, 0), 0.0)
        for ref, to in ((s, S), (k, K)):
            a, b = ref[2 * p], ref[2 * p + 1]
            to[0, at, 8 : 8 + rows] = pick(even_own, a, b)
            to[1, at, 8 : 8 + rows] = pick(even_own, b, a)

    for p in range(own):
        fill(p)
    level = Level(K, S, U, W, D, own, (wide, lanes))
    level.setup(0, inner_span(own, 1))
    level.setup(1, inner_span(own, 1))
    level.sweep(1, inner_span(own, 2))
    level.sweep(0, inner_span(own, 3))


def fine_kernel(plane_a, plane_b, K0, S0, U0, W0, D0,
                field, source_out, to_a, to_b, K1, S1, U1, W1, D1, R, Z):
    from_down, from_up = got_pair(plane_a, plane_b, "outer")
    send = Send(to_a, to_b, "inner")
    planes, rows, lanes = field.shape
    own = planes // 2
    wide = rows + 16
    even = even_mask(wide, lanes)
    even_own = even_mask(rows, lanes)
    row = row_index(lanes)
    def store(ref, early, firsts, pairs):
        return Store(ref, 0, Store(early, HP), [(i, p) for i in firsts for p in pairs])

    inside = inner_span(own, 1)
    K = store(K1, K0, (0, 1), inner_span(own, 0))
    S = store(S1, S0, (0, 1), inner_span(own, 0))
    W = store(W1, W0, range(12), inside)
    D = store(D1, D0, (0, 1), inside)
    U = store(U1, U0, (0,), inside)
    U.early.update({(1, p): Store(U0, HP) for p in inner_span(own, 2)})

    def framed(low_edge, middle, high_edge):
        return jnp.concatenate(
            [pick(row >= 4, low_edge, 0.0), middle, pick(row < 4, high_edge, 0.0)], axis=0)

    def source_at(got, d, up):
        if d == 4:
            mixed = got[7]
            middle = pick(even_own, 0.0, mixed) if up else pick(even_own, mixed, 0.0)
            edge = jnp.zeros((8, lanes), F32)
        else:
            middle = got[d - 1 if up else 3 - d]
            edge = pick(between(row, d, 7 - d), got[8, 8 * d - 8 : 8 * d], 0.0)
            edge = pltpu.roll(edge, 4, 0)
        return framed(edge, middle, edge)

    def mean_at(got, d, up):
        edge = jnp.zeros((8, lanes), F32)
        if d == 6:
            return jnp.zeros((wide, lanes), F32)
        if d == 5:
            mixed = pltpu.roll(got[7], lanes - 1, 1)
            middle = pick(even_own, 0.0, mixed) if up else pick(even_own, mixed, 0.0)
        else:
            middle = got[2 + d if up else 7 - d]
            if d == 1:
                edge = pltpu.roll(got[8, 24:32], 4, 0)
            else:
                edge = pick(between(row, 5 - d, 2 + d), 0.0, got[8, 8 * (4 - d) : 8 * (5 - d)])
        return framed(edge, middle, edge)

    for j in range(HP):
        for to, plane in ((K, mean_at), (S, source_at)):
            if to is S and j == 2:
                continue
            near, far = 2 * j + 1, 2 * j + 2
            a, b = plane(from_up, near, True), plane(from_up, far, True)
            to[0, HP + own + j] = pick(even, a, b)
            to[1, HP + own + j] = pick(even, b, a)
            a, b = plane(from_down, far, False), plane(from_down, near, False)
            to[0, HP - 1 - j] = pick(even, a, b)
            to[1, HP - 1 - j] = pick(even, b, a)
    level = Level(K, S, U, W, D, own, (wide, lanes))
    for colour in (0, 1):
        level.setup(colour, without(span(own, 4 - colour), inner_span(own, 1)))
    level.all_clear(4)
    level.sweep(1, without(span(own, 3), inner_span(own, 2)))
    level.sweep(0, without(span(own, 2), inner_span(own, 3)))
    level.sweep(1, span(own, 1))
    level.residual(R, span(own, 0), 2, 8)
    store_field(U, field, own, even_own, wide)
    zero = jnp.zeros((rows, lanes), F32)
    for colour in (0, 1):
        for at in (0, 1, own + 2, own + 3):
            R[colour, at] = zero
    half = rows // 2
    block = half + 8
    for q in range(own + 2):
        Z[block * q : block * (q + 1)] = product(
            row_restriction(rows, True), restrict_planes(R, q + 1, even_own))
    source = product(Z[...], lane_restriction(lanes))
    row = lax.broadcasted_iota(jnp.int32, (half, lanes // 2), 0)
    for q in range(own + 2):
        at = block * q
        rows_of = source[at : at + half]
        source_out[q] = rows_of
        send.put(q, pick(row == half - 1, source[at + half : at + half + 1], rows_of),
                 pick(row == 0, source[at + half + 1 : at + half + 2], rows_of))


def widen_planes(K, send, planes, of):
    for q in range(planes):
        K[q] = of(q)
    for j in range(6):
        send.put(j, K[j], K[planes - 6 + j])


def mean_planes_kernel(own_rows, from_a, from_b, K, to_a, to_b):
    from_low, from_high = got_pair(from_a, from_b, "inner")

    def of(q):
        return jnp.concatenate([from_low[q], own_rows[q], from_high[q]], axis=0)

    widen_planes(K, Send(to_a, to_b, "outer"), own_rows.shape[0], of)


def middle_setup_kernel(k, from_a, from_b, K, W, D, I):
    from_down, from_up = got_pair(from_a, from_b, "outer")
    _, pairs, wide, lanes = K.shape
    planes = k.shape[0]
    even = even_mask(wide, lanes)

    def plane(i):
        if i < 0:
            return from_down[6 + i]
        return k[i] if i < planes else from_up[i - planes]

    for p in range(pairs):
        a, b = plane(2 * (p - HP)), plane(2 * (p - HP) + 1)
        K[0, p] = pick(even, a, b)
        K[1, p] = pick(even, b, a)
    Level(K, None, None, W, D, pairs - 2 * HP, (wide, lanes)).all_setup(5, I)


def source_planes_kernel(own_rows, sent_a, sent_b, from_a, from_b, S, to_a, to_b):
    planes, rows, lanes = own_rows.shape
    row = lax.broadcasted_iota(jnp.int32, (rows, lanes), 0)
    first, last = row == 0, row == rows - 1
    to_low, to_high = got_pair(sent_a, sent_b, "inner")
    from_low, from_high = got_pair(from_a, from_b, "inner")

    def of(q):
        got_low, got_high = from_low[q], from_high[q]
        low = pick(first, 0.0, got_low) + pick(last, to_low[q], 0.0)
        mine = own_rows[q] + pick(first, got_low, 0.0) + pick(last, got_high, 0.0)
        high = pick(last, 0.0, got_high) + pick(first, to_high[q], 0.0)
        return jnp.concatenate([low, mine, high], axis=0)

    widen_planes(S, Send(to_a, to_b, "outer"), planes, of)


def middle_kernel(s, source_a, source_b, K, W, D, I,
                  field, s_next, k_next, to_a, to_b,
                  S, U, R, Z, Zk):
    from_down, from_up = got_pair(source_a, source_b, "outer")
    send = Send(to_a, to_b, "outer")
    planes = field.shape[0]
    _, pairs, wide, lanes = K.shape
    own = planes // 2
    even = even_mask(wide, lanes)
    zero = jnp.zeros((wide, lanes), F32)

    def source_plane(i):
        if i < -5 or i > planes + 4:
            return zero
        if i < -1:
            return from_down[i + 5]
        if i == -1:
            return from_down[4] + s[0]
        if i == 0:
            return s[1] + from_down[5]
        if i < planes - 1:
            return s[i + 1]
        if i == planes - 1:
            return s[planes] + from_up[0]
        if i == planes:
            return from_up[1] + s[planes + 1]
        return from_up[i - planes + 1]

    level = Level(K, S, U, W, D, own, (wide, lanes))
    for p in range(-HP, own + HP):
        a, b = source_plane(2 * p), source_plane(2 * p + 1)
        S[0, HP + p] = pick(even, a, b)
        S[1, HP + p] = pick(even, b, a)
    for colour in (0, 1):
        for p in span(own, 5 - colour):
            level.begin(colour, p, I[colour, p])
    level.all_clear(5)
    level.all_sweeps(5)
    level.residual(R, span(own, 1), 0, 0)
    rows = field.shape[1]
    store_field(U, field, own, even_mask(rows, lanes), wide)
    half = wide // 2
    for q in range(own):
        Z[half * q : half * (q + 1)] = product(
            row_restriction(wide, False), restrict_planes(R, q + 1, even))
    for q in range(own + 2):
        total = K[0, HP - 1 + q] + K[1, HP - 1 + q]
        Zk[half * q : half * (q + 1)] = product(row_sum(wide), total)
    source = product(Z[...], lane_restriction(lanes))
    mean = product(Zk[...], lane_mean(lanes))
    for q in range(own):
        s_next[q] = source[half * q : half * (q + 1)]
        k_next[q] = mean[half * (q + 1) : half * (q + 2)]
    for j in range(4):
        send.put(j, s_next[j], s_next[own - 4 + j])
    for j in range(5):
        send.put(4 + j, mean[half * (1 + j) : half * (2 + j)],
                 mean[half * (own - 4 + j) : half * (own - 3 + j)])


def coarse_kernel(s, k, from_a, from_b, field, rest, K, S, U, W, D, R):
    from_down, from_up = got_pair(from_a, from_b, "outer")
    planes, wide, lanes = k.shape
    own = planes // 2
    rows = field.shape[1]
    even = even_mask(wide, lanes)
    even_own = even_mask(rows, lanes)
    zero = jnp.zeros((wide, lanes), F32)

    def source_plane(i):
        if i < -4 or i > planes + 3:
            return zero
        if i < 0:
            return from_down[4 + i]
        return s[i] if i < planes else from_up[i - planes]

    def mean_plane(i):
        if i < -5 or i > planes + 4:
            return zero
        if i < 0:
            return from_down[9 + i]
        return k[i] if i < planes else from_up[4 + i - planes]

    for p in range(-HP, own + HP):
        for to, plane in ((S, source_plane), (K, mean_plane)):
            a, b = plane(2 * p), plane(2 * p + 1)
            to[0, HP + p] = pick(even, a, b)
            to[1, HP + p] = pick(even, b, a)
    level = Level(K, S, U, W, D, own, (wide, lanes))
    level.all_setup(4)
    level.all_clear(4)
    level.all_sweeps(4)
    level.residual(R, span(own, 0), 2, (wide - rows) // 2)
    store_field(U, field, own, even_own, wide)
    for p in range(own):
        red, black = R[0, p + 2], R[1, p + 2]
        rest[2 * p] = pick(even_own, red, black)
        rest[2 * p + 1] = pick(even_own, black, red)


def limit(scratch):
    words = 0
    for shape in scratch:
        size = 1
        for n in shape:
            size *= n
        words += size
    return 4 * words + (12 << 20)


def call(kernel, outs, scratch, *args, in_specs=None, name=None, results=False):
    extra = {}
    if in_specs is None:
        args = [pltpu.with_memory_space_constraint(a, pltpu.VMEM) for a in args]
    else:
        args = [pltpu.with_memory_space_constraint(a, pltpu.HBM) for a in args]
        extra = {"in_specs": in_specs, "grid": (1,)}
        extra["out_specs"] = [pl.BlockSpec(memory_space=pltpu.VMEM) for _ in outs]
    if results:
        extra = {"out_specs": [pl.BlockSpec(memory_space=pltpu.VMEM) for _ in outs]}
    return pl.pallas_call(
        kernel,
        out_shape=[jax.ShapeDtypeStruct(o, F32) if results else pltpu.VMEM(o, F32) for o in outs],
        scratch_shapes=[pltpu.VMEM(shape, F32) for shape in scratch],
        compiler_params=pltpu.CompilerParams(vmem_limit_bytes=limit(scratch)),
        name=name,
        **extra,
    )(*args)


def level_arrays(own, wide, lanes):
    block = (2, own + 2 * HP, wide, lanes)
    return [block, block, block, (12, *block[1:]), block]


def exchange(a, b, axis):
    size = lax.axis_size(axis)

    def swapped(x, first):
        pairs = [(i, i + 1) for i in range(first, size - 1, 2)]
        return lax.ppermute(x, axis, pairs + [(j, i) for i, j in pairs])

    return swapped(a, 1), swapped(b, 0)


def body(right_side, coefficient):
    s, k = right_side, coefficient
    planes, rows, lanes = s.shape
    own = planes // 2
    wide = rows + 16

    low = pl.BlockSpec((planes, 8, lanes), lambda i: (0, 0, 0))
    high = pl.BlockSpec((planes, 8, lanes), lambda i: (0, rows // 8 - 1, 0))
    ends, inner = (2, 4, 8, lanes), (2, own - 4, 8, lanes)
    end_a, end_b, inner_a, inner_b = call(
        pack_rows_kernel, [ends, ends, inner, inner], [], s, s, k, k,
        in_specs=[low, high, low, high], name="pack_rows")
    end_halo = exchange(end_a, end_b, "inner")
    inner_halo = exchange(inner_a, inner_b, "inner")
    half, next_lanes = rows // 2, lanes // 2
    (mean,) = call(mean_kernel, [(own, half, next_lanes)], [(half * own, lanes)], k, name="mean")
    message = (9, rows, lanes)
    to_a, to_b = call(pack_planes_kernel, [message] * 2, [], s, k, *end_halo, name="pack_planes")
    mean, to_a, to_b = lax.optimization_barrier((mean, to_a, to_b))
    plane_halo = exchange(to_a, to_b, "outer")
    arrays = level_arrays(own, wide, lanes)
    early = [(a[0], own, wide, lanes) for a in arrays]
    prepared = call(fine_prepare_kernel, early, [], s, k, *end_halo, *inner_halo,
                    name="fine_prepare")
    mean_halo = exchange(mean, mean, "inner")

    count = own + 2
    message = (count, half, next_lanes)
    field0, source, to_a, to_b = call(
        fine_kernel, [s.shape, message, message, message],
        [*arrays, (2, own + 4, rows, lanes), ((half + 8) * count, lanes)],
        *plane_halo, *prepared, name="fine_level")

    planes, rows, lanes = own, half, next_lanes
    own, wide = planes // 2, 3 * rows
    *mean_halo, to_a, to_b = lax.optimization_barrier((*mean_halo, to_a, to_b))
    row_halo = exchange(to_a, to_b, "inner")
    message = (6, wide, lanes)
    k1, *sent = call(
        mean_planes_kernel, [(planes, wide, lanes), message, message], [],
        mean, *mean_halo, name="mean_planes")
    mean_halo = exchange(*sent, "outer")
    K, S, U, W, D = level_arrays(own, wide, lanes)
    constants = call(middle_setup_kernel, [K, W, D, K], [], k1, *mean_halo, name="middle_setup")
    message = (6, wide, lanes)
    s1, *sent = call(
        source_planes_kernel, [(planes + 2, wide, lanes), message, message], [],
        source, to_a, to_b, *row_halo, name="source_planes")
    source_halo = exchange(*sent, "outer")
    half, next_lanes = wide // 2, lanes // 2
    block, message = (own, half, next_lanes), (9, half, next_lanes)
    field1, s2, k2, *sent = call(
        middle_kernel, [(planes, rows, lanes), block, block, message, message],
        [S, U, (2, own + 2, wide, lanes), (half * own, lanes), (half * (own + 2), lanes)],
        s1, *source_halo, *constants, name="middle_level")

    planes, rows, wide, lanes = own, rows // 2, half, next_lanes
    own = planes // 2
    field2, rest = call(
        coarse_kernel, [(planes, rows, lanes)] * 2,
        [*level_arrays(own, wide, lanes), (2, own + 4, rows, lanes)],
        s2, k2, *exchange(*sent, "outer"), name="coarse_level", results=True)
    return field0, field1, field2, rest


def solution(mesh):
    spec = P("outer", "inner", None)
    return jax.shard_map(body, mesh=mesh, in_specs=(spec, spec), out_specs=(spec,) * 4, check_vma=False)
```

```python
import jax
import jax.numpy as jnp
from jax import lax
from jax.experimental import pallas as pl
from jax.experimental.pallas import tpu as pltpu
from jax.sharding import PartitionSpec as P

F32 = jnp.float32
HP = 3


def tiled(tile, rows, lanes):
    wide = jnp.concatenate([tile] * (lanes // 128), axis=1)
    return jnp.concatenate([wide] * (rows // 8), axis=0)


def even_mask(rows, lanes):
    row = lax.broadcasted_iota(jnp.int32, (8, 128), 0)
    lane = lax.broadcasted_iota(jnp.int32, (8, 128), 1)
    return tiled((row + lane) & 1, rows, lanes) == 0


def pick(mask, a, b):
    return jnp.where(mask, a, b)


def odd_on(axis):
    return lax.axis_index(axis) % 2 == 1


def choose(odd, a, b):
    return lax.select(jnp.full(a.shape, odd), a, b)


class Got:
    def __init__(self, a, b, odd, upper):
        self.first, self.second = (a, b) if upper else (b, a)
        self.odd = odd
        self.shape = a.shape

    def __getitem__(self, at):
        return choose(self.odd, self.first[at], self.second[at])


def got_pair(a, b, axis):
    odd = odd_on(axis)
    return Got(a, b, odd, False), Got(a, b, odd, True)


class Send:
    def __init__(self, a, b, axis):
        self.a, self.b, self.odd = a, b, odd_on(axis)

    def put(self, at, low, high):
        self.a[at] = choose(self.odd, high, low)
        self.b[at] = choose(self.odd, low, high)


def row_index(lanes):
    return lax.broadcasted_iota(jnp.int32, (8, lanes), 0)


def lane_edge(value, at_start):
    lanes = value.shape[1]
    lane = lax.broadcasted_iota(jnp.int32, (value.shape[0], 128), 1)
    if at_start:
        edge = pick(lane == 0, 0.0, value[:, :128])
        return edge if lanes == 128 else jnp.concatenate([edge, value[:, 128:]], axis=1)
    edge = pick(lane == 127, 0.0, value[:, lanes - 128 :])
    return edge if lanes == 128 else jnp.concatenate([value[:, : lanes - 128], edge], axis=1)


def neighbours(ref, colour, p, pairs, even):
    other = 1 - colour
    x = ref[other, p]
    if isinstance(p, int):
        below, above = ref[other, max(p - 1, 0)], ref[other, min(p + 1, pairs - 1)]
    else:
        below = ref[other, jnp.maximum(p - 1, 0)]
        above = ref[other, jnp.minimum(p + 1, pairs - 1)]
    far = pick(even, below, above) if colour == 0 else pick(even, above, below)
    rows, lanes = x.shape
    return (
        x,
        far,
        pltpu.roll(x, 1, 0),
        pltpu.roll(x, rows - 1, 0),
        pltpu.roll(x, 1, 1),
        pltpu.roll(x, lanes - 1, 1),
    )


def span(own, layers):
    extra = (layers + 1) // 2
    return range(HP - extra, HP + own + extra)


class Store:
    def __init__(self, ref, start=0, early=None, held=()):
        self.ref, self.start = ref, start
        self.early = {key: early for key in held}

    def place(self, at):
        first, p, *rest = at
        early = self.early.get((first, p))
        if early is not None:
            return early.ref, (first, p - early.start, *rest)
        return self.ref, (first, p - self.start, *rest)

    def __getitem__(self, at):
        ref, at = self.place(at)
        return ref[at]

    def __setitem__(self, at, value):
        self.early.pop((at[0], at[1]), None)
        ref, at = self.place(at)
        ref[at] = value


class Level:
    def __init__(self, K, S, U, W, D, own, shape):
        self.K, self.S, self.U, self.W, self.D, self.own = K, S, U, W, D, own
        self.pairs = own + 2 * HP
        self.rows, self.lanes = shape
        self.even = even_mask(self.rows, self.lanes)

    def setup(self, colour, pairs, inverse_out=None):
        for p in pairs:
            near = list(neighbours(self.K, colour, p, self.pairs, self.even))
            near[4] = lane_edge(near[4], True)
            near[5] = lane_edge(near[5], False)
            centre = self.K[colour, p]
            total = near[0]
            for value in near[1:]:
                total = total + value
            diag = 3.0 * centre + 0.5 * total
            inverse = pick(centre > 0.0, 1.0 / diag, 0.0)
            half = 0.5 * inverse
            for i, value in enumerate(near):
                weight = (centre + value) * half
                if i == 4:
                    weight = lane_edge(weight, True)
                if i == 5:
                    weight = lane_edge(weight, False)
                self.W[colour * 6 + i, p] = weight
            self.D[colour, p] = diag
            if inverse_out is not None:
                inverse_out[colour, p] = inverse
            else:
                self.begin(colour, p, inverse)

    def begin(self, colour, p, inverse):
        start = self.S[colour, p] * inverse
        self.S[colour, p] = start
        if colour == 0:
            self.U[0, p] = start

    def clear(self, colour, pairs):
        zero = jnp.zeros((self.rows, self.lanes), F32)
        for p in range(self.pairs):
            if p not in pairs:
                self.U[colour, p] = zero

    def relaxed(self, colour, p):
        near = neighbours(self.U, colour, p, self.pairs, self.even)
        total = self.S[colour, p]
        for i, value in enumerate(near):
            total = total + self.W[colour * 6 + i, p] * value
        return total

    def sweep(self, colour, pairs):
        for p in pairs:
            self.U[colour, p] = self.relaxed(colour, p)

    def residual(self, R, pairs, pad, inset):
        for i, p in enumerate(pairs):
            for colour in (0, 1):
                rest = self.D[colour, p] * (self.relaxed(colour, p) - self.U[colour, p])
                R[colour, i + pad] = rest[inset : self.rows - inset]

    def all_setup(self, depth, inverse_out=None):
        for colour in (0, 1):
            self.setup(colour, span(self.own, depth - colour), inverse_out)

    def all_clear(self, depth):
        for colour in (0, 1):
            self.clear(colour, span(self.own, depth - colour))

    def all_sweeps(self, depth):
        for i, colour in enumerate((1, 0, 1)):
            self.sweep(colour, span(self.own, depth - 1 - i))


def without(pairs, inner):
    return [p for p in pairs if p not in inner]


def inner_span(own, margin):
    return range(HP + margin, HP + own - margin)


def store_field(U, out, own, even, wide):
    rows = out.shape[1]
    first = (wide - rows) // 2
    for p in range(own):
        red = U[0, HP + p, first : first + rows]
        black = U[1, HP + p, first : first + rows]
        out[2 * p] = pick(even, red, black)
        out[2 * p + 1] = pick(even, black, red)


def restrict_planes(R, at, even):
    red, black = R[0, at], R[1, at]
    odd_below = pick(even, R[1, at - 1], R[0, at - 1])
    even_above = pick(even, R[0, at + 1], R[1, at + 1])
    return (3.0 * (red + black) + (odd_below + even_above)) * 0.125


def row_restriction(rows, ends):
    half = rows // 2
    shape = (half + 8 if ends else half, rows)
    j = lax.broadcasted_iota(jnp.int32, shape, 0)
    m = lax.broadcasted_iota(jnp.int32, shape, 1)
    inner = (m == 2 * j) | (m == 2 * j + 1)
    outer = (m == 2 * j - 1) | (m == 2 * j + 2)
    main = pick(inner, 0.375, pick(outer, 0.125, 0.0)).astype(F32)
    if not ends:
        return main.astype(jnp.bfloat16)
    edge = pick(((j == half) & (m == 0)) | ((j == half + 1) & (m == rows - 1)), 0.125, 0.0)
    return pick(j < half, main, edge).astype(F32).astype(jnp.bfloat16)


def row_sum(rows):
    j = 2 * lax.broadcasted_iota(jnp.int32, (rows // 2, rows), 0)
    m = lax.broadcasted_iota(jnp.int32, (rows // 2, rows), 1)
    return pick((m == j) | (m == j + 1), 1.0, 0.0).astype(F32).astype(jnp.bfloat16)


def split(x):
    parts = []
    for _ in range(3):
        part = x.astype(jnp.bfloat16)
        parts.append(part)
        x = x - part.astype(F32)
    return parts


def product(a, b):
    if a.dtype == jnp.bfloat16:
        parts = [jnp.dot(a, part, preferred_element_type=F32) for part in split(b)]
    else:
        parts = [jnp.dot(part, b, preferred_element_type=F32) for part in split(a)]
    return (parts[2] + parts[1]) + parts[0]


def lane_restriction(lanes):
    m = lax.broadcasted_iota(jnp.int32, (lanes, lanes // 2), 0)
    i = 2 * lax.broadcasted_iota(jnp.int32, (lanes, lanes // 2), 1)
    inner = (m == i) | (m == i + 1)
    outer = (m == i - 1) | (m == i + 2)
    return pick(inner, 1.5, pick(outer, 0.5, 0.0)).astype(F32).astype(jnp.bfloat16)


def lane_mean(lanes):
    m = lax.broadcasted_iota(jnp.int32, (lanes, lanes // 2), 0)
    i = 2 * lax.broadcasted_iota(jnp.int32, (lanes, lanes // 2), 1)
    return pick((m == i) | (m == i + 1), 0.125, 0.0).astype(F32).astype(jnp.bfloat16)


def pack_rows_kernel(s_low, s_high, k_low, k_high, end_a, end_b, inner_a, inner_b):
    planes, _, lanes = s_low.shape
    own = planes // 2
    even = even_mask(8, lanes)
    ends, inner = Send(end_a, end_b, "inner"), Send(inner_a, inner_b, "inner")
    cat = lambda *parts: jnp.concatenate(parts, axis=0)

    for p in range(own):
        def pair(ref):
            a, b = ref[2 * p], ref[2 * p + 1]
            return pick(even, a, b), pick(even, b, a)

        ls, lk, hs, hk = pair(s_low), pair(k_low), pair(s_high), pair(k_high)
        send, at = (inner, p - 2) if 2 <= p < own - 2 else (ends, p if p < 2 else p - own + 4)
        send.put((0, at), cat(lk[0][0:4], ls[0][0:4]), cat(hk[0][4:8], hs[0][4:8]))
        send.put((1, at), cat(lk[1][0:5], ls[1][0:3]), cat(hk[1][3:8], hs[1][5:8]))


def rows_from(got, p, own):
    ends, inner = got
    if 2 <= p < own - 2:
        return inner[0, p - 2], inner[1, p - 2]
    at = p if p < 2 else p - own + 4
    return ends[0, at], ends[1, at]


def between(row, first, last):
    return (row >= first) & (row <= last)


def pack_planes_kernel(s, k, from_a, from_b, to_a, to_b):
    planes, rows, lanes = s.shape
    own = planes // 2
    even = even_mask(8, lanes)
    even_own = even_mask(rows, lanes)
    row = row_index(lanes)
    low, high = got_pair(from_a, from_b, "inner")
    send = Send(to_a, to_b, "outer")

    def edges(plane, of_k):
        lr, lb = rows_from((low, None), plane // 2, own)
        hr, hb = rows_from((high, None), plane // 2, own)
        if of_k:
            red = jnp.concatenate([lr[0:4], hr[0:4]], axis=0)
            black = jnp.concatenate([lb[1:5], hb[0:4]], axis=0)
        else:
            red = jnp.concatenate([lr[4:8], hr[4:8]], axis=0)
            black = jnp.concatenate([lb[4:8], hb[5:8], hb[7:8]], axis=0)
        return (pick(even, red, black), pick(even, black, red))[plane % 2]

    def corners(plane):
        tiles = []
        for d in (1, 2, 3):
            source = edges(plane(d), False)
            mean = pltpu.roll(edges(plane(5 - d), True), 4, 0)
            tiles.append(pick(between(row, d, 7 - d), source, mean))
        return tiles + [edges(plane(1), True)]

    for j in range(3):
        send.put(j, s[j], s[planes - 3 + j])
    for j in range(4):
        send.put(3 + j, k[j], k[planes - 4 + j])
    send.put(7, pick(even_own, pltpu.roll(k[4], 1, 1), s[3]),
             pick(even_own, s[planes - 4], pltpu.roll(k[planes - 5], 1, 1)))
    down, up = corners(lambda d: d - 1), corners(lambda d: planes - d)
    for i in range(4):
        send.put((8, slice(8 * i, 8 * i + 8)), down[i], up[i])


def mean_kernel(k, out, Z):
    planes, rows, lanes = k.shape
    half = rows // 2
    for q in range(planes // 2):
        Z[half * q : half * (q + 1)] = product(row_sum(rows), k[2 * q] + k[2 * q + 1])
    mean = product(Z[...], lane_mean(lanes))
    for q in range(planes // 2):
        out[q] = mean[half * q : half * (q + 1)]


def fine_prepare_kernel(s, k, end_a, end_b, inner_a, inner_b, *arrays):
    planes, rows, lanes = s.shape
    own = planes // 2
    wide = rows + 16
    from_low, from_high = zip(got_pair(end_a, end_b, "inner"), got_pair(inner_a, inner_b, "inner"))
    even_own = even_mask(rows, lanes)
    row = row_index(lanes)
    K, S, U, W, D = [Store(ref, HP) for ref in arrays]

    def fill(p):
        at = HP + p
        lr, lb = rows_from(from_low, p, own)
        hr, hb = rows_from(from_high, p, own)
        K[0, at, 0:8] = pick(row >= 4, pltpu.roll(lr, 4, 0), 0.0)
        K[1, at, 0:8] = pick(row >= 3, pltpu.roll(lb, 3, 0), 0.0)
        S[0, at, 0:8] = pick(row >= 4, lr, 0.0)
        S[1, at, 0:8] = pick(row >= 5, lb, 0.0)
        K[0, at, 8 + rows : wide] = pick(row < 4, hr, 0.0)
        K[1, at, 8 + rows : wide] = pick(row < 5, hb, 0.0)
        S[0, at, 8 + rows : wide] = pick(row < 4, pltpu.roll(hr, 4, 0), 0.0)
        S[1, at, 8 + rows : wide] = pick(row < 3, pltpu.roll(hb, 3, 0), 0.0)
        for ref, to in ((s, S), (k, K)):
            a, b = ref[2 * p], ref[2 * p + 1]
            to[0, at, 8 : 8 + rows] = pick(even_own, a, b)
            to[1, at, 8 : 8 + rows] = pick(even_own, b, a)

    for p in range(own):
        fill(p)
    level = Level(K, S, U, W, D, own, (wide, lanes))
    level.setup(0, inner_span(own, 1))
    level.setup(1, inner_span(own, 1))
    level.sweep(1, inner_span(own, 2))
    level.sweep(0, inner_span(own, 3))


def fine_kernel(plane_a, plane_b, K0, S0, U0, W0, D0,
                field, source_out, to_a, to_b, K1, S1, U1, W1, D1, R, Z):
    from_down, from_up = got_pair(plane_a, plane_b, "outer")
    send = Send(to_a, to_b, "inner")
    planes, rows, lanes = field.shape
    own = planes // 2
    wide = rows + 16
    even = even_mask(wide, lanes)
    even_own = even_mask(rows, lanes)
    row = row_index(lanes)
    def store(ref, early, firsts, pairs):
        return Store(ref, 0, Store(early, HP), [(i, p) for i in firsts for p in pairs])

    inside = inner_span(own, 1)
    K = store(K1, K0, (0, 1), inner_span(own, 0))
    S = store(S1, S0, (0, 1), inner_span(own, 0))
    W = store(W1, W0, range(12), inside)
    D = store(D1, D0, (0, 1), inside)
    U = store(U1, U0, (0,), inside)
    U.early.update({(1, p): Store(U0, HP) for p in inner_span(own, 2)})

    def framed(low_edge, middle, high_edge):
        return jnp.concatenate(
            [pick(row >= 4, low_edge, 0.0), middle, pick(row < 4, high_edge, 0.0)], axis=0)

    def source_at(got, d, up):
        if d == 4:
            mixed = got[7]
            middle = pick(even_own, 0.0, mixed) if up else pick(even_own, mixed, 0.0)
            edge = jnp.zeros((8, lanes), F32)
        else:
            middle = got[d - 1 if up else 3 - d]
            edge = pick(between(row, d, 7 - d), got[8, 8 * d - 8 : 8 * d], 0.0)
            edge = pltpu.roll(edge, 4, 0)
        return framed(edge, middle, edge)

    def mean_at(got, d, up):
        edge = jnp.zeros((8, lanes), F32)
        if d == 6:
            return jnp.zeros((wide, lanes), F32)
        if d == 5:
            mixed = pltpu.roll(got[7], lanes - 1, 1)
            middle = pick(even_own, 0.0, mixed) if up else pick(even_own, mixed, 0.0)
        else:
            middle = got[2 + d if up else 7 - d]
            if d == 1:
                edge = pltpu.roll(got[8, 24:32], 4, 0)
            else:
                edge = pick(between(row, 5 - d, 2 + d), 0.0, got[8, 8 * (4 - d) : 8 * (5 - d)])
        return framed(edge, middle, edge)

    for j in range(HP):
        for to, plane in ((K, mean_at), (S, source_at)):
            if to is S and j == 2:
                continue
            near, far = 2 * j + 1, 2 * j + 2
            a, b = plane(from_up, near, True), plane(from_up, far, True)
            to[0, HP + own + j] = pick(even, a, b)
            to[1, HP + own + j] = pick(even, b, a)
            a, b = plane(from_down, far, False), plane(from_down, near, False)
            to[0, HP - 1 - j] = pick(even, a, b)
            to[1, HP - 1 - j] = pick(even, b, a)
    level = Level(K, S, U, W, D, own, (wide, lanes))
    for colour in (0, 1):
        level.setup(colour, without(span(own, 4 - colour), inner_span(own, 1)))
    level.all_clear(4)
    level.sweep(1, without(span(own, 3), inner_span(own, 2)))
    level.sweep(0, without(span(own, 2), inner_span(own, 3)))
    level.sweep(1, span(own, 1))
    level.residual(R, span(own, 0), 2, 8)
    store_field(U, field, own, even_own, wide)
    zero = jnp.zeros((rows, lanes), F32)
    for colour in (0, 1):
        for at in (0, 1, own + 2, own + 3):
            R[colour, at] = zero
    half = rows // 2
    block = half + 8
    for q in range(own + 2):
        Z[block * q : block * (q + 1)] = product(
            row_restriction(rows, True), restrict_planes(R, q + 1, even_own))
    source = product(Z[...], lane_restriction(lanes))
    row = lax.broadcasted_iota(jnp.int32, (half, lanes // 2), 0)
    for q in range(own + 2):
        at = block * q
        rows_of = source[at : at + half]
        source_out[q] = rows_of
        send.put(q, pick(row == half - 1, source[at + half : at + half + 1], rows_of),
                 pick(row == 0, source[at + half + 1 : at + half + 2], rows_of))


def widen_planes(K, send, planes, of):
    for q in range(planes):
        K[q] = of(q)
    for j in range(6):
        send.put(j, K[j], K[planes - 6 + j])


def mean_planes_kernel(own_rows, from_a, from_b, K, to_a, to_b):
    from_low, from_high = got_pair(from_a, from_b, "inner")

    def of(q):
        return jnp.concatenate([from_low[q], own_rows[q], from_high[q]], axis=0)

    widen_planes(K, Send(to_a, to_b, "outer"), own_rows.shape[0], of)


def middle_setup_kernel(k, from_a, from_b, K, W, D, I, k_next, Zk):
    from_down, from_up = got_pair(from_a, from_b, "outer")
    _, pairs, wide, lanes = K.shape
    planes = k.shape[0]
    even = even_mask(wide, lanes)

    def plane(i):
        if i < 0:
            return from_down[6 + i]
        return k[i] if i < planes else from_up[i - planes]

    for p in range(pairs):
        a, b = plane(2 * (p - HP)), plane(2 * (p - HP) + 1)
        K[0, p] = pick(even, a, b)
        K[1, p] = pick(even, b, a)
    Level(K, None, None, W, D, pairs - 2 * HP, (wide, lanes)).all_setup(5, I)
    half = wide // 2
    for q in range(pairs):
        Zk[half * q : half * (q + 1)] = product(row_sum(wide), K[0, q] + K[1, q])
    mean = product(Zk[...], lane_mean(lanes))
    for q in range(pairs):
        k_next[q] = mean[half * q : half * (q + 1)]


def source_planes_kernel(own_rows, sent_a, sent_b, from_a, from_b, S, to_a, to_b):
    planes, rows, lanes = own_rows.shape
    row = lax.broadcasted_iota(jnp.int32, (rows, lanes), 0)
    first, last = row == 0, row == rows - 1
    to_low, to_high = got_pair(sent_a, sent_b, "inner")
    from_low, from_high = got_pair(from_a, from_b, "inner")

    def of(q):
        got_low, got_high = from_low[q], from_high[q]
        low = pick(first, 0.0, got_low) + pick(last, to_low[q], 0.0)
        mine = own_rows[q] + pick(first, got_low, 0.0) + pick(last, got_high, 0.0)
        high = pick(last, 0.0, got_high) + pick(first, to_high[q], 0.0)
        return jnp.concatenate([low, mine, high], axis=0)

    widen_planes(S, Send(to_a, to_b, "outer"), planes, of)


def middle_kernel(s, source_a, source_b, K, W, D, I, k_next,
                  field, s_next, to_a, to_b, S, U, R, Z):
    from_down, from_up = got_pair(source_a, source_b, "outer")
    send = Send(to_a, to_b, "outer")
    planes = field.shape[0]
    _, pairs, wide, lanes = K.shape
    own = planes // 2
    even = even_mask(wide, lanes)
    zero = jnp.zeros((wide, lanes), F32)

    def source_plane(i):
        if i < -5 or i > planes + 4:
            return zero
        if i < -1:
            return from_down[i + 5]
        if i == -1:
            return from_down[4] + s[0]
        if i == 0:
            return s[1] + from_down[5]
        if i < planes - 1:
            return s[i + 1]
        if i == planes - 1:
            return s[planes] + from_up[0]
        if i == planes:
            return from_up[1] + s[planes + 1]
        return from_up[i - planes + 1]

    level = Level(K, S, U, W, D, own, (wide, lanes))
    for p in range(-HP, own + HP):
        a, b = source_plane(2 * p), source_plane(2 * p + 1)
        S[0, HP + p] = pick(even, a, b)
        S[1, HP + p] = pick(even, b, a)
    for colour in (0, 1):
        for p in span(own, 5 - colour):
            level.begin(colour, p, I[colour, p])
    level.all_clear(5)
    level.all_sweeps(5)
    level.residual(R, span(own, 1), 0, 0)
    rows = field.shape[1]
    store_field(U, field, own, even_mask(rows, lanes), wide)
    half = wide // 2
    for q in range(own):
        Z[half * q : half * (q + 1)] = product(
            row_restriction(wide, False), restrict_planes(R, q + 1, even))
    source = product(Z[...], lane_restriction(lanes))
    for q in range(own):
        s_next[q] = source[half * q : half * (q + 1)]
    for j in range(4):
        send.put(j, s_next[j], s_next[own - 4 + j])
    for j in range(2):
        send.put(4 + j, k_next[HP + 3 + j], k_next[HP + own - 5 + j])


def coarse_kernel(s, k, from_a, from_b, field, rest, K, S, U, W, D, R):
    from_down, from_up = got_pair(from_a, from_b, "outer")
    planes, wide, lanes = s.shape
    own = planes // 2
    rows = field.shape[1]
    even = even_mask(wide, lanes)
    even_own = even_mask(rows, lanes)
    zero = jnp.zeros((wide, lanes), F32)

    def source_plane(i):
        if i < -4 or i > planes + 3:
            return zero
        if i < 0:
            return from_down[4 + i]
        return s[i] if i < planes else from_up[i - planes]

    def mean_plane(i):
        if -HP <= i < planes + HP:
            return k[HP + i]
        if i in (-5, -4):
            return from_down[9 + i]
        return from_up[1 + i - planes] if i in (planes + 3, planes + 4) else zero

    for p in range(-HP, own + HP):
        for to, plane in ((S, source_plane), (K, mean_plane)):
            a, b = plane(2 * p), plane(2 * p + 1)
            to[0, HP + p] = pick(even, a, b)
            to[1, HP + p] = pick(even, b, a)
    level = Level(K, S, U, W, D, own, (wide, lanes))
    level.all_setup(4)
    level.all_clear(4)
    level.all_sweeps(4)
    level.residual(R, span(own, 0), 2, (wide - rows) // 2)
    store_field(U, field, own, even_own, wide)
    for p in range(own):
        red, black = R[0, p + 2], R[1, p + 2]
        rest[2 * p] = pick(even_own, red, black)
        rest[2 * p + 1] = pick(even_own, black, red)


def limit(scratch):
    words = 0
    for shape in scratch:
        size = 1
        for n in shape:
            size *= n
        words += size
    return 4 * words + (12 << 20)


def call(kernel, outs, scratch, *args, in_specs=None, name=None, results=False):
    extra = {}
    if in_specs is None:
        args = [pltpu.with_memory_space_constraint(a, pltpu.VMEM) for a in args]
    else:
        args = [pltpu.with_memory_space_constraint(a, pltpu.HBM) for a in args]
        extra = {"in_specs": in_specs, "grid": (1,)}
        extra["out_specs"] = [pl.BlockSpec(memory_space=pltpu.VMEM) for _ in outs]
    if results:
        extra = {"out_specs": [pl.BlockSpec(memory_space=pltpu.VMEM) for _ in outs]}
    return pl.pallas_call(
        kernel,
        out_shape=[jax.ShapeDtypeStruct(o, F32) if results else pltpu.VMEM(o, F32) for o in outs],
        scratch_shapes=[pltpu.VMEM(shape, F32) for shape in scratch],
        compiler_params=pltpu.CompilerParams(vmem_limit_bytes=limit(scratch)),
        name=name,
        **extra,
    )(*args)


def level_arrays(own, wide, lanes):
    block = (2, own + 2 * HP, wide, lanes)
    return [block, block, block, (12, *block[1:]), block]


def exchange(a, b, axis):
    size = lax.axis_size(axis)

    def swapped(x, first):
        pairs = [(i, i + 1) for i in range(first, size - 1, 2)]
        return lax.ppermute(x, axis, pairs + [(j, i) for i, j in pairs])

    return swapped(a, 1), swapped(b, 0)


def body(right_side, coefficient):
    s, k = right_side, coefficient
    planes, rows, lanes = s.shape
    own = planes // 2
    wide = rows + 16

    low = pl.BlockSpec((planes, 8, lanes), lambda i: (0, 0, 0))
    high = pl.BlockSpec((planes, 8, lanes), lambda i: (0, rows // 8 - 1, 0))
    ends, inner = (2, 4, 8, lanes), (2, own - 4, 8, lanes)
    end_a, end_b, inner_a, inner_b = call(
        pack_rows_kernel, [ends, ends, inner, inner], [], s, s, k, k,
        in_specs=[low, high, low, high], name="pack_rows")
    end_halo = exchange(end_a, end_b, "inner")
    inner_halo = exchange(inner_a, inner_b, "inner")
    half, next_lanes = rows // 2, lanes // 2
    (mean,) = call(mean_kernel, [(own, half, next_lanes)], [(half * own, lanes)], k, name="mean")
    message = (9, rows, lanes)
    to_a, to_b = call(pack_planes_kernel, [message] * 2, [], s, k, *end_halo, name="pack_planes")
    mean, to_a, to_b = lax.optimization_barrier((mean, to_a, to_b))
    plane_halo = exchange(to_a, to_b, "outer")
    arrays = level_arrays(own, wide, lanes)
    early = [(a[0], own, wide, lanes) for a in arrays]
    prepared = call(fine_prepare_kernel, early, [], s, k, *end_halo, *inner_halo,
                    name="fine_prepare")
    mean_halo = exchange(mean, mean, "inner")

    count = own + 2
    message = (count, half, next_lanes)
    field0, source, to_a, to_b = call(
        fine_kernel, [s.shape, message, message, message],
        [*arrays, (2, own + 4, rows, lanes), ((half + 8) * count, lanes)],
        *plane_halo, *prepared, name="fine_level")

    planes, rows, lanes = own, half, next_lanes
    own, wide = planes // 2, 3 * rows
    *mean_halo, to_a, to_b = lax.optimization_barrier((*mean_halo, to_a, to_b))
    row_halo = exchange(to_a, to_b, "inner")
    message = (6, wide, lanes)
    k1, *sent = call(
        mean_planes_kernel, [(planes, wide, lanes), message, message], [],
        mean, *mean_halo, name="mean_planes")
    mean_halo = exchange(*sent, "outer")
    K, S, U, W, D = level_arrays(own, wide, lanes)
    next_half, next_lanes = wide // 2, lanes // 2
    *constants, k2 = call(
        middle_setup_kernel, [K, W, D, K, (own + 2 * HP, next_half, next_lanes)],
        [((own + 2 * HP) * next_half, lanes)], k1, *mean_halo, name="middle_setup")
    message = (6, wide, lanes)
    s1, *sent = call(
        source_planes_kernel, [(planes + 2, wide, lanes), message, message], [],
        source, to_a, to_b, *row_halo, name="source_planes")
    source_halo = exchange(*sent, "outer")
    half = next_half
    message = (6, half, next_lanes)
    field1, s2, *sent = call(
        middle_kernel, [(planes, rows, lanes), (own, half, next_lanes), message, message],
        [S, U, (2, own + 2, wide, lanes), (half * own, lanes)],
        s1, *source_halo, *constants, k2, name="middle_level")

    planes, rows, wide, lanes = own, rows // 2, half, next_lanes
    own = planes // 2
    field2, rest = call(
        coarse_kernel, [(planes, rows, lanes)] * 2,
        [*level_arrays(own, wide, lanes), (2, own + 4, rows, lanes)],
        s2, k2, *exchange(*sent, "outer"), name="coarse_level", results=True)
    return field0, field1, field2, rest


def solution(mesh):
    spec = P("outer", "inner", None)
    return jax.shard_map(body, mesh=mesh, in_specs=(spec, spec), out_specs=(spec,) * 4, check_vma=False)
```

```python
import jax
import jax.numpy as jnp
from jax import lax
from jax.experimental import pallas as pl
from jax.experimental.pallas import tpu as pltpu
from jax.sharding import PartitionSpec as P

F32 = jnp.float32
HP = 3


def tiled(tile, rows, lanes):
    wide = jnp.concatenate([tile] * (lanes // 128), axis=1)
    return jnp.concatenate([wide] * (rows // 8), axis=0)


def even_mask(rows, lanes):
    row = lax.broadcasted_iota(jnp.int32, (8, 128), 0)
    lane = lax.broadcasted_iota(jnp.int32, (8, 128), 1)
    return tiled((row + lane) & 1, rows, lanes) == 0


def pick(mask, a, b):
    return jnp.where(mask, a, b)


def odd_on(axis):
    return lax.axis_index(axis) % 2 == 1


def choose(odd, a, b):
    return lax.select(jnp.full(a.shape, odd), a, b)


class Got:
    def __init__(self, a, b, odd, upper):
        self.first, self.second = (a, b) if upper else (b, a)
        self.odd = odd
        self.shape = a.shape

    def __getitem__(self, at):
        return choose(self.odd, self.first[at], self.second[at])


def got_pair(a, b, axis):
    odd = odd_on(axis)
    return Got(a, b, odd, False), Got(a, b, odd, True)


class Send:
    def __init__(self, a, b, axis):
        self.a, self.b, self.odd = a, b, odd_on(axis)

    def put(self, at, low, high):
        self.a[at] = choose(self.odd, high, low)
        self.b[at] = choose(self.odd, low, high)


def row_index(lanes):
    return lax.broadcasted_iota(jnp.int32, (8, lanes), 0)


def lane_edge(value, at_start):
    lanes = value.shape[1]
    lane = lax.broadcasted_iota(jnp.int32, (value.shape[0], 128), 1)
    if at_start:
        edge = pick(lane == 0, 0.0, value[:, :128])
        return edge if lanes == 128 else jnp.concatenate([edge, value[:, 128:]], axis=1)
    edge = pick(lane == 127, 0.0, value[:, lanes - 128 :])
    return edge if lanes == 128 else jnp.concatenate([value[:, : lanes - 128], edge], axis=1)


def neighbours(ref, colour, p, pairs, even):
    other = 1 - colour
    x = ref[other, p]
    if isinstance(p, int):
        below, above = ref[other, max(p - 1, 0)], ref[other, min(p + 1, pairs - 1)]
    else:
        below = ref[other, jnp.maximum(p - 1, 0)]
        above = ref[other, jnp.minimum(p + 1, pairs - 1)]
    far = pick(even, below, above) if colour == 0 else pick(even, above, below)
    rows, lanes = x.shape
    return (
        x,
        far,
        pltpu.roll(x, 1, 0),
        pltpu.roll(x, rows - 1, 0),
        pltpu.roll(x, 1, 1),
        pltpu.roll(x, lanes - 1, 1),
    )


def span(own, layers):
    extra = (layers + 1) // 2
    return range(HP - extra, HP + own + extra)


class Store:
    def __init__(self, ref, start=0, early=None, held=()):
        self.ref, self.start = ref, start
        self.early = {key: early for key in held}

    def place(self, at):
        first, p, *rest = at
        early = self.early.get((first, p))
        if early is not None:
            return early.ref, (first, p - early.start, *rest)
        return self.ref, (first, p - self.start, *rest)

    def __getitem__(self, at):
        ref, at = self.place(at)
        return ref[at]

    def __setitem__(self, at, value):
        self.early.pop((at[0], at[1]), None)
        ref, at = self.place(at)
        ref[at] = value


class Level:
    def __init__(self, K, S, U, W, D, own, shape):
        self.K, self.S, self.U, self.W, self.D, self.own = K, S, U, W, D, own
        self.pairs = own + 2 * HP
        self.rows, self.lanes = shape
        self.even = even_mask(self.rows, self.lanes)

    def setup(self, colour, pairs, inverse_out=None):
        for p in pairs:
            near = list(neighbours(self.K, colour, p, self.pairs, self.even))
            near[4] = lane_edge(near[4], True)
            near[5] = lane_edge(near[5], False)
            centre = self.K[colour, p]
            total = near[0]
            for value in near[1:]:
                total = total + value
            diag = 3.0 * centre + 0.5 * total
            inverse = pick(centre > 0.0, 1.0 / diag, 0.0)
            half = 0.5 * inverse
            for i, value in enumerate(near):
                weight = (centre + value) * half
                if i == 4:
                    weight = lane_edge(weight, True)
                if i == 5:
                    weight = lane_edge(weight, False)
                self.W[colour * 6 + i, p] = weight
            self.D[colour, p] = diag
            if inverse_out is not None:
                inverse_out[colour, p] = inverse
            else:
                self.begin(colour, p, inverse)

    def begin(self, colour, p, inverse):
        start = self.S[colour, p] * inverse
        self.S[colour, p] = start
        if colour == 0:
            self.U[0, p] = start

    def clear(self, colour, pairs):
        zero = jnp.zeros((self.rows, self.lanes), F32)
        for p in range(self.pairs):
            if p not in pairs:
                self.U[colour, p] = zero

    def relaxed(self, colour, p):
        near = neighbours(self.U, colour, p, self.pairs, self.even)
        total = self.S[colour, p]
        for i, value in enumerate(near):
            total = total + self.W[colour * 6 + i, p] * value
        return total

    def sweep(self, colour, pairs):
        for p in pairs:
            self.U[colour, p] = self.relaxed(colour, p)

    def residual(self, R, pairs, pad, inset):
        for i, p in enumerate(pairs):
            for colour in (0, 1):
                rest = self.D[colour, p] * (self.relaxed(colour, p) - self.U[colour, p])
                R[colour, i + pad] = rest[inset : self.rows - inset]

    def all_setup(self, depth, inverse_out=None):
        for colour in (0, 1):
            self.setup(colour, span(self.own, depth - colour), inverse_out)

    def all_clear(self, depth):
        for colour in (0, 1):
            self.clear(colour, span(self.own, depth - colour))

    def all_sweeps(self, depth):
        for i, colour in enumerate((1, 0, 1)):
            self.sweep(colour, span(self.own, depth - 1 - i))


def without(pairs, inner):
    return [p for p in pairs if p not in inner]


def inner_span(own, margin):
    return range(HP + margin, HP + own - margin)


def store_field(U, out, own, even, wide):
    rows = out.shape[1]
    first = (wide - rows) // 2
    for p in range(own):
        red = U[0, HP + p, first : first + rows]
        black = U[1, HP + p, first : first + rows]
        out[2 * p] = pick(even, red, black)
        out[2 * p + 1] = pick(even, black, red)


def restrict_planes(R, at, even):
    red, black = R[0, at], R[1, at]
    odd_below = pick(even, R[1, at - 1], R[0, at - 1])
    even_above = pick(even, R[0, at + 1], R[1, at + 1])
    return (3.0 * (red + black) + (odd_below + even_above)) * 0.125


def row_restriction(rows, ends):
    half = rows // 2
    shape = (half + 8 if ends else half, rows)
    j = lax.broadcasted_iota(jnp.int32, shape, 0)
    m = lax.broadcasted_iota(jnp.int32, shape, 1)
    inner = (m == 2 * j) | (m == 2 * j + 1)
    outer = (m == 2 * j - 1) | (m == 2 * j + 2)
    main = pick(inner, 0.375, pick(outer, 0.125, 0.0)).astype(F32)
    if not ends:
        return main.astype(jnp.bfloat16)
    edge = pick(((j == half) & (m == 0)) | ((j == half + 1) & (m == rows - 1)), 0.125, 0.0)
    return pick(j < half, main, edge).astype(F32).astype(jnp.bfloat16)


def row_sum(rows):
    j = 2 * lax.broadcasted_iota(jnp.int32, (rows // 2, rows), 0)
    m = lax.broadcasted_iota(jnp.int32, (rows // 2, rows), 1)
    return pick((m == j) | (m == j + 1), 1.0, 0.0).astype(F32).astype(jnp.bfloat16)


def split(x):
    parts = []
    for _ in range(3):
        part = x.astype(jnp.bfloat16)
        parts.append(part)
        x = x - part.astype(F32)
    return parts


def product(a, b):
    if a.dtype == jnp.bfloat16:
        parts = [jnp.dot(a, part, preferred_element_type=F32) for part in split(b)]
    else:
        parts = [jnp.dot(part, b, preferred_element_type=F32) for part in split(a)]
    return (parts[2] + parts[1]) + parts[0]


def lane_restriction(lanes):
    m = lax.broadcasted_iota(jnp.int32, (lanes, lanes // 2), 0)
    i = 2 * lax.broadcasted_iota(jnp.int32, (lanes, lanes // 2), 1)
    inner = (m == i) | (m == i + 1)
    outer = (m == i - 1) | (m == i + 2)
    return pick(inner, 1.5, pick(outer, 0.5, 0.0)).astype(F32).astype(jnp.bfloat16)


def lane_mean(lanes):
    m = lax.broadcasted_iota(jnp.int32, (lanes, lanes // 2), 0)
    i = 2 * lax.broadcasted_iota(jnp.int32, (lanes, lanes // 2), 1)
    return pick((m == i) | (m == i + 1), 0.125, 0.0).astype(F32).astype(jnp.bfloat16)


def pack_pairs(send, pairs, s_low, s_high, k_low, k_high):
    cat = lambda *parts: jnp.concatenate(parts, axis=0)
    even = even_mask(8, s_low(0).shape[1])
    for p in range(pairs):
        def pair(of):
            a, b = of(2 * p), of(2 * p + 1)
            return pick(even, a, b), pick(even, b, a)

        ls, lk, hs, hk = pair(s_low), pair(k_low), pair(s_high), pair(k_high)
        send.put((0, p), cat(lk[0][0:4], ls[0][0:4]), cat(hk[0][4:8], hs[0][4:8]))
        send.put((1, p), cat(lk[1][0:5], ls[1][0:3]), cat(hk[1][3:8], hs[1][5:8]))


def pack_ends_kernel(*refs):
    def planes(first, last):
        return lambda i: first[i] if i < 4 else last[i - 4]

    sources = [planes(refs[2 * i], refs[2 * i + 1]) for i in range(4)]
    pack_pairs(Send(*refs[8:], "inner"), 4, *sources)


def pack_inner_kernel(s, k, to_a, to_b):
    planes, rows, _ = s.shape

    def plane(ref, first):
        return lambda i: ref[4 + i, first : first + 8]

    pack_pairs(Send(to_a, to_b, "inner"), planes // 2 - 4,
               plane(s, 0), plane(s, rows - 8), plane(k, 0), plane(k, rows - 8))


def rows_from(got, p, own):
    ends, inner = got
    if 2 <= p < own - 2:
        return inner[0, p - 2], inner[1, p - 2]
    at = p if p < 2 else p - own + 4
    return ends[0, at], ends[1, at]


def between(row, first, last):
    return (row >= first) & (row <= last)


def pack_planes_kernel(s, k, from_a, from_b, to_a, to_b):
    planes, rows, lanes = s.shape
    own = planes // 2
    even = even_mask(8, lanes)
    even_own = even_mask(rows, lanes)
    row = row_index(lanes)
    low, high = got_pair(from_a, from_b, "inner")
    send = Send(to_a, to_b, "outer")

    def edges(plane, of_k):
        lr, lb = rows_from((low, None), plane // 2, own)
        hr, hb = rows_from((high, None), plane // 2, own)
        if of_k:
            red = jnp.concatenate([lr[0:4], hr[0:4]], axis=0)
            black = jnp.concatenate([lb[1:5], hb[0:4]], axis=0)
        else:
            red = jnp.concatenate([lr[4:8], hr[4:8]], axis=0)
            black = jnp.concatenate([lb[4:8], hb[5:8], hb[7:8]], axis=0)
        return (pick(even, red, black), pick(even, black, red))[plane % 2]

    def corners(plane):
        tiles = []
        for d in (1, 2, 3):
            source = edges(plane(d), False)
            mean = pltpu.roll(edges(plane(5 - d), True), 4, 0)
            tiles.append(pick(between(row, d, 7 - d), source, mean))
        return tiles + [edges(plane(1), True)]

    for j in range(3):
        send.put(j, s[j], s[planes - 3 + j])
    for j in range(4):
        send.put(3 + j, k[j], k[planes - 4 + j])
    send.put(7, pick(even_own, pltpu.roll(k[4], 1, 1), s[3]),
             pick(even_own, s[planes - 4], pltpu.roll(k[planes - 5], 1, 1)))
    down, up = corners(lambda d: d - 1), corners(lambda d: planes - d)
    for i in range(4):
        send.put((8, slice(8 * i, 8 * i + 8)), down[i], up[i])


def mean_kernel(k, out, Z):
    planes, rows, lanes = k.shape
    half = rows // 2
    for q in range(planes // 2):
        Z[half * q : half * (q + 1)] = product(row_sum(rows), k[2 * q] + k[2 * q + 1])
    mean = product(Z[...], lane_mean(lanes))
    for q in range(planes // 2):
        out[q] = mean[half * q : half * (q + 1)]


def fine_prepare_kernel(s, k, end_a, end_b, inner_a, inner_b, *arrays):
    planes, rows, lanes = s.shape
    own = planes // 2
    wide = rows + 16
    from_low, from_high = zip(got_pair(end_a, end_b, "inner"), got_pair(inner_a, inner_b, "inner"))
    even_own = even_mask(rows, lanes)
    row = row_index(lanes)
    K, S, U, W, D = [Store(ref, HP) for ref in arrays]

    def fill(p):
        at = HP + p
        lr, lb = rows_from(from_low, p, own)
        hr, hb = rows_from(from_high, p, own)
        K[0, at, 0:8] = pick(row >= 4, pltpu.roll(lr, 4, 0), 0.0)
        K[1, at, 0:8] = pick(row >= 3, pltpu.roll(lb, 3, 0), 0.0)
        S[0, at, 0:8] = pick(row >= 4, lr, 0.0)
        S[1, at, 0:8] = pick(row >= 5, lb, 0.0)
        K[0, at, 8 + rows : wide] = pick(row < 4, hr, 0.0)
        K[1, at, 8 + rows : wide] = pick(row < 5, hb, 0.0)
        S[0, at, 8 + rows : wide] = pick(row < 4, pltpu.roll(hr, 4, 0), 0.0)
        S[1, at, 8 + rows : wide] = pick(row < 3, pltpu.roll(hb, 3, 0), 0.0)
        for ref, to in ((s, S), (k, K)):
            a, b = ref[2 * p], ref[2 * p + 1]
            to[0, at, 8 : 8 + rows] = pick(even_own, a, b)
            to[1, at, 8 : 8 + rows] = pick(even_own, b, a)

    for p in range(own):
        fill(p)
    level = Level(K, S, U, W, D, own, (wide, lanes))
    level.setup(0, inner_span(own, 1))
    level.setup(1, inner_span(own, 1))
    level.sweep(1, inner_span(own, 2))
    level.sweep(0, inner_span(own, 3))


def fine_kernel(plane_a, plane_b, K0, S0, U0, W0, D0,
                field, source_out, to_a, to_b, K1, S1, U1, W1, D1, R, Z):
    from_down, from_up = got_pair(plane_a, plane_b, "outer")
    send = Send(to_a, to_b, "inner")
    planes, rows, lanes = field.shape
    own = planes // 2
    wide = rows + 16
    even = even_mask(wide, lanes)
    even_own = even_mask(rows, lanes)
    row = row_index(lanes)
    def store(ref, early, firsts, pairs):
        return Store(ref, 0, Store(early, HP), [(i, p) for i in firsts for p in pairs])

    inside = inner_span(own, 1)
    K = store(K1, K0, (0, 1), inner_span(own, 0))
    S = store(S1, S0, (0, 1), inner_span(own, 0))
    W = store(W1, W0, range(12), inside)
    D = store(D1, D0, (0, 1), inside)
    U = store(U1, U0, (0,), inside)
    U.early.update({(1, p): Store(U0, HP) for p in inner_span(own, 2)})

    def framed(low_edge, middle, high_edge):
        return jnp.concatenate(
            [pick(row >= 4, low_edge, 0.0), middle, pick(row < 4, high_edge, 0.0)], axis=0)

    def source_at(got, d, up):
        if d == 4:
            mixed = got[7]
            middle = pick(even_own, 0.0, mixed) if up else pick(even_own, mixed, 0.0)
            edge = jnp.zeros((8, lanes), F32)
        else:
            middle = got[d - 1 if up else 3 - d]
            edge = pick(between(row, d, 7 - d), got[8, 8 * d - 8 : 8 * d], 0.0)
            edge = pltpu.roll(edge, 4, 0)
        return framed(edge, middle, edge)

    def mean_at(got, d, up):
        edge = jnp.zeros((8, lanes), F32)
        if d == 6:
            return jnp.zeros((wide, lanes), F32)
        if d == 5:
            mixed = pltpu.roll(got[7], lanes - 1, 1)
            middle = pick(even_own, 0.0, mixed) if up else pick(even_own, mixed, 0.0)
        else:
            middle = got[2 + d if up else 7 - d]
            if d == 1:
                edge = pltpu.roll(got[8, 24:32], 4, 0)
            else:
                edge = pick(between(row, 5 - d, 2 + d), 0.0, got[8, 8 * (4 - d) : 8 * (5 - d)])
        return framed(edge, middle, edge)

    for j in range(HP):
        for to, plane in ((K, mean_at), (S, source_at)):
            if to is S and j == 2:
                continue
            near, far = 2 * j + 1, 2 * j + 2
            a, b = plane(from_up, near, True), plane(from_up, far, True)
            to[0, HP + own + j] = pick(even, a, b)
            to[1, HP + own + j] = pick(even, b, a)
            a, b = plane(from_down, far, False), plane(from_down, near, False)
            to[0, HP - 1 - j] = pick(even, a, b)
            to[1, HP - 1 - j] = pick(even, b, a)
    level = Level(K, S, U, W, D, own, (wide, lanes))
    for colour in (0, 1):
        level.setup(colour, without(span(own, 4 - colour), inner_span(own, 1)))
    level.all_clear(4)
    level.sweep(1, without(span(own, 3), inner_span(own, 2)))
    level.sweep(0, without(span(own, 2), inner_span(own, 3)))
    level.sweep(1, span(own, 1))
    level.residual(R, span(own, 0), 2, 8)
    store_field(U, field, own, even_own, wide)
    zero = jnp.zeros((rows, lanes), F32)
    for colour in (0, 1):
        for at in (0, 1, own + 2, own + 3):
            R[colour, at] = zero
    half = rows // 2
    block = half + 8
    for q in range(own + 2):
        Z[block * q : block * (q + 1)] = product(
            row_restriction(rows, True), restrict_planes(R, q + 1, even_own))
    source = product(Z[...], lane_restriction(lanes))
    row = lax.broadcasted_iota(jnp.int32, (half, lanes // 2), 0)
    for q in range(own + 2):
        at = block * q
        rows_of = source[at : at + half]
        source_out[q] = rows_of
        send.put(q, pick(row == half - 1, source[at + half : at + half + 1], rows_of),
                 pick(row == 0, source[at + half + 1 : at + half + 2], rows_of))


def widen_planes(K, send, planes, of):
    for q in range(planes):
        K[q] = of(q)
    for j in range(6):
        send.put(j, K[j], K[planes - 6 + j])


def mean_planes_kernel(own_rows, from_a, from_b, K, to_a, to_b):
    from_low, from_high = got_pair(from_a, from_b, "inner")

    def of(q):
        return jnp.concatenate([from_low[q], own_rows[q], from_high[q]], axis=0)

    widen_planes(K, Send(to_a, to_b, "outer"), own_rows.shape[0], of)


def middle_setup_kernel(k, from_a, from_b, K, W, D, I, k_next, Zk):
    from_down, from_up = got_pair(from_a, from_b, "outer")
    _, pairs, wide, lanes = K.shape
    planes = k.shape[0]
    even = even_mask(wide, lanes)

    def plane(i):
        if i < 0:
            return from_down[6 + i]
        return k[i] if i < planes else from_up[i - planes]

    for p in range(pairs):
        a, b = plane(2 * (p - HP)), plane(2 * (p - HP) + 1)
        K[0, p] = pick(even, a, b)
        K[1, p] = pick(even, b, a)
    Level(K, None, None, W, D, pairs - 2 * HP, (wide, lanes)).all_setup(5, I)
    half = wide // 2
    for q in range(pairs):
        Zk[half * q : half * (q + 1)] = product(row_sum(wide), K[0, q] + K[1, q])
    mean = product(Zk[...], lane_mean(lanes))
    for q in range(pairs):
        k_next[q] = mean[half * q : half * (q + 1)]


def source_planes_kernel(own_rows, sent_a, sent_b, from_a, from_b, S, to_a, to_b):
    planes, rows, lanes = own_rows.shape
    row = lax.broadcasted_iota(jnp.int32, (rows, lanes), 0)
    first, last = row == 0, row == rows - 1
    to_low, to_high = got_pair(sent_a, sent_b, "inner")
    from_low, from_high = got_pair(from_a, from_b, "inner")

    def of(q):
        got_low, got_high = from_low[q], from_high[q]
        low = pick(first, 0.0, got_low) + pick(last, to_low[q], 0.0)
        mine = own_rows[q] + pick(first, got_low, 0.0) + pick(last, got_high, 0.0)
        high = pick(last, 0.0, got_high) + pick(first, to_high[q], 0.0)
        return jnp.concatenate([low, mine, high], axis=0)

    widen_planes(S, Send(to_a, to_b, "outer"), planes, of)


def middle_kernel(s, source_a, source_b, K, W, D, I, k_next,
                  field, s_next, to_a, to_b, S, U, R, Z):
    from_down, from_up = got_pair(source_a, source_b, "outer")
    send = Send(to_a, to_b, "outer")
    planes = field.shape[0]
    _, pairs, wide, lanes = K.shape
    own = planes // 2
    even = even_mask(wide, lanes)
    zero = jnp.zeros((wide, lanes), F32)

    def source_plane(i):
        if i < -5 or i > planes + 4:
            return zero
        if i < -1:
            return from_down[i + 5]
        if i == -1:
            return from_down[4] + s[0]
        if i == 0:
            return s[1] + from_down[5]
        if i < planes - 1:
            return s[i + 1]
        if i == planes - 1:
            return s[planes] + from_up[0]
        if i == planes:
            return from_up[1] + s[planes + 1]
        return from_up[i - planes + 1]

    level = Level(K, S, U, W, D, own, (wide, lanes))
    for p in range(-HP, own + HP):
        a, b = source_plane(2 * p), source_plane(2 * p + 1)
        S[0, HP + p] = pick(even, a, b)
        S[1, HP + p] = pick(even, b, a)
    for colour in (0, 1):
        for p in span(own, 5 - colour):
            level.begin(colour, p, I[colour, p])
    level.all_clear(5)
    level.all_sweeps(5)
    level.residual(R, span(own, 1), 0, 0)
    rows = field.shape[1]
    store_field(U, field, own, even_mask(rows, lanes), wide)
    half = wide // 2
    for q in range(own):
        Z[half * q : half * (q + 1)] = product(
            row_restriction(wide, False), restrict_planes(R, q + 1, even))
    source = product(Z[...], lane_restriction(lanes))
    for q in range(own):
        s_next[q] = source[half * q : half * (q + 1)]
    for j in range(4):
        send.put(j, s_next[j], s_next[own - 4 + j])
    for j in range(2):
        send.put(4 + j, k_next[HP + 3 + j], k_next[HP + own - 5 + j])


def coarse_kernel(s, k, from_a, from_b, field, rest, K, S, U, W, D, R):
    from_down, from_up = got_pair(from_a, from_b, "outer")
    planes, wide, lanes = s.shape
    own = planes // 2
    rows = field.shape[1]
    even = even_mask(wide, lanes)
    even_own = even_mask(rows, lanes)
    zero = jnp.zeros((wide, lanes), F32)

    def source_plane(i):
        if i < -4 or i > planes + 3:
            return zero
        if i < 0:
            return from_down[4 + i]
        return s[i] if i < planes else from_up[i - planes]

    def mean_plane(i):
        if -HP <= i < planes + HP:
            return k[HP + i]
        if i in (-5, -4):
            return from_down[9 + i]
        return from_up[1 + i - planes] if i in (planes + 3, planes + 4) else zero

    for p in range(-HP, own + HP):
        for to, plane in ((S, source_plane), (K, mean_plane)):
            a, b = plane(2 * p), plane(2 * p + 1)
            to[0, HP + p] = pick(even, a, b)
            to[1, HP + p] = pick(even, b, a)
    level = Level(K, S, U, W, D, own, (wide, lanes))
    level.all_setup(4)
    level.all_clear(4)
    level.all_sweeps(4)
    level.residual(R, span(own, 0), 2, (wide - rows) // 2)
    store_field(U, field, own, even_own, wide)
    for p in range(own):
        red, black = R[0, p + 2], R[1, p + 2]
        rest[2 * p] = pick(even_own, red, black)
        rest[2 * p + 1] = pick(even_own, black, red)


def limit(scratch):
    words = 0
    for shape in scratch:
        size = 1
        for n in shape:
            size *= n
        words += size
    return 4 * words + (12 << 20)


def call(kernel, outs, scratch, *args, in_specs=None, name=None, results=False):
    extra = {}
    if in_specs is None:
        args = [pltpu.with_memory_space_constraint(a, pltpu.VMEM) for a in args]
    else:
        args = [pltpu.with_memory_space_constraint(a, pltpu.HBM) for a in args]
        extra = {"in_specs": in_specs, "grid": (1,)}
        extra["out_specs"] = [pl.BlockSpec(memory_space=pltpu.VMEM) for _ in outs]
    if results:
        extra = {"out_specs": [pl.BlockSpec(memory_space=pltpu.VMEM) for _ in outs]}
    return pl.pallas_call(
        kernel,
        out_shape=[jax.ShapeDtypeStruct(o, F32) if results else pltpu.VMEM(o, F32) for o in outs],
        scratch_shapes=[pltpu.VMEM(shape, F32) for shape in scratch],
        compiler_params=pltpu.CompilerParams(vmem_limit_bytes=limit(scratch)),
        name=name,
        **extra,
    )(*args)


def level_arrays(own, wide, lanes):
    block = (2, own + 2 * HP, wide, lanes)
    return [block, block, block, (12, *block[1:]), block]


def exchange(a, b, axis):
    size = lax.axis_size(axis)

    def swapped(x, first):
        pairs = [(i, i + 1) for i in range(first, size - 1, 2)]
        return lax.ppermute(x, axis, pairs + [(j, i) for i, j in pairs])

    return swapped(a, 1), swapped(b, 0)


def body(right_side, coefficient):
    s, k = right_side, coefficient
    planes, rows, lanes = s.shape
    own = planes // 2
    wide = rows + 16

    blocks = [pl.BlockSpec((4, 8, lanes), lambda i, p=p, r=r: (p, r, 0))
              for r in (0, rows // 8 - 1) for p in (0, planes // 4 - 1)]
    ends, inner = (2, 4, 8, lanes), (2, own - 4, 8, lanes)
    sent = call(pack_ends_kernel, [ends, ends], [], *[s] * 4, *[k] * 4,
                in_specs=blocks * 2, name="pack_ends")
    *end_halo, late_s, late_k = lax.optimization_barrier((*exchange(*sent, "inner"), s, k))
    sent = call(pack_inner_kernel, [inner, inner], [], late_s, late_k, name="pack_inner")
    inner_halo = exchange(*sent, "inner")
    half, next_lanes = rows // 2, lanes // 2
    (mean,) = call(mean_kernel, [(own, half, next_lanes)], [(half * own, lanes)], k, name="mean")
    message = (9, rows, lanes)
    to_a, to_b = call(pack_planes_kernel, [message] * 2, [], s, k, *end_halo, name="pack_planes")
    mean, to_a, to_b = lax.optimization_barrier((mean, to_a, to_b))
    plane_halo = exchange(to_a, to_b, "outer")
    arrays = level_arrays(own, wide, lanes)
    early = [(a[0], own, wide, lanes) for a in arrays]
    prepared = call(fine_prepare_kernel, early, [], s, k, *end_halo, *inner_halo,
                    name="fine_prepare")
    mean_halo = exchange(mean, mean, "inner")

    count = own + 2
    message = (count, half, next_lanes)
    field0, source, to_a, to_b = call(
        fine_kernel, [s.shape, message, message, message],
        [*arrays, (2, own + 4, rows, lanes), ((half + 8) * count, lanes)],
        *plane_halo, *prepared, name="fine_level")

    planes, rows, lanes = own, half, next_lanes
    own, wide = planes // 2, 3 * rows
    *mean_halo, to_a, to_b = lax.optimization_barrier((*mean_halo, to_a, to_b))
    row_halo = exchange(to_a, to_b, "inner")
    message = (6, wide, lanes)
    k1, *sent = call(
        mean_planes_kernel, [(planes, wide, lanes), message, message], [],
        mean, *mean_halo, name="mean_planes")
    mean_halo = exchange(*sent, "outer")
    K, S, U, W, D = level_arrays(own, wide, lanes)
    next_half, next_lanes = wide // 2, lanes // 2
    *constants, k2 = call(
        middle_setup_kernel, [K, W, D, K, (own + 2 * HP, next_half, next_lanes)],
        [((own + 2 * HP) * next_half, lanes)], k1, *mean_halo, name="middle_setup")
    message = (6, wide, lanes)
    s1, *sent = call(
        source_planes_kernel, [(planes + 2, wide, lanes), message, message], [],
        source, to_a, to_b, *row_halo, name="source_planes")
    source_halo = exchange(*sent, "outer")
    half = next_half
    message = (6, half, next_lanes)
    field1, s2, *sent = call(
        middle_kernel, [(planes, rows, lanes), (own, half, next_lanes), message, message],
        [S, U, (2, own + 2, wide, lanes), (half * own, lanes)],
        s1, *source_halo, *constants, k2, name="middle_level")

    planes, rows, wide, lanes = own, rows // 2, half, next_lanes
    own = planes // 2
    field2, rest = call(
        coarse_kernel, [(planes, rows, lanes)] * 2,
        [*level_arrays(own, wide, lanes), (2, own + 4, rows, lanes)],
        s2, k2, *exchange(*sent, "outer"), name="coarse_level", results=True)
    return field0, field1, field2, rest


def solution(mesh):
    spec = P("outer", "inner", None)
    return jax.shard_map(body, mesh=mesh, in_specs=(spec, spec), out_specs=(spec,) * 4, check_vma=False)
```
